128 devices in a mesh: gx: 8 (over y, core), gy: 16 (over z, x).
Axes of the slice: x: 4, y: 4, z: 4, core: 2. Of those that a mesh axis runs over, the one named last changes fastest.
Arguments:
- z_factor: float32 [8, 16, 24, 128, 128], P('gx', 'gy'), may hold values from -1 to 1
- fock: float32 [8, 16, 24, 128, 128], P('gx', 'gy'), may hold values from -1 to 1
- cotangent: float32 [8, 16, 24, 128, 128], P('gx', 'gy'), may hold values from -1 to 1
- tasks_zg: int32 [8, 16, 3, 64], P('gx', 'gy'), may hold values from 0 to 119, as said below
- tasks_fock: int32 [8, 16, 3, 64], P('gx', 'gy'), may hold values from 0 to 119, as said below
- tasks_fz: int32 [8, 16, 3, 64], P('gx', 'gy'), may hold values from 0 to 119, as said below
- tasks_zgt: int32 [8, 16, 3, 64], P('gx', 'gy'), may hold values from 0 to 119, as said below
- tasks_trans: int32 [8, 16, 3, 64], P('gx', 'gy'), may hold values from 0 to 119, as said below
Outputs:
- fock_grad: float32 [8, 16, 24, 128, 128], P('gx', 'gy')
- factor_grad: float32 [8, 16, 24, 128, 128], P('gx', 'gy')
The draws below stay inside these ranges and needn't reach their ends.
Inputs may be any that keep to these rules, and one draw needn't show every extreme that they name: `tasks_zg`: each cell column's list holds live entries (out below 24) first and then padding entries (out = 24, a = b = 0); out below 24 and a below 24 on live entries, b below 120; the busiest cell column's list is full. `tasks_fock`: each cell column's list holds live entries (out below 24) first and then padding entries (out = 24, a = b = 0); out below 24 and a below 24 on live entries, b below 120; the busiest cell column's list is full. `tasks_fz`: each cell column's list holds live entries (out below 24) first and then padding entries (out = 24, a = b = 0); out below 24 and a below 24 on live entries, b below 120; the busiest cell column's list is full. `tasks_zgt`: each cell column's list holds live entries (out below 24) first and then padding entries (out = 24, a = b = 0); out below 24 and a below 24 on live entries, b below 120; the busiest cell column's list is full. `tasks_trans`: each cell column's list holds live entries (out below 24) first and then padding entries (out = 24, a = b = 0); a and b below 120 and a // 24 = b // 24 on every entry; the busiest cell column's list is full.
All inputs are finite; a program needn't handle non-finite values.
Results may differ from the reference program's by a relative error of at most 0.0003.
Values sent between devices are 32-bit elements; how exact they have to be, the bound alone decides.
A program may use at most 192 MiB of HBM per device.

```python
import jax
import jax.numpy as jnp
from jax import lax

TILE = 128
CAP = 64
TPD = 24
XCOLS = 8
YCOLS = 16


def device_loads(key):
    raw_counts = jax.random.randint(jax.random.fold_in(key, 7), (XCOLS, YCOLS), 0, 8)
    smooth = raw_counts + jnp.roll(raw_counts, 1, 0) + jnp.roll(raw_counts, -1, 0) + jnp.roll(raw_counts, 1, 1) + jnp.roll(raw_counts, -1, 1)
    cubed = (smooth + 1) ** 3
    floor_count = CAP // 6
    return floor_count + cubed * (CAP - floor_count) // jnp.max(cubed)


def listed_products(key, section_salt, first_range, same_cell):
    loads = device_loads(key)
    section_key = jax.random.fold_in(key, section_salt)
    key_out, key_first, key_second = jax.random.split(section_key, 3)
    grid_shape = (XCOLS, YCOLS, CAP)
    out_index = jax.random.randint(key_out, grid_shape, 0, TPD)
    first_index = jax.random.randint(key_first, grid_shape, 0, first_range)
    second_index = jax.random.randint(key_second, grid_shape, 0, 5 * TPD)
    if same_cell:
        second_index = first_index // TPD * TPD + second_index % TPD
    live = jnp.arange(CAP, dtype=jnp.int32)[None, None, :] < loads[:, :, None]
    out_index = jnp.where(live, out_index, TPD)
    first_index = jnp.where(live, first_index, 0)
    second_index = jnp.where(live, second_index, 0)
    return jnp.stack([out_index, first_index, second_index], axis=2).astype(jnp.int32)


def draw_tasks_zg(key, part):
    return listed_products(key, 11, TPD, False)


def draw_tasks_fock(key, part):
    return listed_products(key, 12, TPD, False)


def draw_tasks_fz(key, part):
    return listed_products(key, 13, TPD, False)


def draw_tasks_zgt(key, part):
    return listed_products(key, 14, TPD, False)


def draw_tasks_trans(key, part):
    return listed_products(key, 15, 5 * TPD, True)


def shard_levels(rng, shape, cuts, smallest, largest):
    gain, own = 1.0, jax.random.fold_in(rng, 6)
    for dim, shards_of in cuts:
        steps = jnp.exp(jax.random.uniform(jax.random.fold_in(own, dim), (shards_of,), jnp.float32, smallest / len(cuts), largest / len(cuts)))
        gain = gain * jnp.repeat(steps, shape[dim] // shards_of).reshape([-1 if axis == dim else 1 for axis in range(len(shape))])
    return gain


def centred(rng, dims, spread, bound, shards=(), held_as=jnp.bfloat16):
    array = jax.random.normal(rng, dims, jnp.float32) * spread
    if len(shards) > 0:
        array = shard_levels(rng, dims, shards, -0.22, 0.18) * array
    return jnp.clip(array, min=-bound, max=bound).astype(held_as)


def setup_inputs(seed: int = 0) -> dict:
    splits = jax.random.split(jax.random.key(seed), 9)
    return {
        "z_factor": centred(splits[0], (XCOLS, YCOLS, TPD, TILE, TILE), (TILE // 4) ** -0.5, 1.0, ((0, 8), (1, 16)), jnp.float32),
        "fock": centred(splits[1], (XCOLS, YCOLS, TPD, TILE, TILE), (TILE // 4) ** -0.5, 1.0, ((0, 8), (1, 16)), jnp.float32),
        "cotangent": centred(splits[2], (XCOLS, YCOLS, TPD, TILE, TILE), (TILE // 4) ** -0.5, 1.0, ((0, 8), (1, 16)), jnp.float32),
        "tasks_zg": draw_tasks_zg(jax.random.fold_in(splits[8], 71), 0),
        "tasks_fock": draw_tasks_fock(jax.random.fold_in(splits[8], 71), 0),
        "tasks_fz": draw_tasks_fz(jax.random.fold_in(splits[8], 71), 0),
        "tasks_zgt": draw_tasks_zgt(jax.random.fold_in(splits[8], 71), 0),
        "tasks_trans": draw_tasks_trans(jax.random.fold_in(splits[8], 71), 0),
    }


def neighbourhood(matrix, col_x, col_y):
    count_x = matrix.shape[0]
    count_y = matrix.shape[1]
    pieces = [matrix[col_x, col_y], matrix[(col_x - 1) % count_x, col_y], matrix[(col_x + 1) % count_x, col_y], matrix[col_x, (col_y - 1) % count_y], matrix[col_x, (col_y + 1) % count_y]]
    return jnp.concatenate(pieces, axis=0)


def listed_sum(left_tiles, right_tiles, task_rows, limit, layout):
    left_rows = jnp.take(left_tiles, task_rows[1], axis=0).astype(jnp.float32)
    right_rows = jnp.take(right_tiles, task_rows[2], axis=0).astype(jnp.float32)
    if layout == "plain":
        form = "tij,tjk->tik"
    elif layout == "right_turned":
        form = "tij,tkj->tik"
    else:
        form = "tji,tjk->tik"
    products = jnp.einsum(form, left_rows, right_rows, precision=lax.Precision.HIGHEST)
    return jax.ops.segment_sum(products, task_rows[0], num_segments=limit)


def over_cells(section_fn, count_x, count_y):
    cells = jnp.arange(count_x * count_y, dtype=jnp.int32)

    def wrapped(index):
        return section_fn(index // count_y, index % count_y)

    result = lax.map(wrapped, cells)
    return result.reshape((count_x, count_y) + result.shape[1:])


def reference(z_factor, fock, cotangent, tasks_zg, tasks_fock, tasks_fz, tasks_zgt, tasks_trans):
    count_x = z_factor.shape[0]
    count_y = z_factor.shape[1]
    per_cell = z_factor.shape[2]

    def section_w(col_x, col_y):
        return listed_sum(z_factor[col_x, col_y], neighbourhood(cotangent, col_x, col_y), tasks_zg[col_x, col_y], per_cell, "plain")

    w_tiles = over_cells(section_w, count_x, count_y)

    def section_fock(col_x, col_y):
        return listed_sum(w_tiles[col_x, col_y], neighbourhood(z_factor, col_x, col_y), tasks_fock[col_x, col_y], per_cell, "right_turned")

    fock_grad = over_cells(section_fock, count_x, count_y)

    def section_u(col_x, col_y):
        return listed_sum(fock[col_x, col_y], neighbourhood(z_factor, col_x, col_y), tasks_fz[col_x, col_y], per_cell, "plain")

    u_tiles = over_cells(section_u, count_x, count_y)

    def section_factor(col_x, col_y):
        first_term = listed_sum(u_tiles[col_x, col_y], neighbourhood(cotangent, col_x, col_y), tasks_zgt[col_x, col_y], per_cell, "right_turned")
        second_term = listed_sum(neighbourhood(fock, col_x, col_y), neighbourhood(w_tiles, col_x, col_y), tasks_trans[col_x, col_y], per_cell, "left_turned")
        return first_term + second_term

    factor_grad = over_cells(section_factor, count_x, count_y)
    return fock_grad, factor_grad
```

```python
import functools

import jax
import jax.numpy as jnp
from jax import lax
from jax.experimental import pallas as pl
from jax.experimental.pallas import tpu as pltpu
from jax.sharding import PartitionSpec as P


TILE = 128
UNROLL = 4


def split(tile):
    high = tile.astype(jnp.bfloat16)
    low = (tile - high.astype(jnp.float32)).astype(jnp.bfloat16)
    return jnp.concatenate([high, low], axis=1)


def product(left, right, turned):
    if turned:
        high, low = right[:, :TILE], right[:, TILE:]
        rows = jnp.concatenate([high, low], axis=0)
        operand = jnp.concatenate([rows, rows], axis=1)
        both = lax.dot_general(left, operand, (((1,), (1,)), ((), ())), preferred_element_type=jnp.float32)
    else:
        operand = jnp.concatenate([right, right], axis=0)
        both = lax.dot_general(left, operand, (((1,), (0,)), ((), ())), preferred_element_type=jnp.float32)
    return both[:, :TILE] + both[:, TILE:]


def run_list(count, entry, left_of, right_of, turned, total):
    def step(turn, _):
        entries = [entry(turn * UNROLL + i) for i in range(UNROLL)]
        values = [product(left_of(a), right_of(b), turned) for _, a, b in entries]
        for (t, _, _), value in zip(entries, values):
            total[t] += value
        return 0

    lax.fori_loop(0, (count + UNROLL - 1) // UNROLL, step, 0)


def live_count(tasks, per_cell):
    length = tasks.shape[1]
    return lax.while_loop(
        lambda n: jnp.logical_and(n < length, tasks[0, jnp.minimum(n, length - 1)] < per_cell),
        lambda n: n + 1,
        jnp.int32(0),
    )


def split_all(source, target, per_cell, transposed=False):
    def step(i, _):
        tile = source[i]
        target[i] = split(tile.T if transposed else tile)
        return 0

    lax.fori_loop(0, per_cell, step, 0)


def plain_entry(tasks):
    return lambda e: (tasks[0, e], tasks[1, e], tasks[2, e])


def fetch(sources, grown, sems, per_cell):
    copies = [
        pltpu.make_async_copy(src, grown.at[pl.ds(k * per_cell, per_cell)], sems.at[k])
        for k, src in enumerate(sources)
    ]
    for c in copies:
        c.start()
    return copies


def w_kernel(tasks, z, g0, g1, g2, g3, g4, w, grown, zs, total, sems, osem):
    per_cell = z.shape[0]
    copies = fetch((g0, g1, g2, g3, g4), grown, sems, per_cell)
    split_all(z, zs, per_cell)
    total[...] = jnp.zeros_like(total)
    for c in copies:
        c.wait()
    run_list(live_count(tasks, per_cell), plain_entry(tasks), lambda a: zs[a], lambda b: split(grown[b]), False, total)
    out = pltpu.make_async_copy(total.at[pl.ds(0, per_cell)], w, osem)
    out.start()
    out.wait()


def p_kernel(t0, t1, t2, t3, t4, f, w, p0, p1, p2, p3, p4, fs, ws, total, listed, osem):
    per_cell = f.shape[0]
    split_all(f, fs, per_cell, transposed=True)
    split_all(w, ws, per_cell)
    total[...] = jnp.zeros_like(total)
    outs = []
    for slot, (k, tasks, p) in enumerate(((3, t3, p3), (4, t4, p4), (1, t1, p1), (2, t2, p2), (0, t0, p0))):
        base = k * per_cell

        def pick(e, n, tasks=tasks, base=base):
            a = tasks[1, e]
            here = jnp.logical_and(a >= base, a < base + per_cell)
            listed[0, n] = tasks[0, e]
            listed[1, n] = a - base
            listed[2, n] = tasks[2, e] - base
            return n + here.astype(jnp.int32)

        count = lax.fori_loop(0, live_count(tasks, per_cell), pick, jnp.int32(0))
        for i in range(UNROLL - 1):
            listed[0, count + i] = per_cell
            listed[1, count + i] = 0
            listed[2, count + i] = 0
        run_list(count, plain_entry(listed), lambda a: fs[a], lambda b: ws[b], False, total.at[slot])
        out = pltpu.make_async_copy(total.at[slot, pl.ds(0, per_cell)], p, osem.at[slot])
        out.start()
        outs.append(out)
    for out in outs:
        out.wait()


def rest_kernel(tfock, tfz, tzgt, f, w, p0, z0, z1, z2, z3, z4, g0, g1, g2, g3, g4, fock, factor, zgrown, ggrown, fs, ws, us, total, zsem, gsem, osem):
    per_cell = f.shape[0]
    zcopies = fetch((z0, z1, z2, z3, z4), zgrown, zsem, per_cell)
    gcopies = fetch((g0, g1, g2, g3, g4), ggrown, gsem, per_cell)
    split_all(f, fs, per_cell)
    split_all(w, ws, per_cell)
    total[0] = jnp.zeros_like(total[0])
    total[1] = jnp.zeros_like(total[1])
    total[2, pl.ds(0, per_cell)] = p0[...]
    for c in zcopies:
        c.wait()
    run_list(live_count(tfz, per_cell), plain_entry(tfz), lambda a: fs[a], lambda b: split(zgrown[b]), False, total.at[0])
    split_all(total.at[0], us, per_cell)
    run_list(live_count(tfock, per_cell), plain_entry(tfock), lambda a: ws[a], lambda b: split(zgrown[b]), True, total.at[1])
    out1 = pltpu.make_async_copy(total.at[1, pl.ds(0, per_cell)], fock, osem.at[0])
    out1.start()
    for c in gcopies:
        c.wait()
    run_list(live_count(tzgt, per_cell), plain_entry(tzgt), lambda a: us[a], lambda b: split(ggrown[b]), True, total.at[2])
    out2 = pltpu.make_async_copy(total.at[2, pl.ds(0, per_cell)], factor, osem.at[1])
    out2.start()
    out1.wait()
    out2.wait()


SMEM = pl.BlockSpec(memory_space=pltpu.SMEM)
VMEM = pl.BlockSpec(memory_space=pltpu.VMEM)
ANY = pl.BlockSpec(memory_space=pl.ANY)
F32 = jnp.float32


def cost(tasks, tiles):
    return pl.CostEstimate(flops=tasks * 2 * TILE**3 * 8, bytes_accessed=tiles * TILE * TILE * 4, transcendentals=0)


def body(z_factor, fock, cotangent, tasks_zg, tasks_fock, tasks_fz, tasks_zgt, tasks_trans):
    per_cell = z_factor.shape[2]
    cap = tasks_zg.shape[3]
    z, f, g = z_factor[0, 0], fock[0, 0], cotangent[0, 0]
    tzg, tfock, tfz, tzgt, ttrans = (t[0, 0] for t in (tasks_zg, tasks_fock, tasks_fz, tasks_zgt, tasks_trans))
    steps = (("gx", -1), ("gx", 1), ("gy", -1), ("gy", 1))

    def shifted(array, axis, by):
        n = lax.axis_size(axis)
        return lax.ppermute(array, axis, [(i, (i + by) % n) for i in range(n)])

    def halo(array):
        return [shifted(array, axis, -by) for axis, by in (steps[2], steps[3], steps[0], steps[1])]

    def ordered(h):
        return (h[2], h[3], h[0], h[1])

    gn = ordered(halo(g))
    tn = [shifted(ttrans, axis, by) for axis, by in steps]
    zn = ordered(halo(z))

    tiles = jax.ShapeDtypeStruct((per_cell, TILE, TILE), F32)
    grown = pltpu.VMEM((5 * per_cell, TILE, TILE), F32)
    cut = pltpu.VMEM((per_cell, TILE, 2 * TILE), jnp.bfloat16)
    params = pltpu.CompilerParams(vmem_limit_bytes=40 * 2**20)
    w = pl.pallas_call(
        w_kernel,
        name="w_kernel",
        out_shape=tiles,
        in_specs=[SMEM, VMEM] + [ANY] * 5,
        out_specs=ANY,
        scratch_shapes=[grown, cut, pltpu.VMEM((per_cell + 1, TILE, TILE), F32), pltpu.SemaphoreType.DMA((5,)), pltpu.SemaphoreType.DMA],
        compiler_params=params,
        cost_estimate=cost(cap, 7 * per_cell),
    )(tzg, z, g, *gn)
    p = pl.pallas_call(
        p_kernel,
        name="p_kernel",
        out_shape=[tiles] * 5,
        in_specs=[SMEM] * 5 + [VMEM] * 2,
        out_specs=[ANY] * 5,
        scratch_shapes=[cut, cut, pltpu.VMEM((5, per_cell + 1, TILE, TILE), F32), pltpu.SMEM((3, cap + UNROLL), jnp.int32), pltpu.SemaphoreType.DMA((5,))],
        compiler_params=params,
        cost_estimate=cost(2 * cap, 7 * per_cell),
    )(ttrans, *tn, f, w)
    pn = [shifted(p[k + 1], *((steps[k][0], -steps[k][1]))) for k in range(4)]
    fock_grad, part = pl.pallas_call(
        rest_kernel,
        name="rest_kernel",
        out_shape=[tiles] * 2,
        in_specs=[SMEM] * 3 + [VMEM] * 3 + [ANY] * 10,
        out_specs=[ANY] * 2,
        scratch_shapes=[grown, grown, cut, cut, cut, pltpu.VMEM((3, per_cell + 1, TILE, TILE), F32)]
        + [pltpu.SemaphoreType.DMA((5,))] * 2
        + [pltpu.SemaphoreType.DMA((2,))],
        compiler_params=params,
        cost_estimate=cost(3 * cap, 14 * per_cell),
    )(tfock, tfz, tzgt, f, w, p[0], z, *zn, g, *gn)
    factor_grad = part + ((pn[0] + pn[1]) + (pn[2] + pn[3]))
    return fock_grad[None, None], factor_grad[None, None]


def solution(mesh):
    tiles = P("gx", "gy", None, None, None)
    lists = P("gx", "gy", None, None)
    return jax.shard_map(
        body,
        mesh=mesh,
        in_specs=(tiles,) * 3 + (lists,) * 5,
        out_specs=(tiles, tiles),
        check_vma=False,
    )
```

```python
import functools

import jax
import jax.numpy as jnp
from jax import lax
from jax.experimental import pallas as pl
from jax.experimental.pallas import tpu as pltpu
from jax.sharding import PartitionSpec as P


TILE = 128
UNROLL = 4
F32 = jnp.float32
MESH = pl.DeviceIdType.MESH
STEPS = (("gx", -1), ("gx", 1), ("gy", -1), ("gy", 1))


def split(tile):
    high = tile.astype(jnp.bfloat16)
    low = (tile - high.astype(F32)).astype(jnp.bfloat16)
    return jnp.concatenate([high, low], axis=1)


def product(left, right, turned):
    if turned:
        high, low = right[:, :TILE], right[:, TILE:]
        rows = jnp.concatenate([high, low], axis=0)
        operand = jnp.concatenate([rows, rows], axis=1)
        both = lax.dot_general(left, operand, (((1,), (1,)), ((), ())), preferred_element_type=F32)
    else:
        operand = jnp.concatenate([right, right], axis=0)
        both = lax.dot_general(left, operand, (((1,), (0,)), ((), ())), preferred_element_type=F32)
    return both[:, :TILE] + both[:, TILE:]


def run_list(count, entry, left_of, right_of, turned, total):
    def step(turn, _):
        entries = [entry(turn * UNROLL + i) for i in range(UNROLL)]
        values = [product(left_of(a), right_of(b), turned) for _, a, b in entries]
        for (t, _, _), value in zip(entries, values):
            total[t] += value
        return 0

    lax.fori_loop(0, (count + UNROLL - 1) // UNROLL, step, 0)


def live_count(tasks, per_cell):
    length = tasks.shape[1]
    return lax.while_loop(
        lambda n: jnp.logical_and(n < length, tasks[0, jnp.minimum(n, length - 1)] < per_cell),
        lambda n: n + 1,
        jnp.int32(0),
    )


def split_all(source, target, per_cell, transposed=False):
    def step(i, _):
        tile = source[i]
        target[i] = split(tile.T if transposed else tile)
        return 0

    lax.fori_loop(0, per_cell, step, 0)


def plain_entry(tasks):
    return lambda e: (tasks[0, e], tasks[1, e], tasks[2, e])


def fetch(sources, grown, sems, per_cell):
    copies = [
        pltpu.make_async_copy(src, grown.at[pl.ds(k * per_cell, src.shape[0])], sems.at[k])
        for k, src in enumerate(sources)
    ]
    for c in copies:
        c.start()
    return copies


def mark(lists, key_row, base, flags, per_cell, value_row=None):
    for i in range(per_cell):
        flags[i] = 0
    for tasks in lists:

        def note(e, _, tasks=tasks):
            at = tasks[key_row, e] - base
            here = jnp.logical_and(at >= 0, at < per_cell)
            if value_row is not None:
                at = tasks[value_row, e]
            flags[jnp.where(here, at, per_cell)] = 1
            return 0

        lax.fori_loop(0, live_count(tasks, per_cell), note, 0)


def rank(flags, ranks, first, offset, per_cell):
    n = jnp.int32(0)
    for i in range(per_cell):
        ranks[first + i] = offset + n
        n = n + flags[i]


def share_kernel(tfock, tfz, ttrans, g, gn1, gn2, gn3, gn4, tn1, tn2, tn3, tn4, fn3, fn4, zn3, zn4, most, msg, line, lines, bulk_s, bulk_r, list_s, list_r, line_s, line_r, lines_s, lines_r, own):
    nx, ny = lines.shape[0], line.shape[0]
    per_cell = g.shape[0]
    ix, iy = lax.axis_index("gx"), lax.axis_index("gy")
    barrier = pltpu.get_barrier_semaphore()
    for j in range(1, ny):
        pl.semaphore_signal(barrier, inc=1, device_id=(ix, lax.rem(iy + j, ny)), device_id_type=MESH)
    for j in range(1, nx):
        pl.semaphore_signal(barrier, inc=1, device_id=(lax.rem(ix + j, nx), iy), device_id_type=MESH)

    row = lax.broadcasted_iota(jnp.int32, (per_cell, tfock.shape[1]), 0)

    def hit(key):
        return (jnp.broadcast_to(key, row.shape) == row).astype(jnp.int32)

    def count(hits):
        return jnp.sum(jnp.max(hits, axis=1, keepdims=True))

    counts = []
    for k in (3, 4):
        base = k * per_cell
        z_hits = jnp.maximum(hit(tfock[2:3, :] - base), hit(tfz[2:3, :] - base))
        cell = ttrans[1:2, :]
        here = jnp.logical_and(cell >= base, cell < base + per_cell)
        p_hits = hit(jnp.where(here, ttrans[0:1, :], per_cell))
        counts.append((count(z_hits), count(p_hits)))
    z_most = jnp.maximum(counts[0][0], counts[1][0])
    p_most = jnp.maximum(counts[0][1], counts[1][1])
    upper = lax.broadcasted_iota(jnp.int32, msg.shape, 0) < 4
    msg[...] = jnp.where(upper, z_most, p_most)
    pl.semaphore_wait(barrier, nx + ny - 2)

    keep = pltpu.make_async_copy(msg, line.at[0], own.at[0])
    keep.start()
    first = []
    for j in range(1, ny):
        first.append(
            pltpu.make_async_remote_copy(
                msg, line.at[j], line_s.at[j], line_r.at[j], device_id=(ix, lax.rem(iy + j, ny)), device_id_type=MESH
            )
        )
        first[-1].start()
    others = []
    for k, (axis, by) in enumerate(STEPS):
        n, i = (nx, ix) if axis == "gx" else (ny, iy)
        others.append((lax.rem(i + by + n, n), iy) if axis == "gx" else (ix, lax.rem(i + by + n, n)))
    lists = [(ttrans, tn, others[k]) for k, tn in enumerate((tn1, tn2, tn3, tn4))]
    lists += [(tfock, fn3, others[2]), (tfz, zn3, others[2]), (tfock, fn4, others[3]), (tfz, zn4, others[3])]
    small = []
    for i, (src, dst, to) in enumerate(lists):
        small.append(
            pltpu.make_async_remote_copy(src, dst, list_s.at[i], list_r.at[i], device_id=to, device_id_type=MESH)
        )
        small[-1].start()
    bulk = [
        pltpu.make_async_remote_copy(
            g, (gn1, gn2, gn3, gn4)[k ^ 1], bulk_s.at[k], bulk_r.at[k], device_id=others[k], device_id_type=MESH
        )
        for k in range(4)
    ]
    bulk[2].start()
    bulk[3].start()
    keep.wait()
    for c in first:
        c.wait()
    keep = pltpu.make_async_copy(line, lines.at[0], own.at[1])
    keep.start()
    second = []
    for j in range(1, nx):
        second.append(
            pltpu.make_async_remote_copy(
                line, lines.at[j], lines_s.at[j], lines_r.at[j], device_id=(lax.rem(ix + j, nx), iy), device_id_type=MESH
            )
        )
        second[-1].start()
    bulk[0].start()
    bulk[1].start()
    keep.wait()
    for c in second:
        c.wait()
    most[...] = jnp.max(jnp.max(lines[...], axis=0), axis=0)
    for c in small + bulk:
        c.wait()


def pack_kernel(f3, z3, f4, z4, z, out3, out4, flags, sems):
    per_cell, room = z.shape[0], out3.shape[0]
    for side, (lists, base, out) in enumerate((((f3, z3), 3 * per_cell, out3), ((f4, z4), 4 * per_cell, out4))):
        mark(lists, 2, base, flags, per_cell)
        n = jnp.int32(0)
        for i in range(per_cell):

            @pl.when(flags[i] == 1)
            def _(i=i, n=n):
                pltpu.make_async_copy(z.at[i], out.at[jnp.minimum(n, room - 1)], sems.at[side]).start()

            n = n + flags[i]

        def finish(_, c, out=out, side=side):
            pltpu.make_async_copy(z.at[0], out.at[0], sems.at[side]).wait()
            return c

        lax.fori_loop(0, n, finish, 0)


def w_kernel(tasks, z, g0, g1, g2, g3, g4, w, grown, zs, total, sems, osem):
    per_cell = z.shape[0]
    copies = fetch((g0, g1, g2, g3, g4), grown, sems, per_cell)
    split_all(z, zs, per_cell)
    total[...] = jnp.zeros_like(total)
    for c in copies:
        c.wait()
    run_list(live_count(tasks, per_cell), plain_entry(tasks), lambda a: zs[a], lambda b: split(grown[b]), False, total)
    out = pltpu.make_async_copy(total.at[pl.ds(0, per_cell)], w, osem)
    out.start()
    out.wait()


def p_kernel(t0, t1, t2, t3, t4, f, w, p0, p1, p2, p3, p4, fs, ws, total, listed, flags, ranks, osem):
    per_cell = f.shape[0]
    stride = per_cell + 1
    split_all(f, fs, per_cell, transposed=True)
    split_all(w, ws, per_cell)

    def clear(i, _):
        total[i] = jnp.zeros_like(total[i])
        return 0

    lax.fori_loop(0, 5 * stride, clear, 0)
    n = jnp.int32(0)
    for k, tasks in enumerate((t0, t1, t2, t3, t4)):
        base = k * per_cell
        if k >= 3:
            mark((tasks,), 1, base, flags, per_cell, value_row=0)
            rank(flags, ranks, 0, k * stride, per_cell)

        def pick(e, n, tasks=tasks, base=base, k=k):
            t, a = tasks[0, e], tasks[1, e]
            here = jnp.logical_and(a >= base, a < base + per_cell)
            listed[0, n] = ranks[t] if k >= 3 else k * stride + t
            listed[1, n] = a - base
            listed[2, n] = tasks[2, e] - base
            return n + here.astype(jnp.int32)

        n = lax.fori_loop(0, live_count(tasks, per_cell), pick, n)
    for i in range(UNROLL - 1):
        listed[0, n + i] = per_cell
        listed[1, n + i] = 0
        listed[2, n + i] = 0
    run_list(n, plain_entry(listed), lambda a: fs[a], lambda b: ws[b], False, total)
    outs = [
        pltpu.make_async_copy(total.at[pl.ds(k * stride, p.shape[0])], p, osem.at[k])
        for k, p in enumerate((p0, p1, p2, p3, p4))
    ]
    for out in outs:
        out.start()
    for out in outs:
        out.wait()


def rest_kernel(tfock, tfz, tzgt, f, w, p0, z0, z1, z2, z3, z4, g0, g1, g2, g3, g4, fock, factor, zgrown, ggrown, fs, ws, us, total, flags, ranks, zsem, gsem, osem):
    per_cell = f.shape[0]
    zcopies = fetch((z0, z1, z2, z3, z4), zgrown, zsem, per_cell)
    gcopies = fetch((g0, g1, g2, g3, g4), ggrown, gsem, per_cell)
    split_all(f, fs, per_cell)
    split_all(w, ws, per_cell)
    total[0] = jnp.zeros_like(total[0])
    total[1] = jnp.zeros_like(total[1])
    total[2, pl.ds(0, per_cell)] = p0[...]
    for i in range(3 * per_cell):
        ranks[i] = i
    for k in (3, 4):
        mark((tfock, tfz), 2, k * per_cell, flags, per_cell)
        rank(flags, ranks, k * per_cell, k * per_cell, per_cell)
    for c in zcopies:
        c.wait()

    def z_tile(b):
        return split(zgrown[ranks[b]])

    run_list(live_count(tfz, per_cell), plain_entry(tfz), lambda a: fs[a], z_tile, False, total.at[0])
    split_all(total.at[0], us, per_cell)
    run_list(live_count(tfock, per_cell), plain_entry(tfock), lambda a: ws[a], z_tile, True, total.at[1])
    out1 = pltpu.make_async_copy(total.at[1, pl.ds(0, per_cell)], fock, osem.at[0])
    out1.start()
    for c in gcopies:
        c.wait()
    run_list(live_count(tzgt, per_cell), plain_entry(tzgt), lambda a: us[a], lambda b: split(ggrown[b]), True, total.at[2])
    out2 = pltpu.make_async_copy(total.at[2, pl.ds(0, per_cell)], factor, osem.at[1])
    out2.start()
    out1.wait()
    out2.wait()


def join_kernel(tasks, part, p3, p4, factor, total, flags, ranks, sems):
    per_cell = part.shape[0]
    for side, (k, p) in enumerate(((3, p3), (4, p4))):
        mark((tasks,), 1, k * per_cell, flags.at[side], per_cell, value_row=0)
        rank(flags.at[side], ranks, side * per_cell, 0, per_cell)
    copies = []
    for t in range(per_cell):
        total[t] = part[t]
        for side, p in enumerate((p3, p4)):

            @pl.when(flags[side, t] == 1)
            def _(t=t, p=p, side=side):
                total[t] += p[jnp.minimum(ranks[side * per_cell + t], p.shape[0] - 1)]

        copies.append(pltpu.make_async_copy(total.at[t], factor.at[t], sems.at[t]))
        copies[-1].start()
    for c in copies:
        c.wait()


SMEM = pl.BlockSpec(memory_space=pltpu.SMEM)
VMEM = pl.BlockSpec(memory_space=pltpu.VMEM)
ANY = pl.BlockSpec(memory_space=pl.ANY)
DMA = pltpu.SemaphoreType.DMA
I32 = jnp.int32


def cost(tasks, tiles):
    return pl.CostEstimate(flops=tasks * 2 * TILE**3 * 8, bytes_accessed=tiles * TILE * TILE * 4, transcendentals=0)


def shifted(array, axis, by):
    n = lax.axis_size(axis)
    return lax.ppermute(array, axis, [(i, (i + by) % n) for i in range(n)])


def tiles(n):
    return jax.ShapeDtypeStruct((n, TILE, TILE), F32)


def finish(z_room, p_room, z, f, g, tzg, tfock, tfz, tzgt, ttrans, gn, tn, fn, zn_lists):
    per_cell = z.shape[0]
    cap = tzg.shape[1]
    grown = pltpu.VMEM((5 * per_cell, TILE, TILE), F32)
    cut = pltpu.VMEM((per_cell, TILE, 2 * TILE), jnp.bfloat16)
    flags = pltpu.SMEM((per_cell + 1,), I32)
    params = pltpu.CompilerParams(vmem_limit_bytes=40 * 2**20)
    z3, z4 = pl.pallas_call(
        pack_kernel,
        name="pack_kernel",
        out_shape=[tiles(z_room)] * 2,
        in_specs=[SMEM] * 4 + [VMEM],
        out_specs=[ANY] * 2,
        scratch_shapes=[flags, DMA((2,))],
        cost_estimate=cost(0, 4 * per_cell),
    )(fn[0], zn_lists[0], fn[1], zn_lists[1], z)
    zn = [shifted(z, "gx", 1), shifted(z, "gx", -1), shifted(z3, "gy", 1), shifted(z4, "gy", -1)]
    w = pl.pallas_call(
        w_kernel,
        name="w_kernel",
        out_shape=tiles(per_cell),
        in_specs=[SMEM, VMEM] + [ANY] * 5,
        out_specs=ANY,
        scratch_shapes=[grown, cut, pltpu.VMEM((per_cell + 1, TILE, TILE), F32), DMA((5,)), DMA],
        compiler_params=params,
        cost_estimate=cost(cap, 7 * per_cell),
    )(tzg, z, g, *gn)
    p = pl.pallas_call(
        p_kernel,
        name="p_kernel",
        out_shape=[tiles(per_cell)] * 3 + [tiles(p_room)] * 2,
        in_specs=[SMEM] * 5 + [VMEM] * 2,
        out_specs=[ANY] * 5,
        scratch_shapes=[
            cut,
            cut,
            pltpu.VMEM((5 * (per_cell + 1), TILE, TILE), F32),
            pltpu.SMEM((3, 5 * cap + UNROLL), I32),
            flags,
            flags,
            DMA((5,)),
        ],
        compiler_params=params,
        cost_estimate=cost(2 * cap, 7 * per_cell),
    )(ttrans, *tn, f, w)
    pn = [shifted(p[k + 1], axis, -by) for k, (axis, by) in enumerate(STEPS)]
    fock_grad, part = pl.pallas_call(
        rest_kernel,
        name="rest_kernel",
        out_shape=[tiles(per_cell)] * 2,
        in_specs=[SMEM] * 3 + [VMEM] * 3 + [ANY] * 10,
        out_specs=[ANY] * 2,
        scratch_shapes=[grown, grown, cut, cut, cut, pltpu.VMEM((3, per_cell + 1, TILE, TILE), F32)]
        + [flags, pltpu.SMEM((5 * per_cell,), I32)]
        + [DMA((5,))] * 2
        + [DMA((2,))],
        compiler_params=params,
        cost_estimate=cost(3 * cap, 14 * per_cell),
    )(tfock, tfz, tzgt, f, w, p[0], z, *zn, g, *gn)
    part = part + pn[0] + pn[1]
    factor_grad = pl.pallas_call(
        join_kernel,
        name="join_kernel",
        out_shape=tiles(per_cell),
        in_specs=[SMEM] + [VMEM] * 3,
        out_specs=ANY,
        scratch_shapes=[
            pltpu.VMEM((per_cell, TILE, TILE), F32),
            pltpu.SMEM((2, per_cell + 1), I32),
            pltpu.SMEM((2 * per_cell,), I32),
            DMA((per_cell,)),
        ],
        cost_estimate=cost(0, 4 * per_cell),
    )(ttrans, part, pn[2], pn[3])
    return fock_grad, factor_grad


def rooms(per_cell):
    return [(per_cell * a // 24, per_cell * b // 24) for a, b in ((18, 12), (20, 14), (22, 16))] + [(per_cell, per_cell)]


def body(z_factor, fock, cotangent, tasks_zg, tasks_fock, tasks_fz, tasks_zgt, tasks_trans):
    per_cell = z_factor.shape[2]
    nx, ny = lax.axis_size("gx"), lax.axis_size("gy")
    z, f, g = z_factor[0, 0], fock[0, 0], cotangent[0, 0]
    tzg, tfock, tfz, tzgt, ttrans = (t[0, 0] for t in (tasks_zg, tasks_fock, tasks_fz, tasks_zgt, tasks_trans))
    a_list = jax.ShapeDtypeStruct(tzg.shape, I32)
    shared = pl.pallas_call(
        share_kernel,
        name="share_kernel",
        out_shape=[tiles(per_cell)] * 4 + [a_list] * 8 + [jax.ShapeDtypeStruct((8, TILE), I32)],
        in_specs=[VMEM] * 3 + [ANY],
        out_specs=[ANY] * 4 + [VMEM] * 9,
        scratch_shapes=[
            pltpu.VMEM((8, TILE), I32),
            pltpu.VMEM((ny, 8, TILE), I32),
            pltpu.VMEM((nx, ny, 8, TILE), I32),
            DMA((4,)),
            DMA((4,)),
            DMA((8,)),
            DMA((8,)),
            DMA((ny,)),
            DMA((ny,)),
            DMA((nx,)),
            DMA((nx,)),
            DMA((2,)),
        ],
        compiler_params=pltpu.CompilerParams(collective_id=0, has_side_effects=True),
    )(tfock, tfz, ttrans, g)
    gn, tn, fn, zl, most = shared[:4], shared[4:8], shared[8:10], shared[10:12], shared[12]
    levels = rooms(per_cell)
    z_most, p_most = most[0, 0], most[4, 0]
    level = sum(jnp.logical_or(z_most > a, p_most > b).astype(I32) for a, b in levels[:-1])
    branches = [functools.partial(finish, a, b) for a, b in levels]
    fock_grad, factor_grad = lax.switch(level, branches, z, f, g, tzg, tfock, tfz, tzgt, ttrans, gn, tn, fn, zl)
    return fock_grad[None, None], factor_grad[None, None]


def solution(mesh):
    cells = P("gx", "gy", None, None, None)
    lists = P("gx", "gy", None, None)
    return jax.shard_map(
        body,
        mesh=mesh,
        in_specs=(cells,) * 3 + (lists,) * 5,
        out_specs=(cells, cells),
        check_vma=False,
    )
```

```python
import functools

import jax
import jax.numpy as jnp
from jax import lax
from jax.experimental import pallas as pl
from jax.experimental.pallas import tpu as pltpu
from jax.sharding import PartitionSpec as P


TILE = 128
UNROLL = 4
F32 = jnp.float32
I32 = jnp.int32
MESH = pl.DeviceIdType.MESH
STEPS = (("gx", -1), ("gx", 1), ("gy", -1), ("gy", 1))


def split(tile):
    high = tile.astype(jnp.bfloat16)
    low = (tile - high.astype(F32)).astype(jnp.bfloat16)
    return jnp.concatenate([high, low], axis=1)


def product(left, right, turned):
    if turned:
        high, low = right[:, :TILE], right[:, TILE:]
        rows = jnp.concatenate([high, low], axis=0)
        operand = jnp.concatenate([rows, rows], axis=1)
        both = lax.dot_general(left, operand, (((1,), (1,)), ((), ())), preferred_element_type=F32)
    else:
        operand = jnp.concatenate([right, right], axis=0)
        both = lax.dot_general(left, operand, (((1,), (0,)), ((), ())), preferred_element_type=F32)
    return both[:, :TILE] + both[:, TILE:]


def run_list(count, entry, left_of, right_of, turned, total):
    def step(turn, _):
        entries = [entry(turn * UNROLL + i) for i in range(UNROLL)]
        values = [product(left_of(a), right_of(b), turned) for _, a, b in entries]
        for (t, _, _), value in zip(entries, values):
            total[t] += value
        return 0

    lax.fori_loop(0, (count + UNROLL - 1) // UNROLL, step, 0)


def live_count(tasks, per_cell):
    length = tasks.shape[1]
    return lax.while_loop(
        lambda n: jnp.logical_and(n < length, tasks[0, jnp.minimum(n, length - 1)] < per_cell),
        lambda n: n + 1,
        jnp.int32(0),
    )


def split_all(source, target, per_cell, transposed=False):
    def step(i, _):
        tile = source[i]
        target[i] = split(tile.T if transposed else tile)
        return 0

    lax.fori_loop(0, per_cell, step, 0)


def plain_entry(tasks):
    return lambda e: (tasks[0, e], tasks[1, e], tasks[2, e])


def fetch(sources, grown, sems, per_cell):
    copies = [
        pltpu.make_async_copy(src, grown.at[pl.ds(k * per_cell, src.shape[0])], sems.at[k])
        for k, src in enumerate(sources)
    ]
    for c in copies:
        c.start()
    return copies


def share_kernel(tfock, tfz, ttrans, z, g, *refs, z_rooms, p_rooms, lead):
    levels = len(z_rooms)
    gn, tn, fn, zl, zp = refs[:4], refs[4:8], refs[8:10], refs[10:12], refs[12 : 12 + 2 * levels]
    (level, msg, line, lines, pick, packed, picked, bulk_s, bulk_r, list_s, list_r, line_s, line_r, lines_s, lines_r, own, put) = refs[12 + 2 * levels :]
    nx, ny = line.shape[0], lines.shape[0]
    per_cell = g.shape[0]
    ix, iy = lax.axis_index("gx"), lax.axis_index("gy")
    barrier = pltpu.get_barrier_semaphore()
    for j in range(1, nx):
        pl.semaphore_signal(barrier, inc=1, device_id=(lax.rem(ix + j, nx), iy), device_id_type=MESH)
    for j in range(1, ny):
        pl.semaphore_signal(barrier, inc=1, device_id=(ix, lax.rem(iy + j, ny)), device_id_type=MESH)

    row = lax.broadcasted_iota(I32, (per_cell, tfock.shape[1]), 0)

    def named(keys):
        hits = sum((jnp.broadcast_to(key, row.shape) == row).astype(I32) for key in keys)
        return jnp.minimum(jnp.max(hits, axis=1, keepdims=True), 1)

    z_most, p_most = jnp.int32(0), jnp.int32(0)
    for k in range(1, 5):
        base = k * per_cell
        if k >= 3:
            z_most = jnp.maximum(z_most, jnp.sum(named((tfock[2:3, :] - base, tfz[2:3, :] - base))))
        cell = ttrans[1:2, :]
        here = jnp.logical_and(cell >= base, cell < base + per_cell)
        p_most = jnp.maximum(p_most, jnp.sum(named((jnp.where(here, ttrans[0:1, :], per_cell),))))
    left_half = lax.broadcasted_iota(I32, msg.shape, 1) < TILE // 2
    msg[...] = jnp.where(left_half, z_most, p_most)
    pl.semaphore_wait(barrier, nx + ny - 2)

    keep = pltpu.make_async_copy(msg, line.at[pl.ds(0, 1)], own.at[0])
    keep.start()
    first = []
    for j in range(1, nx):
        to = (lax.rem(ix + j, nx), iy)
        first.append(pltpu.make_async_remote_copy(msg, line.at[pl.ds(j, 1)], line_s.at[j], line_r.at[j], device_id=to, device_id_type=MESH))
        first[-1].start()
    others = []
    for axis, by in STEPS:
        others.append((lax.rem(ix + by + nx, nx), iy) if axis == "gx" else (ix, lax.rem(iy + by + ny, ny)))
    lists = [(ttrans, tn[k], others[k]) for k in range(4)]
    lists += [(tfock, fn[0], others[2]), (tfz, zl[0], others[2]), (tfock, fn[1], others[3]), (tfz, zl[1], others[3])]
    small = []
    for i, (src, dst, to) in enumerate(lists):
        small.append(pltpu.make_async_remote_copy(src, dst, list_s.at[i], list_r.at[i], device_id=to, device_id_type=MESH))
        small[-1].start()

    def bulk(i, k, start, size):
        part = pl.ds(start, size)
        return pltpu.make_async_remote_copy(
            g.at[part], gn[k ^ 1].at[part], bulk_s.at[i], bulk_r.at[i], device_id=others[k], device_id_type=MESH
        )

    large = [bulk(0, 2, 0, lead), bulk(1, 3, 0, lead), bulk(2, 0, 0, per_cell), bulk(3, 1, 0, per_cell)]
    for c in large:
        c.start()
    keep.wait()
    for c in first:
        c.wait()
    keep = pltpu.make_async_copy(line, lines.at[0], own.at[1])
    keep.start()
    second = []
    for j in range(1, ny):
        to = (ix, lax.rem(iy + j, ny))
        second.append(pltpu.make_async_remote_copy(line, lines.at[j], lines_s.at[j], lines_r.at[j], device_id=to, device_id_type=MESH))
        second[-1].start()
    rest = [bulk(4, 2, lead, per_cell - lead), bulk(5, 3, lead, per_cell - lead)]
    for c in rest:
        c.start()
    for c in small:
        c.wait()

    below = lax.broadcasted_iota(I32, (per_cell, per_cell), 1) < lax.broadcasted_iota(I32, (per_cell, per_cell), 0)
    lane = lax.broadcasted_iota(I32, (per_cell, TILE), 1).astype(F32)
    number = lax.broadcasted_iota(I32, (per_cell, TILE), 0)
    for side in range(2):
        base = (3 + side) * per_cell
        wanted = jnp.broadcast_to(named((fn[side][2:3, :] - base, zl[side][2:3, :] - base)), lane.shape)
        rank = jnp.dot(below.astype(F32), wanted.astype(F32), preferred_element_type=F32)
        here = jnp.logical_and(rank == lane, wanted == 1)
        pick[side : side + 1, :] = jnp.sum(jnp.where(here, number, 0), axis=0, keepdims=True)
    copy = pltpu.make_async_copy(pick, picked, own.at[2])
    copy.start()
    copy.wait()
    puts = []
    for side in range(2):

        def take(s, _, side=side):
            packed[side, s] = z[picked[side, s]]
            return 0

        lax.fori_loop(0, z_rooms[-1], take, 0)
        for i, room in enumerate(z_rooms):
            out = zp[2 * i + side]
            puts.append(pltpu.make_async_copy(packed.at[side, pl.ds(0, room)], out, put.at[2 * i + side]))
            puts[-1].start()

    keep.wait()
    for c in second:
        c.wait()
    found = jnp.max(lines[...], axis=0)
    half = lax.broadcasted_iota(I32, found.shape, 1) < TILE // 2
    z_all = jnp.max(jnp.where(half, found, 0))
    p_all = jnp.max(jnp.where(half, 0, found))
    level[0, 0] = sum(
        jnp.logical_or(z_all > a, p_all > b).astype(I32) for a, b in zip(z_rooms, p_rooms)
    )
    for c in large + rest + puts:
        c.wait()


def w_kernel(tasks, z, g0, g1, g2, g3, g4, ws, grown, zs, total, sems, osem):
    per_cell = z.shape[0]
    copies = fetch((g0, g1, g2, g3, g4), grown, sems, per_cell)
    split_all(z, zs, per_cell)
    total[...] = jnp.zeros_like(total)
    for c in copies:
        c.wait()
    run_list(live_count(tasks, per_cell), plain_entry(tasks), lambda a: zs[a], lambda b: split(grown[b]), False, total)
    split_all(total, zs, per_cell)
    out = pltpu.make_async_copy(zs, ws, osem)
    out.start()
    out.wait()


def clear(flags, n):
    for i in range(n):
        flags[i] = 0


def p_kernel(t0, t1, t2, t3, t4, tfock, tfz, f, ws, p0, p1, p2, p3, p4, fs, bpos, tmap, ft, fcat, total, listed, flags, ranks, osem):
    per_cell, room = f.shape[0], p1.shape[0]

    def start(k):
        return 0 if k == 0 else per_cell + (k - 1) * room

    def cut(i, _):
        tile = f[i]
        fcat[i] = split(tile)
        ft[i] = split(tile.T)
        return 0

    lax.fori_loop(0, per_cell, cut, 0)
    out_f = pltpu.make_async_copy(fcat, fs, osem.at[5])
    out_f.start()

    def zero(i, _):
        total[i] = jnp.zeros_like(total[i])
        return 0

    lax.fori_loop(0, start(5), zero, 0)
    n = jnp.int32(0)
    for k, tasks in enumerate((t0, t1, t2, t3, t4)):
        base = k * per_cell
        live = live_count(tasks, per_cell)

        def inside(e, tasks=tasks, base=base):
            a = tasks[1, e]
            return jnp.logical_and(a >= base, a < base + per_cell)

        if k > 0:
            clear(flags, per_cell)

            def note(e, _, tasks=tasks, inside=inside):
                flags[jnp.where(inside(e), tasks[0, e], per_cell)] = 1
                return 0

            lax.fori_loop(0, live, note, 0)
            slot = jnp.int32(start(k))
            for i in range(per_cell):
                ranks[i] = slot
                slot = slot + flags[i]

        def place(e, n, tasks=tasks, base=base, k=k, inside=inside):
            t = tasks[0, e]
            listed[0, n] = ranks[t] if k > 0 else t
            listed[1, n] = tasks[1, e] - base
            listed[2, n] = tasks[2, e] - base
            return n + inside(e).astype(I32)

        n = lax.fori_loop(0, live, place, n)
    for i in range(UNROLL - 1):
        listed[0, n + i] = start(5)
        listed[1, n + i] = 0
        listed[2, n + i] = 0
    run_list(n, plain_entry(listed), lambda a: ft[a], lambda b: ws[b], False, total)
    outs = [
        pltpu.make_async_copy(total.at[pl.ds(start(k), p.shape[0])], p, osem.at[k])
        for k, p in enumerate((p0, p1, p2, p3, p4))
    ]
    for out in outs:
        out.start()

    clear(flags, 5 * per_cell)
    lists = [(tasks, live_count(tasks, per_cell)) for tasks in (tfock, tfz)]
    for tasks, live in lists:

        def seen(e, _, tasks=tasks):
            flags[tasks[2, e]] = 1
            return 0

        lax.fori_loop(0, live, seen, 0)
    for k in range(5):
        at = jnp.int32(k * per_cell)
        for i in range(per_cell):
            ranks[k * per_cell + i] = at if k >= 3 else k * per_cell + i
            at = at + flags[k * per_cell + i]
    for i, (tasks, _) in enumerate(lists):

        def move(e, _, tasks=tasks, i=i):
            bpos[i, e] = ranks[tasks[2, e]]
            return 0

        lax.fori_loop(0, tasks.shape[1], move, 0)
    for k in range(1, 5):
        clear(flags, per_cell)

        def touch(e, _, k=k):
            a = t0[1, e]
            here = jnp.logical_and(a >= k * per_cell, a < (k + 1) * per_cell)
            flags[jnp.where(here, t0[0, e], per_cell)] = 1
            return 0

        lax.fori_loop(0, live_count(t0, per_cell), touch, 0)
        n = jnp.int32(0)
        for i in range(per_cell):
            tmap[k - 1, n] = i
            n = n + flags[i]
        tmap[k - 1, per_cell] = n
    for out in outs + [out_f]:
        out.wait()


def rest_kernel(tfock, tfz, tzgt, bpos, fs, ws, p0, z0, z1, z2, z3, z4, g0, g1, g2, g3, g4, fock, factor, zgrown, ggrown, us, total, zsem, gsem, osem):
    per_cell = p0.shape[0]
    zcopies = fetch((z0, z1, z2, z3, z4), zgrown, zsem, per_cell)
    gcopies = fetch((g0, g1, g2, g3, g4), ggrown, gsem, per_cell)
    total[0] = jnp.zeros_like(total[0])
    total[1] = jnp.zeros_like(total[1])
    total[2, pl.ds(0, per_cell)] = p0[...]
    for c in zcopies:
        c.wait()

    def moved_entry(tasks, i):
        return lambda e: (tasks[0, e], tasks[1, e], bpos[i, e])

    run_list(live_count(tfz, per_cell), moved_entry(tfz, 1), lambda a: fs[a], lambda b: split(zgrown[b]), False, total.at[0])
    split_all(total.at[0], us, per_cell)
    run_list(live_count(tfock, per_cell), moved_entry(tfock, 0), lambda a: ws[a], lambda b: split(zgrown[b]), True, total.at[1])
    out1 = pltpu.make_async_copy(total.at[1, pl.ds(0, per_cell)], fock, osem.at[0])
    out1.start()
    for c in gcopies:
        c.wait()
    run_list(live_count(tzgt, per_cell), plain_entry(tzgt), lambda a: us[a], lambda b: split(ggrown[b]), True, total.at[2])
    out2 = pltpu.make_async_copy(total.at[2, pl.ds(0, per_cell)], factor, osem.at[1])
    out2.start()
    out1.wait()
    out2.wait()


def join_kernel(tmap, part, pa, pb, factor, total, sems, *, sides):
    per_cell, room = part.shape[0], pa.shape[0]
    load = pltpu.make_async_copy(part, total, sems.at[0])
    load.start()
    load.wait()
    for side, p in zip(sides, (pa, pb)):

        def add(s, _, side=side, p=p):
            total[tmap[side, s]] += p[s]
            return 0

        lax.fori_loop(0, jnp.minimum(tmap[side, per_cell], room), add, 0)
    out = pltpu.make_async_copy(total, factor, sems.at[1])
    out.start()
    out.wait()


SMEM = pl.BlockSpec(memory_space=pltpu.SMEM)
VMEM = pl.BlockSpec(memory_space=pltpu.VMEM)
ANY = pl.BlockSpec(memory_space=pl.ANY)
HBM = pl.BlockSpec(memory_space=pltpu.HBM)
DMA = pltpu.SemaphoreType.DMA


def cost(tasks, tiles):
    return pl.CostEstimate(flops=tasks * 2 * TILE**3 * 8, bytes_accessed=tiles * TILE * TILE * 4, transcendentals=0)


def shifted(array, axis, by):
    n = lax.axis_size(axis)
    return lax.ppermute(array, axis, [(i, (i + by) % n) for i in range(n)])


def tiles(n):
    return jax.ShapeDtypeStruct((n, TILE, TILE), F32)


def join(tmap, part, pa, pb, sides):
    per_cell = part.shape[0]
    return pl.pallas_call(
        functools.partial(join_kernel, sides=sides),
        name="join_kernel",
        out_shape=tiles(per_cell),
        in_specs=[SMEM, ANY, VMEM, VMEM],
        out_specs=HBM,
        scratch_shapes=[pltpu.VMEM((per_cell, TILE, TILE), F32), DMA((2,))],
        cost_estimate=cost(0, 4 * per_cell),
    )(tmap, part, pa, pb)


def finish(p_room, z3, z4, z, f, g, tzg, tfock, tfz, tzgt, ttrans, gn, tn):
    per_cell = z.shape[0]
    cap = tzg.shape[1]
    grown = pltpu.VMEM((5 * per_cell, TILE, TILE), F32)
    cut = pltpu.VMEM((per_cell, TILE, 2 * TILE), jnp.bfloat16)
    cut_shape = jax.ShapeDtypeStruct((per_cell, TILE, 2 * TILE), jnp.bfloat16)
    params = pltpu.CompilerParams(vmem_limit_bytes=40 * 2**20)
    zy = [shifted(z3, "gy", 1), shifted(z4, "gy", -1)]
    zn = [shifted(z, "gx", 1), shifted(z, "gx", -1)] + zy
    ws = pl.pallas_call(
        w_kernel,
        name="w_kernel",
        out_shape=cut_shape,
        in_specs=[SMEM, VMEM] + [ANY] * 5,
        out_specs=ANY,
        scratch_shapes=[grown, cut, pltpu.VMEM((per_cell + 1, TILE, TILE), F32), DMA((5,)), DMA],
        compiler_params=params,
        cost_estimate=cost(cap, 7 * per_cell),
    )(tzg, z, g, *gn)
    *p, fs, bpos, tmap = pl.pallas_call(
        p_kernel,
        name="p_kernel",
        out_shape=[tiles(per_cell)]
        + [tiles(p_room)] * 4
        + [cut_shape, jax.ShapeDtypeStruct((2, cap), I32), jax.ShapeDtypeStruct((4, per_cell + 1), I32)],
        in_specs=[SMEM] * 7 + [VMEM] * 2,
        out_specs=[ANY] * 6 + [SMEM] * 2,
        scratch_shapes=[
            cut,
            cut,
            pltpu.VMEM((per_cell + 4 * p_room + 1, TILE, TILE), F32),
            pltpu.SMEM((3, 5 * cap + UNROLL), I32),
            pltpu.SMEM((5 * per_cell,), I32),
            pltpu.SMEM((5 * per_cell,), I32),
            DMA((6,)),
        ],
        compiler_params=params,
        cost_estimate=cost(2 * cap, 7 * per_cell),
    )(ttrans, *tn, tfock, tfz, f, ws)
    pn = [shifted(p[k + 1], axis, -by) for k, (axis, by) in enumerate(STEPS)]
    fock_grad, part = pl.pallas_call(
        rest_kernel,
        name="rest_kernel",
        out_shape=[tiles(per_cell)] * 2,
        in_specs=[SMEM] * 4 + [VMEM] * 3 + [ANY] * 10,
        out_specs=[HBM, ANY],
        scratch_shapes=[grown, grown, cut, pltpu.VMEM((3, per_cell + 1, TILE, TILE), F32), DMA((5,)), DMA((5,)), DMA((2,))],
        compiler_params=params,
        cost_estimate=cost(3 * cap, 14 * per_cell),
    )(tfock, tfz, tzgt, bpos, fs, ws, p[0], z, *zn, g, *gn)
    part = join(tmap, part, pn[0], pn[1], (0, 1))
    return fock_grad, join(tmap, part, pn[2], pn[3], (2, 3))


def rooms(per_cell):
    return [(per_cell * a // 24, per_cell * b // 24) for a, b in ((19, 13), (20, 14), (22, 16))]


def body(z_factor, fock, cotangent, tasks_zg, tasks_fock, tasks_fz, tasks_zgt, tasks_trans):
    per_cell = z_factor.shape[2]
    nx, ny = lax.axis_size("gx"), lax.axis_size("gy")
    z, f, g = z_factor[0, 0], fock[0, 0], cotangent[0, 0]
    tzg, tfock, tfz, tzgt, ttrans = (t[0, 0] for t in (tasks_zg, tasks_fock, tasks_fz, tasks_zgt, tasks_trans))
    a_list = jax.ShapeDtypeStruct(tzg.shape, I32)
    z_rooms, p_rooms = zip(*rooms(per_cell))
    levels = len(z_rooms)
    shared = pl.pallas_call(
        functools.partial(share_kernel, z_rooms=z_rooms + (per_cell,), p_rooms=p_rooms, lead=per_cell // 4),
        name="share_kernel",
        out_shape=[tiles(per_cell)] * 4
        + [a_list] * 8
        + [tiles(room) for room in z_rooms + (per_cell,) for _ in range(2)]
        + [jax.ShapeDtypeStruct((1, 1), I32)],
        in_specs=[VMEM] * 4 + [ANY],
        out_specs=[ANY] * 4 + [VMEM] * 8 + [ANY] * (2 * levels + 2) + [SMEM],
        scratch_shapes=[
            pltpu.VMEM((1, TILE), I32),
            pltpu.VMEM((nx, TILE), I32),
            pltpu.VMEM((ny, nx, TILE), I32),
            pltpu.VMEM((8, TILE), I32),
            pltpu.VMEM((2, per_cell, TILE, TILE), F32),
            pltpu.SMEM((8, TILE), I32),
            DMA((6,)),
            DMA((6,)),
            DMA((8,)),
            DMA((8,)),
            DMA((nx,)),
            DMA((nx,)),
            DMA((ny,)),
            DMA((ny,)),
            DMA((3,)),
            DMA((2 * levels + 2,)),
        ],
        compiler_params=pltpu.CompilerParams(collective_id=0, has_side_effects=True),
    )(tfock, tfz, ttrans, z, g)
    gn, tn = shared[:4], shared[4:8]
    packs = shared[12 : 12 + 2 * levels + 2]
    branches = [
        lambda packs, *rest, i=i, room=room: finish(room, packs[2 * i], packs[2 * i + 1], *rest)
        for i, room in enumerate(p_rooms + (per_cell,))
    ]
    fock_grad, factor_grad = lax.switch(shared[-1][0, 0], branches, packs, z, f, g, tzg, tfock, tfz, tzgt, ttrans, gn, tn)
    return fock_grad[None, None], factor_grad[None, None]


def solution(mesh):
    cells = P("gx", "gy", None, None, None)
    lists = P("gx", "gy", None, None)
    return jax.shard_map(
        body,
        mesh=mesh,
        in_specs=(cells,) * 3 + (lists,) * 5,
        out_specs=(cells, cells),
        check_vma=False,
    )
```

```python
import functools

import jax
import jax.numpy as jnp
from jax import lax
from jax.experimental import pallas as pl
from jax.experimental.pallas import tpu as pltpu
from jax.sharding import PartitionSpec as P


TILE = 128
UNROLL = 8
F32 = jnp.float32
I32 = jnp.int32
MESH = pl.DeviceIdType.MESH
STEPS = (("gx", -1), ("gx", 1), ("gy", -1), ("gy", 1))


def split(tile):
    high = tile.astype(jnp.bfloat16)
    low = (tile - high.astype(F32)).astype(jnp.bfloat16)
    return jnp.concatenate([high, low], axis=1)


def product(left, right, turned):
    if turned:
        high, low = right[:, :TILE], right[:, TILE:]
        rows = jnp.concatenate([high, low], axis=0)
        operand = jnp.concatenate([rows, rows], axis=1)
        both = lax.dot_general(left, operand, (((1,), (1,)), ((), ())), preferred_element_type=F32)
    else:
        operand = jnp.concatenate([right, right], axis=0)
        both = lax.dot_general(left, operand, (((1,), (0,)), ((), ())), preferred_element_type=F32)
    return both[:, :TILE] + both[:, TILE:]


def run_list(count, entry, left_of, right_of, turned, total):
    def step(turn, _):
        entries = [entry(turn * UNROLL + i) for i in range(UNROLL)]
        values = [product(left_of(a), right_of(b), turned) for _, a, b in entries]
        for (t, _, _), value in zip(entries, values):
            total[t] += value
        return 0

    lax.fori_loop(0, (count + UNROLL - 1) // UNROLL, step, 0)


def live_count(tasks, per_cell):
    length = tasks.shape[2]
    return lax.while_loop(
        lambda n: jnp.logical_and(n < length, tasks[0, 0, jnp.minimum(n, length - 1)] < per_cell),
        lambda n: n + 1,
        jnp.int32(0),
    )


def split_all(source, target, per_cell):
    def step(i, _):
        target[i] = split(source[i])
        return 0

    lax.fori_loop(0, per_cell, step, 0)


def plain_entry(tasks):
    return lambda e: (tasks[0, 0, e], tasks[1, 0, e], tasks[2, 0, e])


def fetch(sources, grown, sems, per_cell):
    copies = [
        pltpu.make_async_copy(src, grown.at[pl.ds(k * per_cell, src.shape[0])], sems.at[k])
        for k, src in enumerate(sources)
    ]
    for c in copies:
        c.start()
    return copies


FOCK_ROW, FZ_ROW, MAP_ROW, LIST_ROW, PLAN_ROWS = 0, 1, 2, 8, 32


def share_kernel(tfock, tfz, ttrans, f, z, g, *refs, z_rooms, p_rooms, lead):
    packs = 2 * len(z_rooms)
    gn, zn, tn, fn, zl, zp = refs[:4], refs[4:6], refs[6:10], refs[10:12], refs[12:14], refs[14 : 14 + packs]
    (level, plan, fs, ft, zs, msg, line, lines, pick, packed, picked, table, fv, zv, cut, bulk_s, bulk_r, list_s, list_r) = refs[14 + packs : 33 + packs]
    line_s, line_r, lines_s, lines_r, own, put = refs[33 + packs :]
    nx, ny = line.shape[0], lines.shape[0]
    per_cell = g.shape[0]
    ix, iy = lax.axis_index("gx"), lax.axis_index("gy")
    barrier = pltpu.get_barrier_semaphore()
    for j in range(1, nx):
        pl.semaphore_signal(barrier, inc=1, device_id=(lax.rem(ix + j, nx), iy), device_id_type=MESH)
    for j in range(1, ny):
        pl.semaphore_signal(barrier, inc=1, device_id=(ix, lax.rem(iy + j, ny)), device_id_type=MESH)
    loads = [pltpu.make_async_copy(z, zv, own.at[3]), pltpu.make_async_copy(f, fv, own.at[4])]
    for c in loads:
        c.start()

    length = tfock.shape[2]
    row = lax.broadcasted_iota(I32, (per_cell, length), 0)

    def hits(key):
        return jnp.broadcast_to(key, row.shape) == row

    def named(keys):
        found = sum(hits(key).astype(I32) for key in keys)
        return jnp.minimum(jnp.max(found, axis=1, keepdims=True), 1)

    def inside(tasks, k):
        a = tasks[1]
        here = jnp.logical_and(a >= k * per_cell, a < (k + 1) * per_cell)
        return jnp.logical_and(here, tasks[0] < per_cell)

    z_named = {k: named((tfock[2] - k * per_cell, tfz[2] - k * per_cell)) for k in (3, 4)}
    p_named = {k: named((jnp.where(inside(ttrans, k), ttrans[0], per_cell),)) for k in range(1, 5)}
    z_most = functools.reduce(jnp.maximum, [jnp.sum(v) for v in z_named.values()])
    p_most = functools.reduce(jnp.maximum, [jnp.sum(v) for v in p_named.values()])
    left_half = lax.broadcasted_iota(I32, msg.shape, 1) < TILE // 2
    msg[...] = jnp.where(left_half, z_most, p_most)
    pl.semaphore_wait(barrier, nx + ny - 2)

    keep = pltpu.make_async_copy(msg, line.at[pl.ds(0, 1)], own.at[0])
    keep.start()
    first = []
    for j in range(1, nx):
        to = (lax.rem(ix + j, nx), iy)
        first.append(pltpu.make_async_remote_copy(msg, line.at[pl.ds(j, 1)], line_s.at[j], line_r.at[j], device_id=to, device_id_type=MESH))
        first[-1].start()
    others = []
    for axis, by in STEPS:
        others.append((lax.rem(ix + by + nx, nx), iy) if axis == "gx" else (ix, lax.rem(iy + by + ny, ny)))
    lists = [(ttrans, tn[k], others[k]) for k in range(4)]
    lists += [(tfock, fn[0], others[2]), (tfz, zl[0], others[2]), (tfock, fn[1], others[3]), (tfz, zl[1], others[3])]
    small = []
    for i, (src, dst, to) in enumerate(lists):
        small.append(pltpu.make_async_remote_copy(src, dst, list_s.at[i], list_r.at[i], device_id=to, device_id_type=MESH))
        small[-1].start()

    def bulk(i, k, src, dst, start, size):
        part = pl.ds(start, size)
        return pltpu.make_async_remote_copy(
            src.at[part], dst.at[part], bulk_s.at[i], bulk_r.at[i], device_id=others[k], device_id_type=MESH
        )

    large = [bulk(0, 2, g, gn[3], 0, lead), bulk(1, 3, g, gn[2], 0, lead)]
    large += [bulk(2, 0, g, gn[1], 0, per_cell), bulk(3, 1, g, gn[0], 0, per_cell)]
    large += [bulk(4, 0, z, zn[1], 0, per_cell), bulk(5, 1, z, zn[0], 0, per_cell)]
    for c in large:
        c.start()
    keep.wait()
    for c in first:
        c.wait()
    keep = pltpu.make_async_copy(line, lines.at[0], own.at[1])
    keep.start()
    second = []
    for j in range(1, ny):
        to = (ix, lax.rem(iy + j, ny))
        second.append(pltpu.make_async_remote_copy(line, lines.at[j], lines_s.at[j], lines_r.at[j], device_id=to, device_id_type=MESH))
        second[-1].start()
    rest = [bulk(6, 2, g, gn[3], lead, per_cell - lead), bulk(7, 3, g, gn[2], lead, per_cell - lead)]
    for c in rest:
        c.start()
    for c in small:
        c.wait()

    square = (per_cell, per_cell)
    below = (lax.broadcasted_iota(I32, square, 1) < lax.broadcasted_iota(I32, square, 0)).astype(F32)
    lane = lax.broadcasted_iota(I32, (1, TILE), 1)
    number = lax.broadcasted_iota(I32, (per_cell, TILE), 0)

    def ranked(found):
        return jnp.dot(below, jnp.broadcast_to(found, number.shape).astype(F32), preferred_element_type=F32)

    def packed_rows(found):
        here = jnp.logical_and(ranked(found) == jnp.broadcast_to(lane, number.shape).astype(F32), jnp.broadcast_to(found, number.shape) == 1)
        order = jnp.sum(jnp.where(here, number, 0), axis=0, keepdims=True)
        return jnp.where(lane == TILE - 1, jnp.sum(found), order)

    def rank_of(key, found):
        rank = ranked(found)[:, :length].astype(I32)
        return jnp.sum(jnp.where(hits(key), rank, 0), axis=0, keepdims=True)

    for side in range(2):
        base = (3 + side) * per_cell
        pick[side : side + 1, :] = packed_rows(named((fn[side][2] - base, zl[side][2] - base)))
    copy = pltpu.make_async_copy(pick, picked, own.at[2])
    copy.start()
    copy.wait()
    for c in loads:
        c.wait()
    puts = []
    for side in range(2):

        def take(s, _, side=side):
            packed[side, s] = zv[picked[side, s]]
            return 0

        lax.fori_loop(0, z_rooms[-1], take, 0)
        for i, room in enumerate(z_rooms):
            out = zp[2 * i + side]
            puts.append(pltpu.make_async_copy(packed.at[side, pl.ds(0, room)], out, put.at[2 * i + side]))
            puts[-1].start()

    def cut_all(i, _):
        tile = fv[i]
        cut[0, i] = split(tile)
        cut[1, i] = split(tile.T)
        cut[2, i] = split(zv[i])
        return 0

    lax.fori_loop(0, per_cell, cut_all, 0)
    for i, out in enumerate((fs, ft, zs)):
        puts.append(pltpu.make_async_copy(cut.at[i], out, put.at[packs + i]))
        puts[-1].start()

    plan[...] = jnp.zeros_like(plan)
    for at, tasks in ((FOCK_ROW, tfock), (FZ_ROW, tfz)):
        place = tasks[2]
        for k in (3, 4):
            key = tasks[2] - k * per_cell
            here = jnp.logical_and(key >= 0, key < per_cell)
            place = jnp.where(here, k * per_cell + rank_of(key, z_named[k]), place)
        plan[at : at + 1, pl.ds(0, length)] = place
    for k in range(1, 5):
        plan[MAP_ROW + k - 1 : MAP_ROW + k, :] = packed_rows(p_named[k])
    square = (length, length)
    before = (lax.broadcasted_iota(I32, square, 0) < lax.broadcasted_iota(I32, square, 1)).astype(F32)
    same = (lax.broadcasted_iota(I32, square, 0) == lax.broadcasted_iota(I32, square, 1)).astype(F32)
    slots = lax.broadcasted_iota(I32, (length, TILE), 1).astype(F32)
    table[...] = jnp.zeros_like(table)
    for k, tasks in enumerate((ttrans,) + tuple(tn)):
        here = inside(tasks, k)
        out = jnp.where(here, tasks[0], per_cell)
        slot = out if k == 0 else rank_of(out, named((out,)))
        for i, value in enumerate((slot, tasks[1] - k * per_cell, tasks[2] - k * per_cell, here)):
            table[i : i + 1, :] = value.astype(F32)
        earlier = jnp.dot(table[...], before, preferred_element_type=F32)
        table[4:5, :] = earlier[3:4, :]
        turned = lax.dot_general(same, table[...], (((1,), (1,)), ((), ())), preferred_element_type=F32)
        to_slot = jnp.logical_and(jnp.broadcast_to(turned[:, 4:5], slots.shape) == slots, jnp.broadcast_to(turned[:, 3:4], slots.shape) > 0.5)
        moved = jnp.dot(table[...], to_slot.astype(F32), preferred_element_type=F32).astype(I32)
        count = jnp.sum(here.astype(I32))
        at = LIST_ROW + 4 * k
        for i in range(3):
            plan[at + i : at + i + 1, :] = moved[i : i + 1, :]
        plan[at : at + 1, :] = jnp.where(lane < count, moved[0:1, :], TILE - 1)
        plan[at + 3 : at + 4, :] = jnp.where(lane == TILE - 1, count, 0)

    keep.wait()
    for c in second:
        c.wait()
    found = jnp.max(lines[...], axis=0)
    half = lax.broadcasted_iota(I32, found.shape, 1) < TILE // 2
    z_all = jnp.max(jnp.where(half, found, 0))
    p_all = jnp.max(jnp.where(half, 0, found))
    level[0, 0] = sum(
        jnp.logical_or(z_all > a, p_all > b).astype(I32) for a, b in zip(z_rooms, p_rooms)
    )
    for c in large + rest + puts:
        c.wait()


def w_kernel(tasks, zs, g0, g1, g2, g3, g4, ws, grown, cut, total, sems, osem):
    per_cell = zs.shape[0]
    copies = fetch((g0, g1, g2, g3, g4), grown, sems, per_cell)
    total[...] = jnp.zeros_like(total)
    live = live_count(tasks, per_cell)
    for c in copies:
        c.wait()
    run_list(live, plain_entry(tasks), lambda a: zs[a], lambda b: split(grown[b]), False, total)
    split_all(total, cut, per_cell)
    out = pltpu.make_async_copy(cut, ws, osem)
    out.start()
    out.wait()


def p_kernel(plan, ft, ws, p0, p1, p2, p3, p4, total, osem):
    per_cell, room = p0.shape[0], p1.shape[0]

    def start(k):
        return per_cell + (k - 1) * room if k else 0

    last = start(5)

    def zero(i, _):
        total[i] = jnp.zeros_like(total[i])
        return 0

    lax.fori_loop(0, last, zero, 0)

    def one(k, _):
        at = LIST_ROW + 4 * k
        first = jnp.where(k == 0, 0, per_cell + (k - 1) * room)

        def entry(e):
            return jnp.minimum(first + plan[at, e], last), plan[at + 1, e], plan[at + 2, e]

        run_list(plan[at + 3, TILE - 1], entry, lambda a: ft[a], lambda b: ws[b], False, total)
        return 0

    lax.fori_loop(0, 5, one, 0)
    outs = [
        pltpu.make_async_copy(total.at[pl.ds(start(k), p.shape[0])], p, osem.at[k])
        for k, p in enumerate((p0, p1, p2, p3, p4))
    ]
    for out in outs:
        out.start()
    for out in outs:
        out.wait()


def rest_kernel(tfock, tfz, tzgt, plan, fs, ws, p0, z0, z1, z2, z3, z4, g0, g1, g2, g3, g4, fock, factor, zgrown, ggrown, us, total, zsem, gsem, osem):
    per_cell = p0.shape[0]
    zcopies = fetch((z0, z1, z2, z3, z4), zgrown, zsem, per_cell)
    gcopies = fetch((g0, g1, g2, g3, g4), ggrown, gsem, per_cell)
    total[0] = jnp.zeros_like(total[0])
    total[1] = jnp.zeros_like(total[1])
    total[2, pl.ds(0, per_cell)] = p0[...]
    fz_live, fock_live, zgt_live = (live_count(tasks, per_cell) for tasks in (tfz, tfock, tzgt))
    for c in zcopies:
        c.wait()

    def moved_entry(tasks, at):
        return lambda e: (tasks[0, 0, e], tasks[1, 0, e], plan[at, e])

    run_list(fz_live, moved_entry(tfz, FZ_ROW), lambda a: fs[a], lambda b: split(zgrown[b]), False, total.at[0])
    split_all(total.at[0], us, per_cell)
    run_list(fock_live, moved_entry(tfock, FOCK_ROW), lambda a: ws[a], lambda b: split(zgrown[b]), True, total.at[1])
    out1 = pltpu.make_async_copy(total.at[1, pl.ds(0, per_cell)], fock, osem.at[0])
    out1.start()
    for c in gcopies:
        c.wait()
    run_list(zgt_live, plain_entry(tzgt), lambda a: us[a], lambda b: split(ggrown[b]), True, total.at[2])
    out2 = pltpu.make_async_copy(total.at[2, pl.ds(0, per_cell)], factor, osem.at[1])
    out2.start()
    out1.wait()
    out2.wait()


def join_kernel(plan, part, pa, pb, factor, total, got, sems, *, sides):
    per_cell, room = part.shape[0], pa.shape[0]
    load = pltpu.make_async_copy(part, total, sems.at[0])
    load.start()
    gets = [pltpu.make_async_copy(p, got.at[i], sems.at[2 + i]) for i, p in enumerate((pa, pb))]
    for c in gets:
        c.start()
    load.wait()
    for i, side in enumerate(sides):
        at = MAP_ROW + side
        gets[i].wait()

        def add(s, _, i=i, at=at):
            total[plan[at, s]] += got[i, s]
            return 0

        lax.fori_loop(0, jnp.minimum(plan[at, TILE - 1], room), add, 0)
    out = pltpu.make_async_copy(total, factor, sems.at[1])
    out.start()
    out.wait()


SMEM = pl.BlockSpec(memory_space=pltpu.SMEM)
VMEM = pl.BlockSpec(memory_space=pltpu.VMEM)
ANY = pl.BlockSpec(memory_space=pl.ANY)
HBM = pl.BlockSpec(memory_space=pltpu.HBM)
DMA = pltpu.SemaphoreType.DMA


def cost(tasks, tiles):
    return pl.CostEstimate(flops=tasks * 2 * TILE**3 * 8, bytes_accessed=tiles * TILE * TILE * 4, transcendentals=0)


def shifted(array, axis, by):
    n = lax.axis_size(axis)
    return lax.ppermute(array, axis, [(i, (i + by) % n) for i in range(n)])


def tiles(n):
    return jax.ShapeDtypeStruct((n, TILE, TILE), F32)


def cut_tiles(n):
    return jax.ShapeDtypeStruct((n, TILE, 2 * TILE), jnp.bfloat16)


def join(plan, part, pa, pb, sides):
    per_cell, room = part.shape[0], pa.shape[0]
    return pl.pallas_call(
        functools.partial(join_kernel, sides=sides),
        name="join_kernel",
        out_shape=tiles(per_cell),
        in_specs=[SMEM, ANY, ANY, ANY],
        out_specs=ANY,
        scratch_shapes=[pltpu.VMEM((per_cell, TILE, TILE), F32), pltpu.VMEM((2, room, TILE, TILE), F32), DMA((4,))],
        compiler_params=pltpu.CompilerParams(vmem_limit_bytes=62 * 2**20),
        cost_estimate=cost(0, 4 * per_cell),
    )(plan, part, pa, pb)


def finish(p_room, z3, z4, z, g, tzg, tfock, tfz, tzgt, plan, fs, ft, zs, gn, zx):
    per_cell = z.shape[0]
    cap = tzg.shape[2]
    grown = pltpu.VMEM((5 * per_cell, TILE, TILE), F32)
    cut = pltpu.VMEM((per_cell, TILE, 2 * TILE), jnp.bfloat16)
    params = pltpu.CompilerParams(vmem_limit_bytes=40 * 2**20)
    zn = list(zx) + [shifted(z3, "gy", 1), shifted(z4, "gy", -1)]
    ws = pl.pallas_call(
        w_kernel,
        name="w_kernel",
        out_shape=cut_tiles(per_cell),
        in_specs=[SMEM, VMEM] + [ANY] * 5,
        out_specs=ANY,
        scratch_shapes=[grown, cut, pltpu.VMEM((per_cell + 1, TILE, TILE), F32), DMA((5,)), DMA],
        compiler_params=params,
        cost_estimate=cost(cap, 7 * per_cell),
    )(tzg, zs, g, *gn)
    p = pl.pallas_call(
        p_kernel,
        name="p_kernel",
        out_shape=[tiles(per_cell)] + [tiles(p_room)] * 4,
        in_specs=[SMEM] + [VMEM] * 2,
        out_specs=[ANY] * 5,
        scratch_shapes=[pltpu.VMEM((per_cell + 4 * p_room + 1, TILE, TILE), F32), DMA((5,))],
        compiler_params=params,
        cost_estimate=cost(2 * cap, 7 * per_cell),
    )(plan, ft, ws)
    pn = [shifted(p[k + 1], axis, -by) for k, (axis, by) in enumerate(STEPS)]
    fock_grad, part = pl.pallas_call(
        rest_kernel,
        name="rest_kernel",
        out_shape=[tiles(per_cell)] * 2,
        in_specs=[SMEM] * 4 + [VMEM] * 3 + [ANY] * 10,
        out_specs=[ANY, ANY],
        scratch_shapes=[grown, grown, cut, pltpu.VMEM((3, per_cell + 1, TILE, TILE), F32), DMA((5,)), DMA((5,)), DMA((2,))],
        compiler_params=params,
        cost_estimate=cost(3 * cap, 14 * per_cell),
    )(tfock, tfz, tzgt, plan, fs, ws, p[0], z, *zn, g, *gn)
    part = join(plan, part, pn[0], pn[1], (0, 1))
    return fock_grad, join(plan, part, pn[2], pn[3], (2, 3))


def rooms(per_cell):
    return [(per_cell * a // 24, per_cell * b // 24) for a, b in ((19, 13), (20, 14), (22, 16))]


def body(z_factor, fock, cotangent, tasks_zg, tasks_fock, tasks_fz, tasks_zgt, tasks_trans):
    per_cell = z_factor.shape[2]
    nx, ny = lax.axis_size("gx"), lax.axis_size("gy")
    z, f, g = z_factor[0, 0], fock[0, 0], cotangent[0, 0]
    lists = (tasks_zg, tasks_fock, tasks_fz, tasks_zgt, tasks_trans)
    tzg, tfock, tfz, tzgt, ttrans = (t.reshape(t.shape[2], 1, t.shape[3]) for t in lists)
    a_list = jax.ShapeDtypeStruct(tzg.shape, I32)
    z_rooms, p_rooms = zip(*rooms(per_cell))
    z_rooms = z_rooms + (per_cell,)
    packs = 2 * len(z_rooms)
    shared = pl.pallas_call(
        functools.partial(share_kernel, z_rooms=z_rooms, p_rooms=p_rooms, lead=per_cell // 4),
        name="share_kernel",
        out_shape=[tiles(per_cell)] * 6
        + [a_list] * 8
        + [tiles(room) for room in z_rooms for _ in range(2)]
        + [jax.ShapeDtypeStruct((1, 1), I32), jax.ShapeDtypeStruct((PLAN_ROWS, TILE), I32)]
        + [cut_tiles(per_cell)] * 3,
        in_specs=[VMEM] * 3 + [ANY] * 3,
        out_specs=[ANY] * 6 + [VMEM] * 8 + [ANY] * packs + [SMEM, VMEM] + [ANY] * 3,
        scratch_shapes=[
            pltpu.VMEM((1, TILE), I32),
            pltpu.VMEM((nx, TILE), I32),
            pltpu.VMEM((ny, nx, TILE), I32),
            pltpu.VMEM((8, TILE), I32),
            pltpu.VMEM((2, per_cell, TILE, TILE), F32),
            pltpu.SMEM((8, TILE), I32),
            pltpu.VMEM((8, tzg.shape[2]), F32),
            pltpu.VMEM((per_cell, TILE, TILE), F32),
            pltpu.VMEM((per_cell, TILE, TILE), F32),
            pltpu.VMEM((3, per_cell, TILE, 2 * TILE), jnp.bfloat16),
            DMA((8,)),
            DMA((8,)),
            DMA((8,)),
            DMA((8,)),
            DMA((nx,)),
            DMA((nx,)),
            DMA((ny,)),
            DMA((ny,)),
            DMA((5,)),
            DMA((packs + 3,)),
        ],
        compiler_params=pltpu.CompilerParams(collective_id=0, has_side_effects=True),
    )(tfock, tfz, ttrans, f, z, g)
    gn, zx, zp = shared[:4], shared[4:6], shared[14 : 14 + packs]
    level, plan, fs, ft, zs = shared[14 + packs :]
    branches = [
        lambda zp, *rest, i=i, room=room: finish(room, zp[2 * i], zp[2 * i + 1], *rest)
        for i, room in enumerate(p_rooms + (per_cell,))
    ]
    operands = (zp, z, g, tzg, tfock, tfz, tzgt, plan, fs, ft, zs, gn, zx)
    fock_grad, factor_grad = lax.switch(level[0, 0], branches, *operands)
    return fock_grad[None, None], factor_grad[None, None]


def solution(mesh):
    cells = P("gx", "gy", None, None, None)
    lists = P("gx", "gy", None, None)
    return jax.shard_map(
        body,
        mesh=mesh,
        in_specs=(cells,) * 3 + (lists,) * 5,
        out_specs=(cells, cells),
        check_vma=False,
    )
```

```python
import functools

import jax
import jax.numpy as jnp
from jax import lax
from jax.experimental import pallas as pl
from jax.experimental.pallas import tpu as pltpu
from jax.sharding import PartitionSpec as P


TILE = 128
UNROLL = 8
F32 = jnp.float32
I32 = jnp.int32
MESH = pl.DeviceIdType.MESH
STEPS = (("gx", -1), ("gx", 1), ("gy", -1), ("gy", 1))


def split(tile):
    high = tile.astype(jnp.bfloat16)
    low = (tile - high.astype(F32)).astype(jnp.bfloat16)
    return jnp.concatenate([high, low], axis=1)


def product(left, right, turned):
    if turned:
        high, low = right[:, :TILE], right[:, TILE:]
        rows = jnp.concatenate([high, low], axis=0)
        operand = jnp.concatenate([rows, rows], axis=1)
        both = lax.dot_general(left, operand, (((1,), (1,)), ((), ())), preferred_element_type=F32)
    else:
        operand = jnp.concatenate([right, right], axis=0)
        both = lax.dot_general(left, operand, (((1,), (0,)), ((), ())), preferred_element_type=F32)
    return both[:, :TILE] + both[:, TILE:]


def run_list(count, entry, left_of, right_of, turned, total):
    def step(turn, _):
        entries = [entry(turn * UNROLL + i) for i in range(UNROLL)]
        values = [product(left_of(a), right_of(b), turned) for _, a, b in entries]
        for (t, _, _), value in zip(entries, values):
            total[t] += value
        return 0

    lax.fori_loop(0, (count + UNROLL - 1) // UNROLL, step, 0)


def live_count(tasks, per_cell):
    length = tasks.shape[2]
    return lax.while_loop(
        lambda n: jnp.logical_and(n < length, tasks[0, 0, jnp.minimum(n, length - 1)] < per_cell),
        lambda n: n + 1,
        jnp.int32(0),
    )


def split_all(source, target, per_cell):
    def step(i, _):
        target[i] = split(source[i])
        return 0

    lax.fori_loop(0, per_cell, step, 0)


def plain_entry(tasks):
    return lambda e: (tasks[0, 0, e], tasks[1, 0, e], tasks[2, 0, e])


def fetch(sources, grown, sems, per_cell):
    copies = [
        pltpu.make_async_copy(src, grown.at[pl.ds(k * per_cell, src.shape[0])], sems.at[k])
        for k, src in enumerate(sources)
    ]
    for c in copies:
        c.start()
    return copies


FOCK_ROW, FZ_ROW, MAP_ROW, LIST_ROW, PLAN_ROWS = 0, 1, 2, 8, 32


def by_part(lane, a, b, c):
    return jnp.where(lane < TILE // 4, a, jnp.where(lane < TILE // 2, b, c))


def share_kernel(tfock, tfz, ttrans, f, z, g, *refs, rooms, z_rooms, lead):
    packs = 2 * len(z_rooms)
    gn, zn, tn, fn, zl, zp = refs[:4], refs[4:6], refs[6:10], refs[10:12], refs[12:14], refs[14 : 14 + packs]
    (level, plan, fs, ft, zs, msg, line, lines, pick, packed, picked, table, fv, zv, cut, bulk_s, bulk_r, list_s, list_r) = refs[14 + packs : 33 + packs]
    line_s, line_r, lines_s, lines_r, own, put = refs[33 + packs :]
    nx, ny = line.shape[0], lines.shape[0]
    per_cell = g.shape[0]
    ix, iy = lax.axis_index("gx"), lax.axis_index("gy")
    barrier = pltpu.get_barrier_semaphore()
    for j in range(1, nx):
        pl.semaphore_signal(barrier, inc=1, device_id=(lax.rem(ix + j, nx), iy), device_id_type=MESH)
    for j in range(1, ny):
        pl.semaphore_signal(barrier, inc=1, device_id=(ix, lax.rem(iy + j, ny)), device_id_type=MESH)
    loads = [pltpu.make_async_copy(z, zv, own.at[3]), pltpu.make_async_copy(f, fv, own.at[4])]
    for c in loads:
        c.start()

    length = tfock.shape[2]
    row = lax.broadcasted_iota(I32, (per_cell, length), 0)

    def hits(key):
        return jnp.broadcast_to(key, row.shape) == row

    def named(keys):
        found = sum(hits(key).astype(I32) for key in keys)
        return jnp.minimum(jnp.max(found, axis=1, keepdims=True), 1)

    def inside(tasks, k):
        a = tasks[1]
        here = jnp.logical_and(a >= k * per_cell, a < (k + 1) * per_cell)
        return jnp.logical_and(here, tasks[0] < per_cell)

    z_named = {k: named((tfock[2] - k * per_cell, tfz[2] - k * per_cell)) for k in (3, 4)}
    p_named = {k: named((jnp.where(inside(ttrans, k), ttrans[0], per_cell),)) for k in range(1, 5)}
    z_most = functools.reduce(jnp.maximum, [jnp.sum(v) for v in z_named.values()])
    x_most, y_most = (jnp.maximum(jnp.sum(p_named[k]), jnp.sum(p_named[k + 1])) for k in (1, 3))
    msg[...] = by_part(lax.broadcasted_iota(I32, msg.shape, 1), z_most, x_most, y_most)
    pl.semaphore_wait(barrier, nx + ny - 2)

    keep = pltpu.make_async_copy(msg, line.at[pl.ds(0, 1)], own.at[0])
    keep.start()
    first = []
    for j in range(1, nx):
        to = (lax.rem(ix + j, nx), iy)
        first.append(pltpu.make_async_remote_copy(msg, line.at[pl.ds(j, 1)], line_s.at[j], line_r.at[j], device_id=to, device_id_type=MESH))
        first[-1].start()
    others = []
    for axis, by in STEPS:
        others.append((lax.rem(ix + by + nx, nx), iy) if axis == "gx" else (ix, lax.rem(iy + by + ny, ny)))
    lists = [(ttrans, tn[k], others[k]) for k in range(4)]
    lists += [(tfock, fn[0], others[2]), (tfz, zl[0], others[2]), (tfock, fn[1], others[3]), (tfz, zl[1], others[3])]
    small = []
    for i, (src, dst, to) in enumerate(lists):
        small.append(pltpu.make_async_remote_copy(src, dst, list_s.at[i], list_r.at[i], device_id=to, device_id_type=MESH))
        small[-1].start()

    def bulk(i, k, src, dst, start, size):
        part = pl.ds(start, size)
        return pltpu.make_async_remote_copy(
            src.at[part], dst.at[part], bulk_s.at[i], bulk_r.at[i], device_id=others[k], device_id_type=MESH
        )

    large = [bulk(0, 2, g, gn[3], 0, lead), bulk(1, 3, g, gn[2], 0, lead)]
    large += [bulk(2, 0, g, gn[1], 0, per_cell), bulk(3, 1, g, gn[0], 0, per_cell)]
    large += [bulk(4, 0, z, zn[1], 0, per_cell), bulk(5, 1, z, zn[0], 0, per_cell)]
    for c in large:
        c.start()
    keep.wait()
    for c in first:
        c.wait()
    keep = pltpu.make_async_copy(line, lines.at[0], own.at[1])
    keep.start()
    second = []
    for j in range(1, ny):
        to = (ix, lax.rem(iy + j, ny))
        second.append(pltpu.make_async_remote_copy(line, lines.at[j], lines_s.at[j], lines_r.at[j], device_id=to, device_id_type=MESH))
        second[-1].start()
    rest = [bulk(6, 2, g, gn[3], lead, per_cell - lead), bulk(7, 3, g, gn[2], lead, per_cell - lead)]
    for c in rest:
        c.start()
    for c in small:
        c.wait()

    square = (per_cell, per_cell)
    below = (lax.broadcasted_iota(I32, square, 1) < lax.broadcasted_iota(I32, square, 0)).astype(F32)
    lane = lax.broadcasted_iota(I32, (1, TILE), 1)
    number = lax.broadcasted_iota(I32, (per_cell, TILE), 0)

    def ranked(found):
        return jnp.dot(below, jnp.broadcast_to(found, number.shape).astype(F32), preferred_element_type=F32)

    def packed_rows(found):
        here = jnp.logical_and(ranked(found) == jnp.broadcast_to(lane, number.shape).astype(F32), jnp.broadcast_to(found, number.shape) == 1)
        order = jnp.sum(jnp.where(here, number, 0), axis=0, keepdims=True)
        return jnp.where(lane == TILE - 1, jnp.sum(found), order)

    def rank_of(key, found):
        rank = ranked(found)[:, :length].astype(I32)
        return jnp.sum(jnp.where(hits(key), rank, 0), axis=0, keepdims=True)

    for side in range(2):
        base = (3 + side) * per_cell
        pick[side : side + 1, :] = packed_rows(named((fn[side][2] - base, zl[side][2] - base)))
    copy = pltpu.make_async_copy(pick, picked, own.at[2])
    copy.start()
    copy.wait()
    for c in loads:
        c.wait()
    puts = []
    for side in range(2):

        def take(s, _, side=side):
            packed[side, s] = zv[picked[side, s]]
            return 0

        lax.fori_loop(0, per_cell, take, 0)
        for i, room in enumerate(z_rooms):
            out = zp[2 * i + side]
            puts.append(pltpu.make_async_copy(packed.at[side, pl.ds(0, room)], out, put.at[2 * i + side]))
            puts[-1].start()

    def cut_all(i, _):
        tile = fv[i]
        cut[0, i] = split(tile)
        cut[1, i] = split(tile.T)
        cut[2, i] = split(zv[i])
        return 0

    lax.fori_loop(0, per_cell, cut_all, 0)
    for i, out in enumerate((fs, ft, zs)):
        puts.append(pltpu.make_async_copy(cut.at[i], out, put.at[packs + i]))
        puts[-1].start()

    plan[...] = jnp.zeros_like(plan)
    for at, tasks in ((FOCK_ROW, tfock), (FZ_ROW, tfz)):
        place = tasks[2]
        for k in (3, 4):
            key = tasks[2] - k * per_cell
            here = jnp.logical_and(key >= 0, key < per_cell)
            place = jnp.where(here, k * per_cell + rank_of(key, z_named[k]), place)
        plan[at : at + 1, pl.ds(0, length)] = place
    for k in range(1, 5):
        plan[MAP_ROW + k - 1 : MAP_ROW + k, :] = packed_rows(p_named[k])
    square = (length, length)
    before = (lax.broadcasted_iota(I32, square, 0) < lax.broadcasted_iota(I32, square, 1)).astype(F32)
    same = (lax.broadcasted_iota(I32, square, 0) == lax.broadcasted_iota(I32, square, 1)).astype(F32)
    slots = lax.broadcasted_iota(I32, (length, TILE), 1).astype(F32)
    table[...] = jnp.zeros_like(table)
    for k, tasks in enumerate((ttrans,) + tuple(tn)):
        here = inside(tasks, k)
        out = jnp.where(here, tasks[0], per_cell)
        slot = out if k == 0 else rank_of(out, named((out,)))
        for i, value in enumerate((slot, tasks[1] - k * per_cell, tasks[2] - k * per_cell, here)):
            table[i : i + 1, :] = value.astype(F32)
        earlier = jnp.dot(table[...], before, preferred_element_type=F32)
        table[4:5, :] = earlier[3:4, :]
        turned = lax.dot_general(same, table[...], (((1,), (1,)), ((), ())), preferred_element_type=F32)
        to_slot = jnp.logical_and(jnp.broadcast_to(turned[:, 4:5], slots.shape) == slots, jnp.broadcast_to(turned[:, 3:4], slots.shape) > 0.5)
        moved = jnp.dot(table[...], to_slot.astype(F32), preferred_element_type=F32).astype(I32)
        count = jnp.sum(here.astype(I32))
        at = LIST_ROW + 4 * k
        for i in range(3):
            plan[at + i : at + i + 1, :] = moved[i : i + 1, :]
        plan[at : at + 1, :] = jnp.where(lane < count, moved[0:1, :], TILE - 1)
        plan[at + 3 : at + 4, :] = jnp.where(lane == TILE - 1, count, 0)

    keep.wait()
    for c in second:
        c.wait()
    found = jnp.max(lines[...], axis=0)
    part = lax.broadcasted_iota(I32, found.shape, 1)
    z_all, x_all, y_all = (jnp.max(jnp.where(by_part(part, *(int(j == i) for j in range(3))) == 1, found, 0)) for i in range(3))
    level[0, 0] = sum(
        jnp.logical_or(jnp.logical_or(z_all > a, x_all > b), y_all > c).astype(I32) for a, b, c in rooms[:-1]
    )
    for c in large + rest + puts:
        c.wait()


def w_kernel(tasks, zs, g0, g1, g2, g3, g4, ws, grown, cut, total, sems, osem):
    per_cell = zs.shape[0]
    copies = fetch((g0, g1, g2, g3, g4), grown, sems, per_cell)
    total[...] = jnp.zeros_like(total)
    live = live_count(tasks, per_cell)
    for c in copies:
        c.wait()
    run_list(live, plain_entry(tasks), lambda a: zs[a], lambda b: split(grown[b]), False, total)
    split_all(total, cut, per_cell)
    out = pltpu.make_async_copy(cut, ws, osem)
    out.start()
    out.wait()


def p_kernel(plan, ft, ws, p0, p1, p2, p3, p4, total, osem):
    outs = (p0, p1, p2, p3, p4)
    starts = [sum(p.shape[0] for p in outs[:k]) for k in range(6)]
    last = starts[5]

    def zero(i, _):
        total[i] = jnp.zeros_like(total[i])
        return 0

    lax.fori_loop(0, last, zero, 0)

    def one(k, _):
        at = LIST_ROW + 4 * k
        first = sum(jnp.where(k == i, start, 0) for i, start in enumerate(starts[:5]))

        def entry(e):
            return jnp.minimum(first + plan[at, e], last), plan[at + 1, e], plan[at + 2, e]

        run_list(plan[at + 3, TILE - 1], entry, lambda a: ft[a], lambda b: ws[b], False, total)
        return 0

    lax.fori_loop(0, 5, one, 0)
    copies = [pltpu.make_async_copy(total.at[pl.ds(starts[k], p.shape[0])], p, osem.at[k]) for k, p in enumerate(outs)]
    for c in copies:
        c.start()
    for c in copies:
        c.wait()


def add_packed(plan, side, packed, total):
    at = MAP_ROW + side

    def add(s, _):
        total[plan[at, s]] += packed[s]
        return 0

    lax.fori_loop(0, jnp.minimum(plan[at, TILE - 1], packed.shape[0]), add, 0)


def rest_kernel(tfock, tfz, tzgt, plan, fs, ws, p0, p1, p2, z0, z1, z2, z3, z4, g0, g1, g2, g3, g4, fock, factor, zgrown, ggrown, us, total, zsem, gsem, osem):
    per_cell = p0.shape[0]
    zcopies = fetch((z0, z1, z2, z3, z4), zgrown, zsem, per_cell)
    gcopies = fetch((g0, g1, g2, g3, g4), ggrown, gsem, per_cell)
    total[0] = jnp.zeros_like(total[0])
    total[1] = jnp.zeros_like(total[1])
    total[2, pl.ds(0, per_cell)] = p0[...]
    add_packed(plan, 0, p1, total.at[2])
    add_packed(plan, 1, p2, total.at[2])
    fz_live, fock_live, zgt_live = (live_count(tasks, per_cell) for tasks in (tfz, tfock, tzgt))
    for c in zcopies:
        c.wait()

    def moved_entry(tasks, at):
        return lambda e: (tasks[0, 0, e], tasks[1, 0, e], plan[at, e])

    run_list(fz_live, moved_entry(tfz, FZ_ROW), lambda a: fs[a], lambda b: split(zgrown[b]), False, total.at[0])
    split_all(total.at[0], us, per_cell)
    run_list(fock_live, moved_entry(tfock, FOCK_ROW), lambda a: ws[a], lambda b: split(zgrown[b]), True, total.at[1])
    out1 = pltpu.make_async_copy(total.at[1, pl.ds(0, per_cell)], fock, osem.at[0])
    out1.start()
    for c in gcopies:
        c.wait()
    run_list(zgt_live, plain_entry(tzgt), lambda a: us[a], lambda b: split(ggrown[b]), True, total.at[2])
    out2 = pltpu.make_async_copy(total.at[2, pl.ds(0, per_cell)], factor, osem.at[1])
    out2.start()
    out1.wait()
    out2.wait()


def join_kernel(plan, part, pa, pb, factor, total, got_a, got_b, loads, gets, puts, *, sides, pieces):
    per_cell = part.shape[0]
    size = per_cell // pieces
    lists = tuple(zip(sides, (pa, pb), (got_a, got_b)))
    fetches = [pltpu.make_async_copy(p, got, gets.at[i]) for i, (_, p, got) in enumerate(lists)]
    loaded, stored = [], []
    for i in range(pieces):
        piece = pl.ds(i * size, size)
        loaded.append(pltpu.make_async_copy(part.at[piece], total.at[piece], loads.at[i]))
        stored.append(pltpu.make_async_copy(total.at[piece], factor.at[piece], puts.at[i]))
    for c in loaded + fetches:
        c.start()
    counts = [jnp.minimum(plan[MAP_ROW + side, TILE - 1], got.shape[0]) for side, _, got in lists]
    at = [jnp.int32(0), jnp.int32(0)]
    for c in loaded[:1] + fetches:
        c.wait()
    for i in range(pieces):
        if i:
            loaded[i].wait()
        for j, (side, _, got) in enumerate(lists):

            def more(s, j=j, side=side, i=i):
                return jnp.logical_and(s < counts[j], plan[MAP_ROW + side, s] < (i + 1) * size)

            def add(s, side=side, got=got):
                total[plan[MAP_ROW + side, s]] += got[s]
                return s + 1

            at[j] = lax.while_loop(more, add, at[j])
        stored[i].start()
    for c in stored:
        c.wait()


SMEM = pl.BlockSpec(memory_space=pltpu.SMEM)
VMEM = pl.BlockSpec(memory_space=pltpu.VMEM)
ANY = pl.BlockSpec(memory_space=pl.ANY)
HBM = pl.BlockSpec(memory_space=pltpu.HBM)
DMA = pltpu.SemaphoreType.DMA


def cost(tasks, tiles):
    return pl.CostEstimate(flops=tasks * 2 * TILE**3 * 8, bytes_accessed=tiles * TILE * TILE * 4, transcendentals=0)


def shifted(array, axis, by):
    n = lax.axis_size(axis)
    return lax.ppermute(array, axis, [(i, (i + by) % n) for i in range(n)])


def tiles(n):
    return jax.ShapeDtypeStruct((n, TILE, TILE), F32)


def cut_tiles(n):
    return jax.ShapeDtypeStruct((n, TILE, 2 * TILE), jnp.bfloat16)


def join(plan, part, pa, pb, sides):
    per_cell, room = part.shape[0], pa.shape[0]
    pieces = 4 if per_cell % 4 == 0 else 1
    return pl.pallas_call(
        functools.partial(join_kernel, sides=sides, pieces=pieces),
        name="join_kernel",
        out_shape=pltpu.HBM((per_cell, TILE, TILE), F32),
        in_specs=[SMEM, ANY, ANY, ANY],
        out_specs=HBM,
        scratch_shapes=[pltpu.VMEM((n, TILE, TILE), F32) for n in (per_cell, room, room)] + [DMA((pieces,)), DMA((2,)), DMA((pieces,))],
        compiler_params=pltpu.CompilerParams(vmem_limit_bytes=16 * 2**20),
        cost_estimate=cost(0, 4 * per_cell),
    )(plan, part, pa, pb)


def finish(x_room, y_room, z3, z4, z, g, tzg, tfock, tfz, tzgt, plan, fs, ft, zs, gn, zx):
    per_cell = z.shape[0]
    cap = tzg.shape[2]
    grown = pltpu.VMEM((5 * per_cell, TILE, TILE), F32)
    cut = pltpu.VMEM((per_cell, TILE, 2 * TILE), jnp.bfloat16)
    params = pltpu.CompilerParams(vmem_limit_bytes=40 * 2**20)
    zn = list(zx) + [shifted(z3, "gy", 1), shifted(z4, "gy", -1)]
    ws = pl.pallas_call(
        w_kernel,
        name="w_kernel",
        out_shape=cut_tiles(per_cell),
        in_specs=[SMEM, VMEM] + [ANY] * 5,
        out_specs=ANY,
        scratch_shapes=[grown, cut, pltpu.VMEM((per_cell + 1, TILE, TILE), F32), DMA((5,)), DMA],
        compiler_params=params,
        cost_estimate=cost(cap, 7 * per_cell),
    )(tzg, zs, g, *gn)
    p = pl.pallas_call(
        p_kernel,
        name="p_kernel",
        out_shape=[tiles(n) for n in (per_cell, x_room, x_room, y_room, y_room)],
        in_specs=[SMEM] + [VMEM] * 2,
        out_specs=[ANY] * 5,
        scratch_shapes=[pltpu.VMEM((per_cell + 2 * x_room + 2 * y_room + 1, TILE, TILE), F32), DMA((5,))],
        compiler_params=params,
        cost_estimate=cost(2 * cap, 7 * per_cell),
    )(plan, ft, ws)
    pn = [shifted(p[k + 1], axis, -by) for k, (axis, by) in enumerate(STEPS)]
    fock_grad, part = pl.pallas_call(
        rest_kernel,
        name="rest_kernel",
        out_shape=[pltpu.HBM((per_cell, TILE, TILE), F32), tiles(per_cell)],
        in_specs=[SMEM] * 4 + [VMEM] * 5 + [ANY] * 10,
        out_specs=[HBM, ANY],
        scratch_shapes=[grown, grown, cut, pltpu.VMEM((3, per_cell + 1, TILE, TILE), F32), DMA((5,)), DMA((5,)), DMA((2,))],
        compiler_params=params,
        cost_estimate=cost(3 * cap, 14 * per_cell),
    )(tfock, tfz, tzgt, plan, fs, ws, p[0], pn[0], pn[1], z, *zn, g, *gn)
    return fock_grad, join(plan, part, pn[2], pn[3], (2, 3))


def rooms_of(per_cell):
    levels = ((18, 14, 12), (19, 14, 13), (20, 16, 13), (20, 16, 14), (22, 18, 16))
    return [tuple(per_cell * room // 24 for room in level) for level in levels] + [(per_cell,) * 3]


def body(z_factor, fock, cotangent, tasks_zg, tasks_fock, tasks_fz, tasks_zgt, tasks_trans):
    per_cell = z_factor.shape[2]
    nx, ny = lax.axis_size("gx"), lax.axis_size("gy")
    z, f, g = z_factor[0, 0], fock[0, 0], cotangent[0, 0]
    lists = (tasks_zg, tasks_fock, tasks_fz, tasks_zgt, tasks_trans)
    tzg, tfock, tfz, tzgt, ttrans = (t.reshape(t.shape[2], 1, t.shape[3]) for t in lists)
    a_list = jax.ShapeDtypeStruct(tzg.shape, I32)
    rooms = rooms_of(per_cell)
    z_rooms = sorted({room[0] for room in rooms})
    packs = 2 * len(z_rooms)
    shared = pl.pallas_call(
        functools.partial(share_kernel, rooms=rooms, z_rooms=z_rooms, lead=per_cell // 4),
        name="share_kernel",
        out_shape=[tiles(per_cell)] * 6
        + [a_list] * 8
        + [tiles(room) for room in z_rooms for _ in range(2)]
        + [jax.ShapeDtypeStruct((1, 1), I32), jax.ShapeDtypeStruct((PLAN_ROWS, TILE), I32)]
        + [cut_tiles(per_cell)] * 3,
        in_specs=[VMEM] * 3 + [ANY] * 3,
        out_specs=[ANY] * 6 + [VMEM] * 8 + [ANY] * packs + [SMEM, VMEM] + [ANY] * 3,
        scratch_shapes=[
            pltpu.VMEM((1, TILE), I32),
            pltpu.VMEM((nx, TILE), I32),
            pltpu.VMEM((ny, nx, TILE), I32),
            pltpu.VMEM((8, TILE), I32),
            pltpu.VMEM((2, per_cell, TILE, TILE), F32),
            pltpu.SMEM((8, TILE), I32),
            pltpu.VMEM((8, tzg.shape[2]), F32),
            pltpu.VMEM((per_cell, TILE, TILE), F32),
            pltpu.VMEM((per_cell, TILE, TILE), F32),
            pltpu.VMEM((3, per_cell, TILE, 2 * TILE), jnp.bfloat16),
            DMA((8,)),
            DMA((8,)),
            DMA((8,)),
            DMA((8,)),
            DMA((nx,)),
            DMA((nx,)),
            DMA((ny,)),
            DMA((ny,)),
            DMA((5,)),
            DMA((packs + 3,)),
        ],
        compiler_params=pltpu.CompilerParams(collective_id=0, has_side_effects=True),
    )(tfock, tfz, ttrans, f, z, g)
    gn, zx, zp = shared[:4], shared[4:6], shared[14 : 14 + packs]
    level, plan, fs, ft, zs = shared[14 + packs :]

    def branch(z_room, x_room, y_room):
        at = 2 * z_rooms.index(z_room)
        return lambda zp, *rest: finish(x_room, y_room, zp[at], zp[at + 1], *rest)

    operands = (zp, z, g, tzg, tfock, tfz, tzgt, plan, fs, ft, zs, gn, zx)
    fock_grad, factor_grad = lax.switch(level[0, 0], [branch(*room) for room in rooms], *operands)
    return fock_grad[None, None], factor_grad[None, None]


def solution(mesh):
    cells = P("gx", "gy", None, None, None)
    lists = P("gx", "gy", None, None)
    return jax.shard_map(
        body,
        mesh=mesh,
        in_specs=(cells,) * 3 + (lists,) * 5,
        out_specs=(cells, cells),
        check_vma=False,
    )
```

```python
import functools

import jax
import jax.numpy as jnp
from jax import lax
from jax.experimental import pallas as pl
from jax.experimental.pallas import tpu as pltpu
from jax.sharding import PartitionSpec as P


TILE = 128
UNROLL = 8
F32 = jnp.float32
I32 = jnp.int32
MESH = pl.DeviceIdType.MESH
STEPS = (("gx", -1), ("gx", 1), ("gy", -1), ("gy", 1))


def split(tile):
    high = tile.astype(jnp.bfloat16)
    low = (tile - high.astype(F32)).astype(jnp.bfloat16)
    return jnp.concatenate([high, low], axis=1)


def product(left, right, turned):
    if turned:
        high, low = right[:, :TILE], right[:, TILE:]
        rows = jnp.concatenate([high, low], axis=0)
        operand = jnp.concatenate([rows, rows], axis=1)
        both = lax.dot_general(left, operand, (((1,), (1,)), ((), ())), preferred_element_type=F32)
    else:
        operand = jnp.concatenate([right, right], axis=0)
        both = lax.dot_general(left, operand, (((1,), (0,)), ((), ())), preferred_element_type=F32)
    return both[:, :TILE] + both[:, TILE:]


def run_list(count, entry, left_of, right_of, turned, total, unroll=UNROLL):
    def step(turn, _):
        entries = [entry(turn * unroll + i) for i in range(unroll)]
        values = [product(left_of(a), right_of(b), turned) for _, a, b in entries]
        for (t, _, _), value in zip(entries, values):
            total[t] += value
        return 0

    lax.fori_loop(0, (count + unroll - 1) // unroll, step, 0)


def live_count(tasks, per_cell):
    length = tasks.shape[2]
    return lax.while_loop(
        lambda n: jnp.logical_and(n < length, tasks[0, 0, jnp.minimum(n, length - 1)] < per_cell),
        lambda n: n + 1,
        jnp.int32(0),
    )


def split_all(source, target, per_cell):
    def step(i, _):
        target[i] = split(source[i])
        return 0

    lax.fori_loop(0, per_cell, step, 0)


def plain_entry(tasks):
    return lambda e: (tasks[0, 0, e], tasks[1, 0, e], tasks[2, 0, e])


def moved_entry(tasks, plan, at):
    return lambda e: (tasks[0, 0, e], tasks[1, 0, e], plan[at, e])


def fetch(sources, grown, sems):
    copies = [
        pltpu.make_async_copy(src, grown.at[pl.ds(at, src.shape[0])], sems.at[i]) for i, (src, at) in enumerate(sources)
    ]
    for c in copies:
        c.start()
    return copies


FOCK_ROW, FZ_ROW, MAP_ROW, ZG_ROW, ZGT_ROW, LIST_ROW, PLAN_ROWS = 0, 1, 2, 6, 7, 8, 32


class Tables:
    def __init__(self, per_cell, length):
        self.per_cell, self.length = per_cell, length
        self.row = lax.broadcasted_iota(I32, (per_cell, length), 0)
        self.lane = lax.broadcasted_iota(I32, (1, TILE), 1)
        self.number = lax.broadcasted_iota(I32, (per_cell, TILE), 0)

    def hits(self, key):
        return jnp.broadcast_to(key, self.row.shape) == self.row

    def named(self, keys, first=0):
        found = sum(self.hits(key).astype(I32) for key in keys)
        found = jnp.where(self.row >= first, found, 0)
        return jnp.minimum(jnp.max(found, axis=1, keepdims=True), 1)

    def of_cell(self, lists, k, first=0):
        return self.named([tasks[2] - k * self.per_cell for tasks in lists], first)

    def inside(self, tasks, k):
        a = tasks[1]
        here = jnp.logical_and(a >= k * self.per_cell, a < (k + 1) * self.per_cell)
        return jnp.logical_and(here, tasks[0] < self.per_cell)

    def outs(self, tasks, k):
        return jnp.where(self.inside(tasks, k), tasks[0], self.per_cell)

    def ranked(self, found):
        square = (self.per_cell, self.per_cell)
        below = (lax.broadcasted_iota(I32, square, 1) < lax.broadcasted_iota(I32, square, 0)).astype(F32)
        return jnp.dot(below, jnp.broadcast_to(found, self.number.shape).astype(F32), preferred_element_type=F32)

    def packed_rows(self, found):
        spread = jnp.broadcast_to(self.lane, self.number.shape).astype(F32)
        here = jnp.logical_and(self.ranked(found) == spread, jnp.broadcast_to(found, self.number.shape) == 1)
        order = jnp.sum(jnp.where(here, self.number, 0), axis=0, keepdims=True)
        return jnp.where(self.lane == TILE - 1, jnp.sum(found), order)

    def rank_of(self, key, found):
        rank = self.ranked(found)[:, : self.length].astype(I32)
        return jnp.sum(jnp.where(self.hits(key), rank, 0), axis=0, keepdims=True)

    def places(self, tasks, lists, first=0):
        place = tasks[2]
        for k in (3, 4):
            key = tasks[2] - k * self.per_cell
            here = jnp.logical_and(key >= first, key < self.per_cell)
            rank = self.rank_of(key, self.of_cell(lists, k, first))
            place = jnp.where(here, k * self.per_cell + first + rank, place)
        return place


def by_quarter(lane, values):
    result = values[3]
    for i in (2, 1, 0):
        result = jnp.where(lane < (i + 1) * (TILE // 4), values[i], result)
    return result


def meet_kernel(tzg, tfock, tfz, tzgt, ttrans, g, *refs, rooms, g_rooms, lead, cuts):
    packs = 2 * len(g_rooms)
    ga, tn, fn, zl, gp = refs[:2], refs[2:6], refs[6:8], refs[8:10], refs[10 : 10 + packs]
    (level, gl, gt, msg, line, lines, pick, picked, gv, packed, bulk_s, bulk_r, list_s, list_r) = refs[10 + packs : 24 + packs]
    line_s, line_r, lines_s, lines_r, own, put = refs[24 + packs :]
    nx, ny = line.shape[0], lines.shape[0]
    per_cell = g.shape[0]
    ix, iy = lax.axis_index("gx"), lax.axis_index("gy")
    barrier = pltpu.get_barrier_semaphore()
    for j in range(1, nx):
        pl.semaphore_signal(barrier, inc=1, device_id=(lax.rem(ix + j, nx), iy), device_id_type=MESH)
    for j in range(1, ny):
        pl.semaphore_signal(barrier, inc=1, device_id=(ix, lax.rem(iy + j, ny)), device_id_type=MESH)
    load = pltpu.make_async_copy(g.at[pl.ds(lead, per_cell - lead)], gv, own.at[3])
    load.start()
    others = []
    for axis, by in STEPS:
        others.append((lax.rem(ix + by + nx, nx), iy) if axis == "gx" else (ix, lax.rem(iy + by + ny, ny)))
    pl.semaphore_wait(barrier, nx + ny - 2)

    lists = []
    for i in range(2):
        lists += [(tzg, gl.at[i], others[2 + i]), (tzgt, gt.at[i], others[2 + i])]
        lists += [(tfock, fn[i], others[2 + i]), (tfz, zl[i], others[2 + i])]
    lists += [(ttrans, tn[k], others[k]) for k in range(4)]
    small = []
    for i, (src, dst, to) in enumerate(lists):
        small.append(pltpu.make_async_remote_copy(src, dst, list_s.at[i], list_r.at[i], device_id=to, device_id_type=MESH))
        small[-1].start()

    def bulk(i, k, start, size):
        part = pl.ds(start, size)
        return pltpu.make_async_remote_copy(
            g.at[part], ga[(k ^ 1) - 2].at[part], bulk_s.at[i], bulk_r.at[i], device_id=others[k], device_id_type=MESH
        )

    large = [bulk(0, 2, 0, cuts), bulk(1, 3, 0, cuts)]
    for c in large:
        c.start()

    tables = Tables(per_cell, tfock.shape[2])

    def most(found):
        return functools.reduce(jnp.maximum, [jnp.sum(v) for v in found])

    needs = (
        most([tables.of_cell((tzg, tzgt), k, lead) for k in (3, 4)]),
        most([tables.of_cell((tfock, tfz), k) for k in (3, 4)]),
        most([tables.named((tables.outs(ttrans, k),)) for k in (1, 2)]),
        most([tables.named((tables.outs(ttrans, k),)) for k in (3, 4)]),
    )
    msg[...] = by_quarter(tables.lane, needs)
    keep = pltpu.make_async_copy(msg, line.at[pl.ds(0, 1)], own.at[0])
    keep.start()
    keep.wait()
    first = []
    for j in range(1, nx):
        to = (lax.rem(ix + j, nx), iy)
        row = line.at[pl.ds(0, 1)]
        first.append(pltpu.make_async_remote_copy(row, line.at[pl.ds(j, 1)], line_s.at[j], line_r.at[j], device_id=to, device_id_type=MESH))
        first[-1].start()
    for c in first:
        c.wait()
    keep = pltpu.make_async_copy(line, lines.at[0], own.at[1])
    keep.start()
    second = []
    for j in range(1, ny):
        to = (ix, lax.rem(iy + j, ny))
        second.append(pltpu.make_async_remote_copy(line, lines.at[j], lines_s.at[j], lines_r.at[j], device_id=to, device_id_type=MESH))
        second[-1].start()
    rest = [bulk(2, 2, cuts, lead - cuts), bulk(3, 3, cuts, lead - cuts)]
    for c in rest:
        c.start()
    for c in small:
        c.wait()

    for side in range(2):
        order = tables.packed_rows(tables.of_cell((gl.at[side], gt.at[side]), 3 + side, lead))
        pick[side : side + 1, :] = jnp.maximum(order - lead, 0)
    copy = pltpu.make_async_copy(pick, picked, own.at[2])
    copy.start()
    copy.wait()
    load.wait()
    puts = []
    for side in range(2):

        def take(s, _, side=side):
            packed[side, s] = gv[picked[side, s]]
            return 0

        lax.fori_loop(0, per_cell - lead, take, 0)
        for i, room in enumerate(g_rooms):
            puts.append(pltpu.make_async_copy(packed.at[side, pl.ds(0, room)], gp[2 * i + side], put.at[2 * i + side]))
            puts[-1].start()
    keep.wait()
    for c in second:
        c.wait()
    found = jnp.max(lines[...], axis=0)
    lane = lax.broadcasted_iota(I32, found.shape, 1)
    needs = [jnp.max(jnp.where(by_quarter(lane, [int(i == j) for j in range(4)]) == 1, found, 0)) for i in range(4)]
    short = []
    for level_rooms in rooms[:-1]:
        over = [need > room for need, room in zip(needs, level_rooms)]
        short.append(functools.reduce(jnp.logical_or, over).astype(I32))
    level[0, 0] = sum(short)
    for c in large + rest + puts:
        c.wait()


def pack_kernel(f3, z3, f4, z4, z, out3, out4, pick, packed, picked, own, put):
    per_cell, room = z.shape[0], out3.shape[0]
    tables = Tables(per_cell, f3.shape[2])
    for side, lists in enumerate(((f3, z3), (f4, z4))):
        pick[side : side + 1, :] = tables.packed_rows(tables.of_cell(lists, 3 + side))
    copy = pltpu.make_async_copy(pick, picked, own)
    copy.start()
    copy.wait()
    puts = []
    for side, out in enumerate((out3, out4)):

        def take(s, _, side=side):
            packed[side, s] = z[picked[side, s]]
            return 0

        lax.fori_loop(0, room, take, 0)
        puts.append(pltpu.make_async_copy(packed.at[side], out, put.at[side]))
        puts[-1].start()
    for c in puts:
        c.wait()


def plan_kernel(tzg, tfock, tfz, tzgt, t0, t1, t2, t3, t4, f, z, plan, fs, ft, zs, table, cut, put, *, lead):
    per_cell, length = f.shape[0], tfock.shape[2]

    def cut_all(i, _):
        tile = f[i]
        cut[0, i] = split(tile)
        cut[1, i] = split(tile.T)
        cut[2, i] = split(z[i])
        return 0

    lax.fori_loop(0, per_cell, cut_all, 0)
    puts = [pltpu.make_async_copy(cut.at[i], out, put.at[i]) for i, out in enumerate((fs, ft, zs))]
    for c in puts:
        c.start()
    tables = Tables(per_cell, length)
    lane = tables.lane
    plan[...] = jnp.zeros_like(plan)
    for at, tasks, lists, first in (
        (FOCK_ROW, tfock, (tfock, tfz), 0),
        (FZ_ROW, tfz, (tfock, tfz), 0),
        (ZG_ROW, tzg, (tzg, tzgt), lead),
        (ZGT_ROW, tzgt, (tzg, tzgt), lead),
    ):
        plan[at : at + 1, pl.ds(0, length)] = tables.places(tasks, lists, first)
    for k in range(1, 5):
        plan[MAP_ROW + k - 1 : MAP_ROW + k, :] = tables.packed_rows(tables.named((tables.outs(t0, k),)))
    square = (length, length)
    before = (lax.broadcasted_iota(I32, square, 0) < lax.broadcasted_iota(I32, square, 1)).astype(F32)
    same = (lax.broadcasted_iota(I32, square, 0) == lax.broadcasted_iota(I32, square, 1)).astype(F32)
    slots = lax.broadcasted_iota(I32, (length, TILE), 1).astype(F32)
    table[...] = jnp.zeros_like(table)
    for k, tasks in enumerate((t0, t1, t2, t3, t4)):
        here, out = tables.inside(tasks, k), tables.outs(tasks, k)
        slot = out if k == 0 else tables.rank_of(out, tables.named((out,)))
        for i, value in enumerate((slot, tasks[1] - k * per_cell, tasks[2] - k * per_cell, here)):
            table[i : i + 1, :] = value.astype(F32)
        earlier = jnp.dot(table[...], before, preferred_element_type=F32)
        table[4:5, :] = earlier[3:4, :]
        turned = lax.dot_general(same, table[...], (((1,), (1,)), ((), ())), preferred_element_type=F32)
        to_slot = jnp.logical_and(jnp.broadcast_to(turned[:, 4:5], slots.shape) == slots, jnp.broadcast_to(turned[:, 3:4], slots.shape) > 0.5)
        moved = jnp.dot(table[...], to_slot.astype(F32), preferred_element_type=F32).astype(I32)
        count = jnp.sum(here.astype(I32))
        at = LIST_ROW + 4 * k
        for i in range(3):
            plan[at + i : at + i + 1, :] = moved[i : i + 1, :]
        plan[at : at + 1, :] = jnp.where(lane < count, moved[0:1, :], TILE - 1)
        plan[at + 3 : at + 4, :] = jnp.where(lane == TILE - 1, count, 0)
    for c in puts:
        c.wait()


def w_kernel(tasks, plan, zs, g0, g1, g2, a3, g3, a4, g4, ws, grown, cut, total, sems, osem):
    per_cell, lead = zs.shape[0], a3.shape[0]
    copies = fetch(g_places(per_cell, lead, g0, g1, g2, a3, g3, a4, g4), grown, sems)
    total[...] = jnp.zeros_like(total)
    live = live_count(tasks, per_cell)
    for c in copies:
        c.wait()
    entry = moved_entry(tasks, plan, ZG_ROW)
    run_list(live, entry, lambda a: zs[a], lambda b: split(grown[b]), False, total, 4)
    split_all(total, cut, per_cell)
    out = pltpu.make_async_copy(cut, ws, osem)
    out.start()
    out.wait()


def g_places(per_cell, lead, g0, g1, g2, a3, g3, a4, g4):
    places = [(src, k * per_cell) for k, src in enumerate((g0, g1, g2, a3, a4))]
    return places + [(g3, 3 * per_cell + lead), (g4, 4 * per_cell + lead)]


def p_kernel(plan, ft, ws, p0, p1, p2, p3, p4, total, osem):
    outs = (p0, p1, p2, p3, p4)
    starts = [sum(p.shape[0] for p in outs[:k]) for k in range(6)]
    last = starts[5]

    def zero(i, _):
        total[i] = jnp.zeros_like(total[i])
        return 0

    lax.fori_loop(0, last, zero, 0)

    def one(k, _):
        at = LIST_ROW + 4 * k
        first = sum(jnp.where(k == i, start, 0) for i, start in enumerate(starts[:5]))

        def entry(e):
            return jnp.minimum(first + plan[at, e], last), plan[at + 1, e], plan[at + 2, e]

        run_list(plan[at + 3, TILE - 1], entry, lambda a: ft[a], lambda b: ws[b], False, total, 4)
        return 0

    lax.fori_loop(0, 5, one, 0)
    copies = [pltpu.make_async_copy(total.at[pl.ds(starts[k], p.shape[0])], p, osem.at[k]) for k, p in enumerate(outs)]
    for c in copies:
        c.start()
    for c in copies:
        c.wait()


def add_packed(plan, side, packed, total):
    at = MAP_ROW + side

    def add(s, _):
        total[plan[at, s]] += packed[s]
        return 0

    lax.fori_loop(0, jnp.minimum(plan[at, TILE - 1], packed.shape[0]), add, 0)


def rest_kernel(tfock, tfz, tzgt, plan, fs, ws, p0, p1, p2, z0, z1, z2, z3, z4, g0, g1, g2, a3, g3, a4, g4, fock, factor, zgrown, ggrown, us, total, zsem, gsem, osem):
    per_cell, lead = p0.shape[0], a3.shape[0]
    zcopies = fetch([(src, k * per_cell) for k, src in enumerate((z0, z1, z2, z3, z4))], zgrown, zsem)
    gcopies = fetch(g_places(per_cell, lead, g0, g1, g2, a3, g3, a4, g4), ggrown, gsem)
    total[0] = jnp.zeros_like(total[0])
    total[1] = jnp.zeros_like(total[1])
    total[2, pl.ds(0, per_cell)] = p0[...]
    add_packed(plan, 0, p1, total.at[2])
    add_packed(plan, 1, p2, total.at[2])
    fz_live, fock_live, zgt_live = (live_count(tasks, per_cell) for tasks in (tfz, tfock, tzgt))
    for c in zcopies:
        c.wait()
    run_list(fz_live, moved_entry(tfz, plan, FZ_ROW), lambda a: fs[a], lambda b: split(zgrown[b]), False, total.at[0])
    split_all(total.at[0], us, per_cell)
    run_list(fock_live, moved_entry(tfock, plan, FOCK_ROW), lambda a: ws[a], lambda b: split(zgrown[b]), True, total.at[1])
    out1 = pltpu.make_async_copy(total.at[1, pl.ds(0, per_cell)], fock, osem.at[0])
    out1.start()
    for c in gcopies:
        c.wait()
    run_list(zgt_live, moved_entry(tzgt, plan, ZGT_ROW), lambda a: us[a], lambda b: split(ggrown[b]), True, total.at[2])
    out2 = pltpu.make_async_copy(total.at[2, pl.ds(0, per_cell)], factor, osem.at[1])
    out2.start()
    out1.wait()
    out2.wait()


def join_kernel(plan, part, pa, pb, factor, total, puts, *, sides, pieces):
    per_cell = part.shape[0]
    size = per_cell // pieces
    lists = tuple(zip(sides, (pa, pb)))
    counts = [jnp.minimum(plan[MAP_ROW + side, TILE - 1], p.shape[0]) for side, p in lists]
    at = [jnp.int32(0), jnp.int32(0)]
    stored = []
    for i in range(pieces):
        piece = pl.ds(i * size, size)
        total[piece] = part[piece]
        for j, (side, p) in enumerate(lists):

            def more(s, j=j, side=side, i=i):
                return jnp.logical_and(s < counts[j], plan[MAP_ROW + side, s] < (i + 1) * size)

            def add(s, side=side, p=p):
                total[plan[MAP_ROW + side, s]] += p[s]
                return s + 1

            at[j] = lax.while_loop(more, add, at[j])
        stored.append(pltpu.make_async_copy(total.at[piece], factor.at[piece], puts.at[i]))
        stored[-1].start()
    for c in stored:
        c.wait()


SMEM = pl.BlockSpec(memory_space=pltpu.SMEM)
VMEM = pl.BlockSpec(memory_space=pltpu.VMEM)
ANY = pl.BlockSpec(memory_space=pl.ANY)
HBM = pl.BlockSpec(memory_space=pltpu.HBM)
DMA = pltpu.SemaphoreType.DMA


def cost(tasks, tiles):
    return pl.CostEstimate(flops=tasks * 2 * TILE**3 * 8, bytes_accessed=tiles * TILE * TILE * 4, transcendentals=0)


def shifted(array, axis, by):
    n = lax.axis_size(axis)
    return lax.ppermute(array, axis, [(i, (i + by) % n) for i in range(n)])


def tiles(n):
    return jax.ShapeDtypeStruct((n, TILE, TILE), F32)


def cut_tiles(n):
    return jax.ShapeDtypeStruct((n, TILE, 2 * TILE), jnp.bfloat16)


def join(plan, part, pa, pb, sides):
    per_cell = part.shape[0]
    pieces = 4 if per_cell % 4 == 0 else 1
    return pl.pallas_call(
        functools.partial(join_kernel, sides=sides, pieces=pieces),
        name="join_kernel",
        out_shape=pltpu.HBM((per_cell, TILE, TILE), F32),
        in_specs=[SMEM, VMEM, VMEM, VMEM],
        out_specs=HBM,
        scratch_shapes=[pltpu.VMEM((per_cell, TILE, TILE), F32), DMA((pieces,))],
        compiler_params=pltpu.CompilerParams(vmem_limit_bytes=16 * 2**20),
        cost_estimate=cost(0, 4 * per_cell),
    )(plan, part, pa, pb)


def finish(z_room, x_room, y_room, gp3, gp4, z, f, g, tzg, tfock, tfz, tzgt, ttrans, tn, fn, zl, ga):
    per_cell = z.shape[0]
    cap = tzg.shape[2]
    grown = pltpu.VMEM((5 * per_cell, TILE, TILE), F32)
    cut = pltpu.VMEM((per_cell, TILE, 2 * TILE), jnp.bfloat16)
    params = pltpu.CompilerParams(vmem_limit_bytes=40 * 2**20)
    gn = (shifted(g, "gx", 1), shifted(g, "gx", -1), ga[0], shifted(gp3, "gy", 1), ga[1], shifted(gp4, "gy", -1))
    z3, z4 = pl.pallas_call(
        pack_kernel,
        name="pack_kernel",
        out_shape=[tiles(z_room)] * 2,
        in_specs=[VMEM] * 5,
        out_specs=[ANY] * 2,
        scratch_shapes=[
            pltpu.VMEM((8, TILE), I32),
            pltpu.VMEM((2, z_room, TILE, TILE), F32),
            pltpu.SMEM((8, TILE), I32),
            DMA,
            DMA((2,)),
        ],
        compiler_params=pltpu.CompilerParams(vmem_limit_bytes=16 * 2**20),
        cost_estimate=cost(0, 4 * per_cell),
    )(fn[0], zl[0], fn[1], zl[1], z)
    zn = (shifted(z, "gx", 1), shifted(z, "gx", -1), shifted(z3, "gy", 1), shifted(z4, "gy", -1))
    plan, fs, ft, zs = pl.pallas_call(
        functools.partial(plan_kernel, lead=ga[0].shape[0]),
        name="plan_kernel",
        out_shape=[jax.ShapeDtypeStruct((PLAN_ROWS, TILE), I32)] + [cut_tiles(per_cell)] * 3,
        in_specs=[VMEM] * 11,
        out_specs=[VMEM] + [ANY] * 3,
        scratch_shapes=[pltpu.VMEM((8, cap), F32), pltpu.VMEM((3, per_cell, TILE, 2 * TILE), jnp.bfloat16), DMA((3,))],
        compiler_params=pltpu.CompilerParams(vmem_limit_bytes=24 * 2**20),
        cost_estimate=cost(cap, 8 * per_cell),
    )(tzg, tfock, tfz, tzgt, ttrans, *tn, f, z)
    ws = pl.pallas_call(
        w_kernel,
        name="w_kernel",
        out_shape=cut_tiles(per_cell),
        in_specs=[SMEM, SMEM, VMEM] + [ANY] * 7,
        out_specs=ANY,
        scratch_shapes=[grown, cut, pltpu.VMEM((per_cell + 1, TILE, TILE), F32), DMA((7,)), DMA],
        compiler_params=params,
        cost_estimate=cost(cap, 7 * per_cell),
    )(tzg, plan, zs, g, *gn)
    p = pl.pallas_call(
        p_kernel,
        name="p_kernel",
        out_shape=[tiles(n) for n in (per_cell, x_room, x_room, y_room, y_room)],
        in_specs=[SMEM] + [VMEM] * 2,
        out_specs=[ANY] * 5,
        scratch_shapes=[pltpu.VMEM((per_cell + 2 * x_room + 2 * y_room + 1, TILE, TILE), F32), DMA((5,))],
        compiler_params=params,
        cost_estimate=cost(2 * cap, 7 * per_cell),
    )(plan, ft, ws)
    pn = [shifted(p[k + 1], axis, -by) for k, (axis, by) in enumerate(STEPS)]
    fock_grad, part = pl.pallas_call(
        rest_kernel,
        name="rest_kernel",
        out_shape=[pltpu.HBM((per_cell, TILE, TILE), F32), tiles(per_cell)],
        in_specs=[SMEM] * 4 + [VMEM] * 5 + [ANY] * 12,
        out_specs=[HBM, ANY],
        scratch_shapes=[grown, grown, cut, pltpu.VMEM((3, per_cell + 1, TILE, TILE), F32), DMA((5,)), DMA((7,)), DMA((2,))],
        compiler_params=params,
        cost_estimate=cost(3 * cap, 14 * per_cell),
    )(tfock, tfz, tzgt, plan, fs, ws, p[0], pn[0], pn[1], z, *zn, g, *gn)
    return fock_grad, join(plan, part, pn[2], pn[3], (2, 3))


def rooms_of(per_cell, lead):
    levels = ((13, 18, 15, 12), (13, 19, 15, 13), (14, 20, 16, 14), (15, 21, 18, 16))
    scaled = [tuple(per_cell * room // 24 for room in level) for level in levels]
    return scaled + [(per_cell - lead,) + (per_cell,) * 3]


def body(z_factor, fock, cotangent, tasks_zg, tasks_fock, tasks_fz, tasks_zgt, tasks_trans):
    per_cell = z_factor.shape[2]
    nx, ny = lax.axis_size("gx"), lax.axis_size("gy")
    z, f, g = z_factor[0, 0], fock[0, 0], cotangent[0, 0]
    lists = (tasks_zg, tasks_fock, tasks_fz, tasks_zgt, tasks_trans)
    tzg, tfock, tfz, tzgt, ttrans = (t.reshape(t.shape[2], 1, t.shape[3]) for t in lists)
    a_list = jax.ShapeDtypeStruct(tzg.shape, I32)
    lead = per_cell // 3
    rooms = rooms_of(per_cell, lead)
    g_rooms = sorted({room[0] for room in rooms})
    packs = 2 * len(g_rooms)
    met = pl.pallas_call(
        functools.partial(meet_kernel, rooms=rooms, g_rooms=g_rooms, lead=lead, cuts=lead // 2),
        name="meet_kernel",
        out_shape=[tiles(lead)] * 2 + [a_list] * 8 + [tiles(room) for room in g_rooms for _ in range(2)] + [jax.ShapeDtypeStruct((1, 1), I32)],
        in_specs=[VMEM] * 5 + [ANY],
        out_specs=[ANY] * 2 + [VMEM] * 8 + [ANY] * packs + [SMEM],
        scratch_shapes=[
            pltpu.VMEM((2,) + tzg.shape, I32),
            pltpu.VMEM((2,) + tzg.shape, I32),
            pltpu.VMEM((1, TILE), I32),
            pltpu.VMEM((nx, TILE), I32),
            pltpu.VMEM((ny, nx, TILE), I32),
            pltpu.VMEM((8, TILE), I32),
            pltpu.SMEM((8, TILE), I32),
            pltpu.VMEM((per_cell - lead, TILE, TILE), F32),
            pltpu.VMEM((2, per_cell - lead, TILE, TILE), F32),
            DMA((4,)),
            DMA((4,)),
            DMA((12,)),
            DMA((12,)),
            DMA((nx,)),
            DMA((nx,)),
            DMA((ny,)),
            DMA((ny,)),
            DMA((4,)),
            DMA((packs,)),
        ],
        compiler_params=pltpu.CompilerParams(collective_id=0, has_side_effects=True),
    )(tzg, tfock, tfz, tzgt, ttrans, g)
    ga, tn, fn, zl, gp, level = met[:2], met[2:6], met[6:8], met[8:10], met[10 : 10 + packs], met[-1]

    def branch(g_room, z_room, x_room, y_room):
        at = 2 * g_rooms.index(g_room)
        return lambda gp, *rest: finish(z_room, x_room, y_room, gp[at], gp[at + 1], *rest)

    operands = (gp, z, f, g, tzg, tfock, tfz, tzgt, ttrans, tn, fn, zl, ga)
    fock_grad, factor_grad = lax.switch(level[0, 0], [branch(*room) for room in rooms], *operands)
    return fock_grad[None, None], factor_grad[None, None]


def solution(mesh):
    cells = P("gx", "gy", None, None, None)
    lists = P("gx", "gy", None, None)
    return jax.shard_map(
        body,
        mesh=mesh,
        in_specs=(cells,) * 3 + (lists,) * 5,
        out_specs=(cells, cells),
        check_vma=False,
    )
```

```python
import functools

import jax
import jax.numpy as jnp
from jax import lax
from jax.experimental import pallas as pl
from jax.experimental.pallas import tpu as pltpu
from jax.sharding import PartitionSpec as P


TILE = 128
UNROLL = 8
F32 = jnp.float32
I32 = jnp.int32
MESH = pl.DeviceIdType.MESH
STEPS = (("gx", -1), ("gx", 1), ("gy", -1), ("gy", 1))


def split(tile):
    high = tile.astype(jnp.bfloat16)
    low = (tile - high.astype(F32)).astype(jnp.bfloat16)
    return jnp.concatenate([high, low], axis=1)


def product(left, right, turned):
    if turned:
        high, low = right[:, :TILE], right[:, TILE:]
        rows = jnp.concatenate([high, low], axis=0)
        operand = jnp.concatenate([rows, rows], axis=1)
        both = lax.dot_general(left, operand, (((1,), (1,)), ((), ())), preferred_element_type=F32)
    else:
        operand = jnp.concatenate([right, right], axis=0)
        both = lax.dot_general(left, operand, (((1,), (0,)), ((), ())), preferred_element_type=F32)
    return both[:, :TILE] + both[:, TILE:]


def run_list(count, entry, left_of, right_of, turned, total, unroll=UNROLL):
    def step(turn, _):
        entries = [entry(turn * unroll + i) for i in range(unroll)]
        values = [product(left_of(a), right_of(b), turned) for _, a, b in entries]
        for (t, _, _), value in zip(entries, values):
            total[t] += value
        return 0

    lax.fori_loop(0, (count + unroll - 1) // unroll, step, 0)


def live_count(tasks, per_cell):
    length = tasks.shape[2]
    return lax.while_loop(
        lambda n: jnp.logical_and(n < length, tasks[0, 0, jnp.minimum(n, length - 1)] < per_cell),
        lambda n: n + 1,
        jnp.int32(0),
    )


def split_all(source, target, per_cell):
    def step(i, _):
        target[i] = split(source[i])
        return 0

    lax.fori_loop(0, per_cell, step, 0)


def moved_entry(tasks, plan, at):
    return lambda e: (tasks[0, 0, e], tasks[1, 0, e], plan[at, e])


def fetch(sources, grown, sems):
    copies = [
        pltpu.make_async_copy(src, grown.at[pl.ds(at, src.shape[0])], sems.at[i]) for i, (src, at) in enumerate(sources)
    ]
    for c in copies:
        c.start()
    return copies


FOCK_ROW, FZ_ROW, MAP_ROW, ZG_ROW, ZGT_ROW, LIST_ROW, PLAN_ROWS = 0, 1, 2, 6, 7, 8, 32


class Tables:
    def __init__(self, per_cell, length):
        self.per_cell, self.length = per_cell, length
        self.row = lax.broadcasted_iota(I32, (per_cell, length), 0)
        self.lane = lax.broadcasted_iota(I32, (1, TILE), 1)
        self.number = lax.broadcasted_iota(I32, (per_cell, TILE), 0)

    def hits(self, key):
        return jnp.broadcast_to(key, self.row.shape) == self.row

    def named(self, keys, first=0):
        found = sum(self.hits(key).astype(I32) for key in keys)
        found = jnp.where(self.row >= first, found, 0)
        return jnp.minimum(jnp.max(found, axis=1, keepdims=True), 1)

    def of_cell(self, lists, k, first=0):
        return self.named([tasks[2] - k * self.per_cell for tasks in lists], first)

    def inside(self, tasks, k):
        a = tasks[1]
        here = jnp.logical_and(a >= k * self.per_cell, a < (k + 1) * self.per_cell)
        return jnp.logical_and(here, tasks[0] < self.per_cell)

    def outs(self, tasks, k):
        return jnp.where(self.inside(tasks, k), tasks[0], self.per_cell)

    def ranked(self, found):
        square = (self.per_cell, self.per_cell)
        below = (lax.broadcasted_iota(I32, square, 1) < lax.broadcasted_iota(I32, square, 0)).astype(F32)
        return jnp.dot(below, jnp.broadcast_to(found, self.number.shape).astype(F32), preferred_element_type=F32)

    def packed_rows(self, found):
        spread = jnp.broadcast_to(self.lane, self.number.shape).astype(F32)
        here = jnp.logical_and(self.ranked(found) == spread, jnp.broadcast_to(found, self.number.shape) == 1)
        order = jnp.sum(jnp.where(here, self.number, 0), axis=0, keepdims=True)
        return jnp.where(self.lane == TILE - 1, jnp.sum(found), order)

    def rank_of(self, key, found):
        rank = self.ranked(found)[:, : self.length].astype(I32)
        return jnp.sum(jnp.where(self.hits(key), rank, 0), axis=0, keepdims=True)

    def places(self, tasks, lists, first=0):
        place = tasks[2]
        for k in (3, 4):
            key = tasks[2] - k * self.per_cell
            here = jnp.logical_and(key >= first, key < self.per_cell)
            rank = self.rank_of(key, self.of_cell(lists, k, first))
            place = jnp.where(here, k * self.per_cell + first + rank, place)
        return place


def by_quarter(lane, values):
    result = values[3]
    for i in (2, 1, 0):
        result = jnp.where(lane < (i + 1) * (TILE // 4), values[i], result)
    return result


def meet_kernel(tzg, tfock, tfz, tzgt, ttrans, g, *refs, rooms, g_rooms, lead, cuts):
    packs = 2 * len(g_rooms)
    ga, tn, fn, zl, gp = refs[:2], refs[2:6], refs[6:8], refs[8:10], refs[10 : 10 + packs]
    (level, gl, gt, msg, line, lines, pick, picked, gv, packed, bulk_s, bulk_r, list_s, list_r) = refs[10 + packs : 24 + packs]
    line_s, line_r, lines_s, lines_r, own, put = refs[24 + packs :]
    ny, nx = line.shape[0], lines.shape[0]
    per_cell = g.shape[0]
    ix, iy = lax.axis_index("gx"), lax.axis_index("gy")
    barrier = pltpu.get_barrier_semaphore()
    for j in range(1, nx):
        pl.semaphore_signal(barrier, inc=1, device_id=(lax.rem(ix + j, nx), iy), device_id_type=MESH)
    for j in range(1, ny):
        pl.semaphore_signal(barrier, inc=1, device_id=(ix, lax.rem(iy + j, ny)), device_id_type=MESH)
    load = pltpu.make_async_copy(g.at[pl.ds(lead, per_cell - lead)], gv, own.at[3])
    load.start()
    others = []
    for axis, by in STEPS:
        others.append((lax.rem(ix + by + nx, nx), iy) if axis == "gx" else (ix, lax.rem(iy + by + ny, ny)))
    pl.semaphore_wait(barrier, nx + ny - 2)

    lists = []
    for i in range(2):
        lists += [(tzg, gl.at[i], others[2 + i]), (tzgt, gt.at[i], others[2 + i])]
        lists += [(tfock, fn[i], others[2 + i]), (tfz, zl[i], others[2 + i])]
    lists += [(ttrans, tn[k], others[k]) for k in range(4)]
    small = []
    for i, (src, dst, to) in enumerate(lists):
        small.append(pltpu.make_async_remote_copy(src, dst, list_s.at[i], list_r.at[i], device_id=to, device_id_type=MESH))
        small[-1].start()

    def bulk(i, k, start, size):
        part = pl.ds(start, size)
        return pltpu.make_async_remote_copy(
            g.at[part], ga[(k ^ 1) - 2].at[part], bulk_s.at[i], bulk_r.at[i], device_id=others[k], device_id_type=MESH
        )

    large = [bulk(0, 2, 0, cuts), bulk(1, 3, 0, cuts)]
    for c in large:
        c.start()

    tables = Tables(per_cell, tfock.shape[2])

    def most(found):
        return functools.reduce(jnp.maximum, [jnp.sum(v) for v in found])

    needs = (
        most([tables.of_cell((tzg, tzgt), k, lead) for k in (3, 4)]),
        most([tables.of_cell((tfock, tfz), k) for k in (3, 4)]),
        most([tables.named((tables.outs(ttrans, k),)) for k in (1, 2)]),
        most([tables.named((tables.outs(ttrans, k),)) for k in (3, 4)]),
    )
    msg[...] = by_quarter(tables.lane, needs)
    keep = pltpu.make_async_copy(msg, line.at[pl.ds(0, 1)], own.at[0])
    keep.start()
    keep.wait()
    first = []
    for j in range(1, ny):
        to = (ix, lax.rem(iy + j, ny))
        row = line.at[pl.ds(0, 1)]
        first.append(pltpu.make_async_remote_copy(row, line.at[pl.ds(j, 1)], line_s.at[j], line_r.at[j], device_id=to, device_id_type=MESH))
        first[-1].start()
    rest = [bulk(2, 2, cuts, lead - cuts), bulk(3, 3, cuts, lead - cuts)]
    for c in rest:
        c.start()
    for c in first:
        c.wait()
    keep = pltpu.make_async_copy(line, lines.at[0], own.at[1])
    keep.start()
    second = []
    for j in range(1, nx):
        to = (lax.rem(ix + j, nx), iy)
        second.append(pltpu.make_async_remote_copy(line, lines.at[j], lines_s.at[j], lines_r.at[j], device_id=to, device_id_type=MESH))
        second[-1].start()
    for c in small:
        c.wait()

    for side in range(2):
        order = tables.packed_rows(tables.of_cell((gl.at[side], gt.at[side]), 3 + side, lead))
        pick[side : side + 1, :] = jnp.maximum(order - lead, 0)
    copy = pltpu.make_async_copy(pick, picked, own.at[2])
    copy.start()
    copy.wait()
    load.wait()
    puts = []
    for side in range(2):

        def take(s, _, side=side):
            packed[side, s] = gv[picked[side, s]]
            return 0

        lax.fori_loop(0, per_cell - lead, take, 0)
        for i, room in enumerate(g_rooms):
            puts.append(pltpu.make_async_copy(packed.at[side, pl.ds(0, room)], gp[2 * i + side], put.at[2 * i + side]))
            puts[-1].start()
    keep.wait()
    for c in second:
        c.wait()
    found = jnp.max(lines[...], axis=0)
    lane = lax.broadcasted_iota(I32, found.shape, 1)
    needs = [jnp.max(jnp.where(by_quarter(lane, [int(i == j) for j in range(4)]) == 1, found, 0)) for i in range(4)]
    short = []
    for level_rooms in rooms[:-1]:
        over = [need > room for need, room in zip(needs, level_rooms)]
        short.append(functools.reduce(jnp.logical_or, over).astype(I32))
    level[0, 0] = sum(short)
    for c in large + rest + puts:
        c.wait()


def pack_kernel(f3, z3, f4, z4, z, out3, out4, pick, packed, picked, own, put):
    per_cell, room = z.shape[0], out3.shape[0]
    tables = Tables(per_cell, f3.shape[2])
    for side, lists in enumerate(((f3, z3), (f4, z4))):
        pick[side : side + 1, :] = tables.packed_rows(tables.of_cell(lists, 3 + side))
    copy = pltpu.make_async_copy(pick, picked, own)
    copy.start()
    copy.wait()
    puts = []
    for side, out in enumerate((out3, out4)):

        def take(s, _, side=side):
            packed[side, s] = z[picked[side, s]]
            return 0

        lax.fori_loop(0, room, take, 0)
        puts.append(pltpu.make_async_copy(packed.at[side], out, put.at[side]))
        puts[-1].start()
    for c in puts:
        c.wait()


def plan_kernel(tzg, tfock, tfz, tzgt, t0, t1, t2, t3, t4, f, z, plan, fs, ft, zs, table, cut, put, *, lead):
    per_cell, length = f.shape[0], tfock.shape[2]

    def cut_all(i, _):
        tile = f[i]
        cut[0, i] = split(tile)
        cut[1, i] = split(tile.T)
        cut[2, i] = split(z[i])
        return 0

    lax.fori_loop(0, per_cell, cut_all, 0)
    puts = [pltpu.make_async_copy(cut.at[i], out, put.at[i]) for i, out in enumerate((fs, ft, zs))]
    for c in puts:
        c.start()
    tables = Tables(per_cell, length)
    lane = tables.lane
    plan[...] = jnp.zeros_like(plan)
    for at, tasks, lists, first in (
        (FOCK_ROW, tfock, (tfock, tfz), 0),
        (FZ_ROW, tfz, (tfock, tfz), 0),
        (ZG_ROW, tzg, (tzg, tzgt), lead),
        (ZGT_ROW, tzgt, (tzg, tzgt), lead),
    ):
        plan[at : at + 1, pl.ds(0, length)] = tables.places(tasks, lists, first)
    for k in range(1, 5):
        plan[MAP_ROW + k - 1 : MAP_ROW + k, :] = tables.packed_rows(tables.named((tables.outs(t0, k),)))
    square = (length, length)
    before = (lax.broadcasted_iota(I32, square, 0) < lax.broadcasted_iota(I32, square, 1)).astype(F32)
    same = (lax.broadcasted_iota(I32, square, 0) == lax.broadcasted_iota(I32, square, 1)).astype(F32)
    slots = lax.broadcasted_iota(I32, (length, TILE), 1).astype(F32)
    table[...] = jnp.zeros_like(table)
    for k, tasks in enumerate((t0, t1, t2, t3, t4)):
        here, out = tables.inside(tasks, k), tables.outs(tasks, k)
        slot = out if k == 0 else tables.rank_of(out, tables.named((out,)))
        for i, value in enumerate((slot, tasks[1] - k * per_cell, tasks[2] - k * per_cell, here)):
            table[i : i + 1, :] = value.astype(F32)
        earlier = jnp.dot(table[...], before, preferred_element_type=F32)
        table[4:5, :] = earlier[3:4, :]
        turned = lax.dot_general(same, table[...], (((1,), (1,)), ((), ())), preferred_element_type=F32)
        to_slot = jnp.logical_and(jnp.broadcast_to(turned[:, 4:5], slots.shape) == slots, jnp.broadcast_to(turned[:, 3:4], slots.shape) > 0.5)
        moved = jnp.dot(table[...], to_slot.astype(F32), preferred_element_type=F32).astype(I32)
        count = jnp.sum(here.astype(I32))
        at = LIST_ROW + 4 * k
        for i in range(3):
            plan[at + i : at + i + 1, :] = moved[i : i + 1, :]
        plan[at : at + 1, :] = jnp.where(lane < count, moved[0:1, :], TILE - 1)
        plan[at + 3 : at + 4, :] = jnp.where(lane == TILE - 1, count, 0)
    for c in puts:
        c.wait()


def w_kernel(tasks, plan, zs, g0, g1, g2, a3, g3, a4, g4, ws, grown, cut, total, sems, osem):
    per_cell, lead = zs.shape[0], a3.shape[0]
    copies = fetch(g_places(per_cell, lead, g0, g1, g2, a3, g3, a4, g4), grown, sems)
    total[...] = jnp.zeros_like(total)
    live = live_count(tasks, per_cell)
    for c in copies:
        c.wait()
    entry = moved_entry(tasks, plan, ZG_ROW)
    run_list(live, entry, lambda a: zs[a], lambda b: split(grown[b]), False, total, 4)
    split_all(total, cut, per_cell)
    out = pltpu.make_async_copy(cut, ws, osem)
    out.start()
    out.wait()


def g_places(per_cell, lead, g0, g1, g2, a3, g3, a4, g4):
    places = [(src, k * per_cell) for k, src in enumerate((g0, g1, g2, a3, a4))]
    return places + [(g3, 3 * per_cell + lead), (g4, 4 * per_cell + lead)]


def p_kernel(plan, ft, ws, p0, p1, p2, p3, p4, total, osem):
    outs = (p0, p1, p2, p3, p4)
    starts = [sum(p.shape[0] for p in outs[:k]) for k in range(6)]
    last = starts[5]

    def zero(i, _):
        total[i] = jnp.zeros_like(total[i])
        return 0

    lax.fori_loop(0, last, zero, 0)

    def one(k, _):
        at = LIST_ROW + 4 * k
        first = sum(jnp.where(k == i, start, 0) for i, start in enumerate(starts[:5]))

        def entry(e):
            return jnp.minimum(first + plan[at, e], last), plan[at + 1, e], plan[at + 2, e]

        run_list(plan[at + 3, TILE - 1], entry, lambda a: ft[a], lambda b: ws[b], False, total, 4)
        return 0

    lax.fori_loop(0, 5, one, 0)
    copies = [pltpu.make_async_copy(total.at[pl.ds(starts[k], p.shape[0])], p, osem.at[k]) for k, p in enumerate(outs)]
    for c in copies:
        c.start()
    for c in copies:
        c.wait()


def add_packed(plan, side, packed, total):
    at = MAP_ROW + side

    def add(s, _):
        total[plan[at, s]] += packed[s]
        return 0

    lax.fori_loop(0, jnp.minimum(plan[at, TILE - 1], packed.shape[0]), add, 0)


def rest_kernel(tfock, tfz, tzgt, plan, fs, ws, p0, p1, p2, z0, z1, z2, z3, z4, g0, g1, g2, a3, g3, a4, g4, fock, factor, zgrown, ggrown, us, total, zsem, gsem, osem):
    per_cell, lead = p0.shape[0], a3.shape[0]
    zcopies = fetch([(src, k * per_cell) for k, src in enumerate((z0, z1, z2, z3, z4))], zgrown, zsem)
    gcopies = fetch(g_places(per_cell, lead, g0, g1, g2, a3, g3, a4, g4), ggrown, gsem)
    total[0] = jnp.zeros_like(total[0])
    total[1] = jnp.zeros_like(total[1])
    total[2, pl.ds(0, per_cell)] = p0[...]
    add_packed(plan, 0, p1, total.at[2])
    add_packed(plan, 1, p2, total.at[2])
    fz_live, fock_live, zgt_live = (live_count(tasks, per_cell) for tasks in (tfz, tfock, tzgt))
    for c in zcopies:
        c.wait()
    run_list(fz_live, moved_entry(tfz, plan, FZ_ROW), lambda a: fs[a], lambda b: split(zgrown[b]), False, total.at[0])
    split_all(total.at[0], us, per_cell)
    run_list(fock_live, moved_entry(tfock, plan, FOCK_ROW), lambda a: ws[a], lambda b: split(zgrown[b]), True, total.at[1])
    out1 = pltpu.make_async_copy(total.at[1, pl.ds(0, per_cell)], fock, osem.at[0])
    out1.start()
    for c in gcopies:
        c.wait()
    run_list(zgt_live, moved_entry(tzgt, plan, ZGT_ROW), lambda a: us[a], lambda b: split(ggrown[b]), True, total.at[2])
    out2 = pltpu.make_async_copy(total.at[2, pl.ds(0, per_cell)], factor, osem.at[1])
    out2.start()
    out1.wait()
    out2.wait()


def join_kernel(plan, part, pa, pb, factor, total, puts, *, sides, pieces):
    per_cell = part.shape[0]
    size = per_cell // pieces
    lists = tuple(zip(sides, (pa, pb)))
    counts = [jnp.minimum(plan[MAP_ROW + side, TILE - 1], p.shape[0]) for side, p in lists]
    at = [jnp.int32(0), jnp.int32(0)]
    stored = []
    for i in range(pieces):
        piece = pl.ds(i * size, size)
        total[piece] = part[piece]
        for j, (side, p) in enumerate(lists):

            def more(s, j=j, side=side, i=i):
                return jnp.logical_and(s < counts[j], plan[MAP_ROW + side, s] < (i + 1) * size)

            def add(s, side=side, p=p):
                total[plan[MAP_ROW + side, s]] += p[s]
                return s + 1

            at[j] = lax.while_loop(more, add, at[j])
        stored.append(pltpu.make_async_copy(total.at[piece], factor.at[piece], puts.at[i]))
        stored[-1].start()
    for c in stored:
        c.wait()


SMEM = pl.BlockSpec(memory_space=pltpu.SMEM)
VMEM = pl.BlockSpec(memory_space=pltpu.VMEM)
ANY = pl.BlockSpec(memory_space=pl.ANY)
HBM = pl.BlockSpec(memory_space=pltpu.HBM)
DMA = pltpu.SemaphoreType.DMA


def cost(tasks, tiles):
    return pl.CostEstimate(flops=tasks * 2 * TILE**3 * 8, bytes_accessed=tiles * TILE * TILE * 4, transcendentals=0)


def shifted(array, axis, by):
    n = lax.axis_size(axis)
    return lax.ppermute(array, axis, [(i, (i + by) % n) for i in range(n)])


def tiles(n):
    return jax.ShapeDtypeStruct((n, TILE, TILE), F32)


def cut_tiles(n):
    return jax.ShapeDtypeStruct((n, TILE, 2 * TILE), jnp.bfloat16)


def join(plan, part, pa, pb, sides):
    per_cell = part.shape[0]
    pieces = 4 if per_cell % 4 == 0 else 1
    return pl.pallas_call(
        functools.partial(join_kernel, sides=sides, pieces=pieces),
        name="join_kernel",
        out_shape=pltpu.HBM((per_cell, TILE, TILE), F32),
        in_specs=[SMEM, VMEM, VMEM, VMEM],
        out_specs=HBM,
        scratch_shapes=[pltpu.VMEM((per_cell, TILE, TILE), F32), DMA((pieces,))],
        compiler_params=pltpu.CompilerParams(vmem_limit_bytes=16 * 2**20),
        cost_estimate=cost(0, 4 * per_cell),
    )(plan, part, pa, pb)


def finish(z_room, x_room, y_room, gp3, gp4, z, f, g, tzg, tfock, tfz, tzgt, ttrans, tn, fn, zl, ga):
    per_cell = z.shape[0]
    cap = tzg.shape[2]
    grown = pltpu.VMEM((5 * per_cell, TILE, TILE), F32)
    cut = pltpu.VMEM((per_cell, TILE, 2 * TILE), jnp.bfloat16)
    params = pltpu.CompilerParams(vmem_limit_bytes=40 * 2**20)
    gy = (shifted(gp3, "gy", 1), shifted(gp4, "gy", -1))
    pack = pl.pallas_call(
        pack_kernel,
        name="pack_kernel",
        out_shape=[tiles(z_room)] * 2,
        in_specs=[VMEM] * 5,
        out_specs=[ANY] * 2,
        scratch_shapes=[
            pltpu.VMEM((8, TILE), I32),
            pltpu.VMEM((2, z_room, TILE, TILE), F32),
            pltpu.SMEM((8, TILE), I32),
            DMA,
            DMA((2,)),
        ],
        compiler_params=pltpu.CompilerParams(vmem_limit_bytes=16 * 2**20),
        cost_estimate=cost(0, 4 * per_cell),
    )
    z3, z4 = pack(fn[0], zl[0], fn[1], zl[1], z)
    g_late, z_late, z3, z4 = lax.optimization_barrier((g, z, z3, z4))
    gn = (shifted(g_late, "gx", 1), shifted(g_late, "gx", -1), ga[0], gy[0], ga[1], gy[1])
    zn = (shifted(z_late, "gx", 1), shifted(z_late, "gx", -1), shifted(z3, "gy", 1), shifted(z4, "gy", -1))
    plan, fs, ft, zs = pl.pallas_call(
        functools.partial(plan_kernel, lead=ga[0].shape[0]),
        name="plan_kernel",
        out_shape=[jax.ShapeDtypeStruct((PLAN_ROWS, TILE), I32)] + [cut_tiles(per_cell)] * 3,
        in_specs=[VMEM] * 11,
        out_specs=[VMEM] + [ANY] * 3,
        scratch_shapes=[pltpu.VMEM((8, cap), F32), pltpu.VMEM((3, per_cell, TILE, 2 * TILE), jnp.bfloat16), DMA((3,))],
        compiler_params=pltpu.CompilerParams(vmem_limit_bytes=24 * 2**20),
        cost_estimate=cost(cap, 8 * per_cell),
    )(tzg, tfock, tfz, tzgt, ttrans, *tn, f, z)
    ws = pl.pallas_call(
        w_kernel,
        name="w_kernel",
        out_shape=cut_tiles(per_cell),
        in_specs=[SMEM, SMEM, VMEM] + [ANY] * 7,
        out_specs=ANY,
        scratch_shapes=[grown, cut, pltpu.VMEM((per_cell + 1, TILE, TILE), F32), DMA((7,)), DMA],
        compiler_params=params,
        cost_estimate=cost(cap, 7 * per_cell),
    )(tzg, plan, zs, g, *gn)
    p = pl.pallas_call(
        p_kernel,
        name="p_kernel",
        out_shape=[tiles(n) for n in (per_cell, x_room, x_room, y_room, y_room)],
        in_specs=[SMEM] + [VMEM] * 2,
        out_specs=[ANY] * 5,
        scratch_shapes=[pltpu.VMEM((per_cell + 2 * x_room + 2 * y_room + 1, TILE, TILE), F32), DMA((5,))],
        compiler_params=params,
        cost_estimate=cost(2 * cap, 7 * per_cell),
    )(plan, ft, ws)
    pn = [shifted(p[k + 1], axis, -by) for k, (axis, by) in enumerate(STEPS)]
    fock_grad, part = pl.pallas_call(
        rest_kernel,
        name="rest_kernel",
        out_shape=[pltpu.HBM((per_cell, TILE, TILE), F32), tiles(per_cell)],
        in_specs=[SMEM] * 4 + [VMEM] * 5 + [ANY] * 12,
        out_specs=[HBM, ANY],
        scratch_shapes=[grown, grown, cut, pltpu.VMEM((3, per_cell + 1, TILE, TILE), F32), DMA((5,)), DMA((7,)), DMA((2,))],
        compiler_params=params,
        cost_estimate=cost(3 * cap, 14 * per_cell),
    )(tfock, tfz, tzgt, plan, fs, ws, p[0], pn[0], pn[1], z, *zn, g, *gn)
    return fock_grad, join(plan, part, pn[2], pn[3], (2, 3))


def rooms_of(per_cell, lead):
    levels = ((13, 18, 15, 12), (13, 19, 15, 13), (14, 20, 16, 14), (15, 21, 18, 16))
    scaled = [tuple(per_cell * room // 24 for room in level) for level in levels]
    return scaled + [(per_cell - lead,) + (per_cell,) * 3]


def body(z_factor, fock, cotangent, tasks_zg, tasks_fock, tasks_fz, tasks_zgt, tasks_trans):
    per_cell = z_factor.shape[2]
    nx, ny = lax.axis_size("gx"), lax.axis_size("gy")
    z, f, g = z_factor[0, 0], fock[0, 0], cotangent[0, 0]
    lists = (tasks_zg, tasks_fock, tasks_fz, tasks_zgt, tasks_trans)
    tzg, tfock, tfz, tzgt, ttrans = (t.reshape(t.shape[2], 1, t.shape[3]) for t in lists)
    a_list = jax.ShapeDtypeStruct(tzg.shape, I32)
    lead = per_cell // 3
    rooms = rooms_of(per_cell, lead)
    g_rooms = sorted({room[0] for room in rooms})
    packs = 2 * len(g_rooms)
    met = pl.pallas_call(
        functools.partial(meet_kernel, rooms=rooms, g_rooms=g_rooms, lead=lead, cuts=lead // 4),
        name="meet_kernel",
        out_shape=[tiles(lead)] * 2 + [a_list] * 8 + [tiles(room) for room in g_rooms for _ in range(2)] + [jax.ShapeDtypeStruct((1, 1), I32)],
        in_specs=[VMEM] * 5 + [ANY],
        out_specs=[ANY] * 2 + [VMEM] * 8 + [ANY] * packs + [SMEM],
        scratch_shapes=[
            pltpu.VMEM((2,) + tzg.shape, I32),
            pltpu.VMEM((2,) + tzg.shape, I32),
            pltpu.VMEM((1, TILE), I32),
            pltpu.VMEM((ny, TILE), I32),
            pltpu.VMEM((nx, ny, TILE), I32),
            pltpu.VMEM((8, TILE), I32),
            pltpu.SMEM((8, TILE), I32),
            pltpu.VMEM((per_cell - lead, TILE, TILE), F32),
            pltpu.VMEM((2, per_cell - lead, TILE, TILE), F32),
            DMA((4,)),
            DMA((4,)),
            DMA((12,)),
            DMA((12,)),
            DMA((ny,)),
            DMA((ny,)),
            DMA((nx,)),
            DMA((nx,)),
            DMA((4,)),
            DMA((packs,)),
        ],
        compiler_params=pltpu.CompilerParams(collective_id=0, has_side_effects=True),
    )(tzg, tfock, tfz, tzgt, ttrans, g)
    ga, tn, fn, zl, gp, level = met[:2], met[2:6], met[6:8], met[8:10], met[10 : 10 + packs], met[-1]

    def branch(g_room, z_room, x_room, y_room):
        at = 2 * g_rooms.index(g_room)
        return lambda gp, *rest: finish(z_room, x_room, y_room, gp[at], gp[at + 1], *rest)

    operands = (gp, z, f, g, tzg, tfock, tfz, tzgt, ttrans, tn, fn, zl, ga)
    fock_grad, factor_grad = lax.switch(level[0, 0], [branch(*room) for room in rooms], *operands)
    return fock_grad[None, None], factor_grad[None, None]


def solution(mesh):
    cells = P("gx", "gy", None, None, None)
    lists = P("gx", "gy", None, None)
    return jax.shard_map(
        body,
        mesh=mesh,
        in_specs=(cells,) * 3 + (lists,) * 5,
        out_specs=(cells, cells),
        check_vma=False,
    )
```

```python
import functools

import jax
import jax.numpy as jnp
from jax import lax
from jax.experimental import pallas as pl
from jax.experimental.pallas import tpu as pltpu
from jax.sharding import PartitionSpec as P


TILE = 128
UNROLL = 8
F32 = jnp.float32
I32 = jnp.int32
MESH = pl.DeviceIdType.MESH
STEPS = (("gx", -1), ("gx", 1), ("gy", -1), ("gy", 1))


def split(tile):
    high = tile.astype(jnp.bfloat16)
    low = (tile - high.astype(F32)).astype(jnp.bfloat16)
    return jnp.concatenate([high, low], axis=1)


def product(left, right, turned):
    if turned:
        high, low = right[:, :TILE], right[:, TILE:]
        rows = jnp.concatenate([high, low], axis=0)
        operand = jnp.concatenate([rows, rows], axis=1)
        both = lax.dot_general(left, operand, (((1,), (1,)), ((), ())), preferred_element_type=F32)
    else:
        operand = jnp.concatenate([right, right], axis=0)
        both = lax.dot_general(left, operand, (((1,), (0,)), ((), ())), preferred_element_type=F32)
    return both[:, :TILE] + both[:, TILE:]


def run_list(count, entry, left_of, right_of, turned, total, unroll=UNROLL):
    def step(turn, _):
        entries = [entry(turn * unroll + i) for i in range(unroll)]
        values = [product(left_of(a), right_of(b), turned) for _, a, b in entries]
        for (t, _, _), value in zip(entries, values):
            total[t] += value
        return 0

    lax.fori_loop(0, (count + unroll - 1) // unroll, step, 0)


def live_count(tasks, per_cell):
    length = tasks.shape[2]
    return lax.while_loop(
        lambda n: jnp.logical_and(n < length, tasks[0, 0, jnp.minimum(n, length - 1)] < per_cell),
        lambda n: n + 1,
        jnp.int32(0),
    )


def split_all(source, target, per_cell):
    def step(i, _):
        target[i] = split(source[i])
        return 0

    lax.fori_loop(0, per_cell, step, 0)


def each(count, do):
    def step(i, _):
        do(i)
        return 0

    lax.fori_loop(0, count, step, 0)


def clear(total, first, count):
    def do(i):
        total[first + i] = jnp.zeros(total.shape[1:], total.dtype)

    each(count, do)


def moved_entry(tasks, plan, at):
    return lambda e: (tasks[0, 0, e], tasks[1, 0, e], plan[at, e])


def fetch(sources, grown, sems):
    copies = [
        pltpu.make_async_copy(src, grown.at[pl.ds(at, src.shape[0])], sems.at[i]) for i, (src, at) in enumerate(sources)
    ]
    for c in copies:
        c.start()
    return copies


FOCK_ROW, FZ_ROW, MAP_ROW, ZG_ROW, ZGT_ROW, LIST_ROW, PLAN_ROWS = 0, 1, 2, 6, 7, 8, 32


class Tables:
    def __init__(self, per_cell, length):
        self.per_cell, self.length = per_cell, length
        self.row = lax.broadcasted_iota(I32, (per_cell, length), 0)
        self.lane = lax.broadcasted_iota(I32, (1, TILE), 1)
        self.number = lax.broadcasted_iota(I32, (per_cell, TILE), 0)

    def hits(self, key):
        return jnp.broadcast_to(key, self.row.shape) == self.row

    def named(self, keys, first=0):
        found = sum(self.hits(key).astype(I32) for key in keys)
        found = jnp.where(self.row >= first, found, 0)
        return jnp.minimum(jnp.max(found, axis=1, keepdims=True), 1)

    def of_cell(self, lists, k, first=0):
        return self.named([tasks[2] - k * self.per_cell for tasks in lists], first)

    def inside(self, tasks, k):
        a = tasks[1]
        here = jnp.logical_and(a >= k * self.per_cell, a < (k + 1) * self.per_cell)
        return jnp.logical_and(here, tasks[0] < self.per_cell)

    def outs(self, tasks, k):
        return jnp.where(self.inside(tasks, k), tasks[0], self.per_cell)

    def ranked(self, found):
        square = (self.per_cell, self.per_cell)
        below = (lax.broadcasted_iota(I32, square, 1) < lax.broadcasted_iota(I32, square, 0)).astype(F32)
        return jnp.dot(below, jnp.broadcast_to(found, self.number.shape).astype(F32), preferred_element_type=F32)

    def packed_rows(self, found):
        spread = jnp.broadcast_to(self.lane, self.number.shape).astype(F32)
        here = jnp.logical_and(self.ranked(found) == spread, jnp.broadcast_to(found, self.number.shape) == 1)
        order = jnp.sum(jnp.where(here, self.number, 0), axis=0, keepdims=True)
        return jnp.where(self.lane == TILE - 1, jnp.sum(found), order)

    def rank_of(self, key, found):
        rank = self.ranked(found)[:, : self.length].astype(I32)
        return jnp.sum(jnp.where(self.hits(key), rank, 0), axis=0, keepdims=True)

    def places(self, tasks, lists, first=0):
        place = tasks[2]
        for k in (3, 4):
            key = tasks[2] - k * self.per_cell
            here = jnp.logical_and(key >= first, key < self.per_cell)
            rank = self.rank_of(key, self.of_cell(lists, k, first))
            place = jnp.where(here, k * self.per_cell + first + rank, place)
        return place


def by_quarter(lane, values):
    result = values[3]
    for i in (2, 1, 0):
        result = jnp.where(lane < (i + 1) * (TILE // 4), values[i], result)
    return result


def meet_kernel(tzg, tfock, tfz, tzgt, ttrans, g, *refs, rooms, g_rooms, lead, cuts):
    packs = 2 * len(g_rooms)
    ga, tn, fn, zl, gp = refs[:2], refs[2:6], refs[6:8], refs[8:10], refs[10 : 10 + packs]
    (level, gl, gt, msg, line, lines, pick, picked, gv, packed, bulk_s, bulk_r, list_s, list_r) = refs[10 + packs : 24 + packs]
    line_s, line_r, lines_s, lines_r, own, put = refs[24 + packs :]
    ny, nx = line.shape[0], lines.shape[0]
    per_cell = g.shape[0]
    ix, iy = lax.axis_index("gx"), lax.axis_index("gy")
    barrier = pltpu.get_barrier_semaphore()
    for j in range(1, nx):
        pl.semaphore_signal(barrier, inc=1, device_id=(lax.rem(ix + j, nx), iy), device_id_type=MESH)
    for j in range(1, ny):
        pl.semaphore_signal(barrier, inc=1, device_id=(ix, lax.rem(iy + j, ny)), device_id_type=MESH)
    load = pltpu.make_async_copy(g.at[pl.ds(lead, per_cell - lead)], gv, own.at[3])
    load.start()
    others = []
    for axis, by in STEPS:
        others.append((lax.rem(ix + by + nx, nx), iy) if axis == "gx" else (ix, lax.rem(iy + by + ny, ny)))
    pl.semaphore_wait(barrier, nx + ny - 2)

    def bulk(i, k, start, size):
        part = pl.ds(start, size)
        return pltpu.make_async_remote_copy(
            g.at[part], ga[(k ^ 1) - 2].at[part], bulk_s.at[i], bulk_r.at[i], device_id=others[k], device_id_type=MESH
        )

    large = [bulk(0, 2, 0, cuts), bulk(1, 3, 0, cuts)]
    for c in large:
        c.start()

    lists = []
    for i in range(2):
        lists += [(tzg, gl.at[i], others[2 + i]), (tzgt, gt.at[i], others[2 + i])]
        lists += [(tfock, fn[i], others[2 + i]), (tfz, zl[i], others[2 + i])]
    lists += [(ttrans, tn[k], others[k]) for k in range(4)]
    small = []
    for i, (src, dst, to) in enumerate(lists):
        small.append(pltpu.make_async_remote_copy(src, dst, list_s.at[i], list_r.at[i], device_id=to, device_id_type=MESH))
        small[-1].start()

    tables = Tables(per_cell, tfock.shape[2])

    def most(found):
        return functools.reduce(jnp.maximum, [jnp.sum(v) for v in found])

    needs = (
        most([tables.of_cell((tzg, tzgt), k, lead) for k in (3, 4)]),
        most([tables.of_cell((tfock, tfz), k) for k in (3, 4)]),
        most([tables.named((tables.outs(ttrans, k),)) for k in (1, 2)]),
        most([tables.named((tables.outs(ttrans, k),)) for k in (3, 4)]),
    )
    msg[...] = by_quarter(tables.lane, needs)
    keep = pltpu.make_async_copy(msg, line.at[pl.ds(0, 1)], own.at[0])
    keep.start()
    keep.wait()
    first = []
    for j in range(1, ny):
        to = (ix, lax.rem(iy + j, ny))
        row = line.at[pl.ds(0, 1)]
        first.append(pltpu.make_async_remote_copy(row, line.at[pl.ds(j, 1)], line_s.at[j], line_r.at[j], device_id=to, device_id_type=MESH))
        first[-1].start()
    rest = [bulk(2, 2, cuts, lead - cuts), bulk(3, 3, cuts, lead - cuts)]
    for c in rest:
        c.start()
    for c in first:
        c.wait()
    keep = pltpu.make_async_copy(line, lines.at[0], own.at[1])
    keep.start()
    second = []
    for j in range(1, nx):
        to = (lax.rem(ix + j, nx), iy)
        second.append(pltpu.make_async_remote_copy(line, lines.at[j], lines_s.at[j], lines_r.at[j], device_id=to, device_id_type=MESH))
        second[-1].start()
    for c in small:
        c.wait()

    for side in range(2):
        order = tables.packed_rows(tables.of_cell((gl.at[side], gt.at[side]), 3 + side, lead))
        pick[side : side + 1, :] = jnp.maximum(order - lead, 0)
    copy = pltpu.make_async_copy(pick, picked, own.at[2])
    copy.start()
    copy.wait()
    load.wait()
    puts = []
    for side in range(2):

        def take(s, _, side=side):
            packed[side, s] = gv[picked[side, s]]
            return 0

        lax.fori_loop(0, per_cell - lead, take, 0)
        for i, room in enumerate(g_rooms):
            puts.append(pltpu.make_async_copy(packed.at[side, pl.ds(0, room)], gp[2 * i + side], put.at[2 * i + side]))
            puts[-1].start()
    keep.wait()
    for c in second:
        c.wait()
    found = jnp.max(lines[...], axis=0)
    lane = lax.broadcasted_iota(I32, found.shape, 1)
    needs = [jnp.max(jnp.where(by_quarter(lane, [int(i == j) for j in range(4)]) == 1, found, 0)) for i in range(4)]
    first_fit, unfit = 0, jnp.int32(1)
    for level_rooms in rooms[:-1]:
        over = [need > room for need, room in zip(needs, level_rooms)]
        unfit = unfit * functools.reduce(jnp.logical_or, over).astype(I32)
        first_fit = first_fit + unfit
    level[0, 0] = first_fit
    for c in large + rest + puts:
        c.wait()


def pack_kernel(f3, z3, f4, z4, z, out3, out4, pick, packed, picked, own, put):
    per_cell, room = z.shape[0], out3.shape[0]
    tables = Tables(per_cell, f3.shape[2])
    for side, lists in enumerate(((f3, z3), (f4, z4))):
        pick[side : side + 1, :] = tables.packed_rows(tables.of_cell(lists, 3 + side))
    copy = pltpu.make_async_copy(pick, picked, own)
    copy.start()
    copy.wait()
    puts = []
    for side, out in enumerate((out3, out4)):

        def take(s, _, side=side):
            packed[side, s] = z[picked[side, s]]
            return 0

        lax.fori_loop(0, room, take, 0)
        puts.append(pltpu.make_async_copy(packed.at[side], out, put.at[side]))
        puts[-1].start()
    for c in puts:
        c.wait()


def plan_kernel(tzg, tfock, tfz, tzgt, t0, t1, t2, t3, t4, f, z, plan, fs, ft, zs, table, cut, put, *, lead):
    per_cell, length = f.shape[0], tfock.shape[2]

    def cut_all(i, _):
        tile = f[i]
        cut[0, i] = split(tile)
        cut[1, i] = split(tile.T)
        cut[2, i] = split(z[i])
        return 0

    lax.fori_loop(0, per_cell, cut_all, 0)
    puts = [pltpu.make_async_copy(cut.at[i], out, put.at[i]) for i, out in enumerate((fs, ft, zs))]
    for c in puts:
        c.start()
    tables = Tables(per_cell, length)
    lane = tables.lane
    plan[...] = jnp.zeros_like(plan)
    for at, tasks, lists, first in (
        (FOCK_ROW, tfock, (tfock, tfz), 0),
        (FZ_ROW, tfz, (tfock, tfz), 0),
        (ZG_ROW, tzg, (tzg, tzgt), lead),
        (ZGT_ROW, tzgt, (tzg, tzgt), lead),
    ):
        plan[at : at + 1, pl.ds(0, length)] = tables.places(tasks, lists, first)
    for k in range(1, 5):
        plan[MAP_ROW + k - 1 : MAP_ROW + k, :] = tables.packed_rows(tables.named((tables.outs(t0, k),)))
    square = (length, length)
    before = (lax.broadcasted_iota(I32, square, 0) < lax.broadcasted_iota(I32, square, 1)).astype(F32)
    same = (lax.broadcasted_iota(I32, square, 0) == lax.broadcasted_iota(I32, square, 1)).astype(F32)
    slots = lax.broadcasted_iota(I32, (length, TILE), 1).astype(F32)
    table[...] = jnp.zeros_like(table)
    for k, tasks in enumerate((t0, t1, t2, t3, t4)):
        here, out = tables.inside(tasks, k), tables.outs(tasks, k)
        slot = out if k == 0 else tables.rank_of(out, tables.named((out,)))
        for i, value in enumerate((slot, tasks[1] - k * per_cell, tasks[2] - k * per_cell, here)):
            table[i : i + 1, :] = value.astype(F32)
        earlier = jnp.dot(table[...], before, preferred_element_type=F32)
        table[4:5, :] = earlier[3:4, :]
        turned = lax.dot_general(same, table[...], (((1,), (1,)), ((), ())), preferred_element_type=F32)
        to_slot = jnp.logical_and(jnp.broadcast_to(turned[:, 4:5], slots.shape) == slots, jnp.broadcast_to(turned[:, 3:4], slots.shape) > 0.5)
        moved = jnp.dot(table[...], to_slot.astype(F32), preferred_element_type=F32).astype(I32)
        count = jnp.sum(here.astype(I32))
        at = LIST_ROW + 4 * k
        for i in range(3):
            plan[at + i : at + i + 1, :] = moved[i : i + 1, :]
        plan[at : at + 1, :] = jnp.where(lane < count, moved[0:1, :], TILE - 1)
        plan[at + 3 : at + 4, :] = jnp.where(lane == TILE - 1, count, 0)
    for c in puts:
        c.wait()


def w_kernel(tasks, plan, zs, g0, g1, g2, a3, g3, a4, g4, ws, grown, cut, total, sems, osem):
    per_cell, lead = zs.shape[0], a3.shape[0]
    copies = fetch(g_places(per_cell, lead, g0, g1, g2, a3, g3, a4, g4), grown, sems)
    clear(total, 0, per_cell)
    live = live_count(tasks, per_cell)
    for c in copies:
        c.wait()
    entry = moved_entry(tasks, plan, ZG_ROW)
    run_list(live, entry, lambda a: zs[a], lambda b: split(grown[b]), False, total, 4)
    split_all(total, cut, per_cell)
    out = pltpu.make_async_copy(cut, ws, osem)
    out.start()
    out.wait()


def g_places(per_cell, lead, g0, g1, g2, a3, g3, a4, g4):
    places = [(src, k * per_cell) for k, src in enumerate((g0, g1, g2, a3, a4))]
    return places + [(g3, 3 * per_cell + lead), (g4, 4 * per_cell + lead)]


def p_kernel(plan, ft, ws, p0, p1, p2, p3, p4, total, osem):
    outs = (p0, p1, p2, p3, p4)
    starts = [sum(p.shape[0] for p in outs[:k]) for k in range(6)]
    last = starts[5]

    clear(total, 0, last)

    def one(k, _):
        at = LIST_ROW + 4 * k
        first = sum(jnp.where(k == i, start, 0) for i, start in enumerate(starts[:5]))

        def entry(e):
            return jnp.minimum(first + plan[at, e], last), plan[at + 1, e], plan[at + 2, e]

        run_list(plan[at + 3, TILE - 1], entry, lambda a: ft[a], lambda b: ws[b], False, total, 4)
        return 0

    lax.fori_loop(0, 5, one, 0)
    copies = [pltpu.make_async_copy(total.at[pl.ds(starts[k], p.shape[0])], p, osem.at[k]) for k, p in enumerate(outs)]
    for c in copies:
        c.start()
    for c in copies:
        c.wait()


def add_packed(plan, side, packed, total):
    at = MAP_ROW + side

    def add(s, _):
        total[plan[at, s]] += packed[s]
        return 0

    lax.fori_loop(0, jnp.minimum(plan[at, TILE - 1], packed.shape[0]), add, 0)


def rest_kernel(tfock, tfz, tzgt, plan, fs, ws, p0, p1, p2, z0, z1, z2, z3, z4, g0, g1, g2, a3, g3, a4, g4, fock, factor, zgrown, ggrown, us, total, zsem, gsem, osem):
    per_cell, lead = p0.shape[0], a3.shape[0]
    zcopies = fetch([(src, k * per_cell) for k, src in enumerate((z0, z1, z2, z3, z4))], zgrown, zsem)
    gcopies = fetch(g_places(per_cell, lead, g0, g1, g2, a3, g3, a4, g4), ggrown, gsem)
    clear(total.at[0], 0, per_cell)
    clear(total.at[1], 0, per_cell)

    def begin(i):
        total[2, i] = p0[i]

    each(per_cell, begin)
    add_packed(plan, 0, p1, total.at[2])
    add_packed(plan, 1, p2, total.at[2])
    fz_live, fock_live, zgt_live = (live_count(tasks, per_cell) for tasks in (tfz, tfock, tzgt))
    for c in zcopies:
        c.wait()
    run_list(fz_live, moved_entry(tfz, plan, FZ_ROW), lambda a: fs[a], lambda b: split(zgrown[b]), False, total.at[0])
    split_all(total.at[0], us, per_cell)
    run_list(fock_live, moved_entry(tfock, plan, FOCK_ROW), lambda a: ws[a], lambda b: split(zgrown[b]), True, total.at[1])
    out1 = pltpu.make_async_copy(total.at[1, pl.ds(0, per_cell)], fock, osem.at[0])
    out1.start()
    for c in gcopies:
        c.wait()
    run_list(zgt_live, moved_entry(tzgt, plan, ZGT_ROW), lambda a: us[a], lambda b: split(ggrown[b]), True, total.at[2])
    out2 = pltpu.make_async_copy(total.at[2, pl.ds(0, per_cell)], factor, osem.at[1])
    out2.start()
    out1.wait()
    out2.wait()


def join_kernel(plan, part, pa, pb, factor, total, puts, *, sides, pieces):
    per_cell = part.shape[0]
    size = per_cell // pieces
    lists = tuple(zip(sides, (pa, pb)))
    counts = [jnp.minimum(plan[MAP_ROW + side, TILE - 1], p.shape[0]) for side, p in lists]
    at = [jnp.int32(0), jnp.int32(0)]
    stored = []
    for i in range(pieces):
        piece = pl.ds(i * size, size)

        def begin(t, i=i):
            total[i * size + t] = part[i * size + t]

        each(size, begin)
        for j, (side, p) in enumerate(lists):

            def more(s, j=j, side=side, i=i):
                return jnp.logical_and(s < counts[j], plan[MAP_ROW + side, s] < (i + 1) * size)

            def add(s, side=side, p=p):
                total[plan[MAP_ROW + side, s]] += p[s]
                return s + 1

            at[j] = lax.while_loop(more, add, at[j])
        stored.append(pltpu.make_async_copy(total.at[piece], factor.at[piece], puts.at[i]))
        stored[-1].start()
    for c in stored:
        c.wait()


SMEM = pl.BlockSpec(memory_space=pltpu.SMEM)
VMEM = pl.BlockSpec(memory_space=pltpu.VMEM)
ANY = pl.BlockSpec(memory_space=pl.ANY)
HBM = pl.BlockSpec(memory_space=pltpu.HBM)
DMA = pltpu.SemaphoreType.DMA


def cost(tasks, tiles):
    return pl.CostEstimate(flops=tasks * 2 * TILE**3 * 8, bytes_accessed=tiles * TILE * TILE * 4, transcendentals=0)


def shifted(array, axis, by):
    n = lax.axis_size(axis)
    return lax.ppermute(array, axis, [(i, (i + by) % n) for i in range(n)])


def tiles(n):
    return jax.ShapeDtypeStruct((n, TILE, TILE), F32)


def cut_tiles(n):
    return jax.ShapeDtypeStruct((n, TILE, 2 * TILE), jnp.bfloat16)


def join(plan, part, pa, pb, sides):
    per_cell = part.shape[0]
    pieces = 4 if per_cell % 4 == 0 else 1
    return pl.pallas_call(
        functools.partial(join_kernel, sides=sides, pieces=pieces),
        name="join_kernel",
        out_shape=pltpu.HBM((per_cell, TILE, TILE), F32),
        in_specs=[SMEM, VMEM, VMEM, VMEM],
        out_specs=HBM,
        scratch_shapes=[pltpu.VMEM((per_cell, TILE, TILE), F32), DMA((pieces,))],
        compiler_params=pltpu.CompilerParams(vmem_limit_bytes=16 * 2**20),
        cost_estimate=cost(0, 4 * per_cell),
    )(plan, part, pa, pb)


def finish(z_room, x_room, y_room, gp3, gp4, z, f, g, tzg, tfock, tfz, tzgt, ttrans, tn, fn, zl, ga):
    per_cell = z.shape[0]
    cap = tzg.shape[2]
    grown = pltpu.VMEM((5 * per_cell, TILE, TILE), F32)
    cut = pltpu.VMEM((per_cell, TILE, 2 * TILE), jnp.bfloat16)
    params = pltpu.CompilerParams(vmem_limit_bytes=40 * 2**20)
    gy = (shifted(gp3, "gy", 1), shifted(gp4, "gy", -1))
    pack = pl.pallas_call(
        pack_kernel,
        name="pack_kernel",
        out_shape=[tiles(z_room)] * 2,
        in_specs=[VMEM] * 5,
        out_specs=[ANY] * 2,
        scratch_shapes=[
            pltpu.VMEM((8, TILE), I32),
            pltpu.VMEM((2, z_room, TILE, TILE), F32),
            pltpu.SMEM((8, TILE), I32),
            DMA,
            DMA((2,)),
        ],
        compiler_params=pltpu.CompilerParams(vmem_limit_bytes=16 * 2**20),
        cost_estimate=cost(0, 4 * per_cell),
    )
    z3, z4 = pack(fn[0], zl[0], fn[1], zl[1], z)
    g_late, z_late, z3, z4 = lax.optimization_barrier((g, z, z3, z4))
    gn = (shifted(g_late, "gx", 1), shifted(g_late, "gx", -1), ga[0], gy[0], ga[1], gy[1])
    zn = (shifted(z_late, "gx", 1), shifted(z_late, "gx", -1), shifted(z3, "gy", 1), shifted(z4, "gy", -1))
    plan, fs, ft, zs = pl.pallas_call(
        functools.partial(plan_kernel, lead=ga[0].shape[0]),
        name="plan_kernel",
        out_shape=[jax.ShapeDtypeStruct((PLAN_ROWS, TILE), I32)] + [cut_tiles(per_cell)] * 3,
        in_specs=[VMEM] * 11,
        out_specs=[VMEM] + [ANY] * 3,
        scratch_shapes=[pltpu.VMEM((8, cap), F32), pltpu.VMEM((3, per_cell, TILE, 2 * TILE), jnp.bfloat16), DMA((3,))],
        compiler_params=pltpu.CompilerParams(vmem_limit_bytes=24 * 2**20),
        cost_estimate=cost(cap, 8 * per_cell),
    )(tzg, tfock, tfz, tzgt, ttrans, *tn, f, z)
    ws = pl.pallas_call(
        w_kernel,
        name="w_kernel",
        out_shape=cut_tiles(per_cell),
        in_specs=[SMEM, SMEM, VMEM] + [ANY] * 7,
        out_specs=ANY,
        scratch_shapes=[grown, cut, pltpu.VMEM((per_cell + 1, TILE, TILE), F32), DMA((7,)), DMA],
        compiler_params=params,
        cost_estimate=cost(cap, 7 * per_cell),
    )(tzg, plan, zs, g, *gn)
    p = pl.pallas_call(
        p_kernel,
        name="p_kernel",
        out_shape=[tiles(n) for n in (per_cell, x_room, x_room, y_room, y_room)],
        in_specs=[SMEM] + [VMEM] * 2,
        out_specs=[ANY] * 5,
        scratch_shapes=[pltpu.VMEM((per_cell + 2 * x_room + 2 * y_room + 1, TILE, TILE), F32), DMA((5,))],
        compiler_params=params,
        cost_estimate=cost(2 * cap, 7 * per_cell),
    )(plan, ft, ws)
    pn = [shifted(p[k + 1], axis, -by) for k, (axis, by) in enumerate(STEPS)]
    fock_grad, part = pl.pallas_call(
        rest_kernel,
        name="rest_kernel",
        out_shape=[pltpu.HBM((per_cell, TILE, TILE), F32), tiles(per_cell)],
        in_specs=[SMEM] * 4 + [VMEM] * 5 + [ANY] * 12,
        out_specs=[HBM, ANY],
        scratch_shapes=[grown, grown, cut, pltpu.VMEM((3, per_cell + 1, TILE, TILE), F32), DMA((5,)), DMA((7,)), DMA((2,))],
        compiler_params=params,
        cost_estimate=cost(3 * cap, 14 * per_cell),
    )(tfock, tfz, tzgt, plan, fs, ws, p[0], pn[0], pn[1], z, *zn, g, *gn)
    return fock_grad, join(plan, part, pn[2], pn[3], (2, 3))


def rooms_of(per_cell, lead):
    levels = ((13, 18, 18, 12), (14, 18, 18, 13), (13, 19, 18, 14), (14, 20, 18, 15), (16, 22, 18, 17))
    scaled = [tuple(per_cell * room // 24 for room in level) for level in levels]
    return scaled + [(per_cell - lead,) + (per_cell,) * 3]


def body(z_factor, fock, cotangent, tasks_zg, tasks_fock, tasks_fz, tasks_zgt, tasks_trans):
    per_cell = z_factor.shape[2]
    nx, ny = lax.axis_size("gx"), lax.axis_size("gy")
    z, f, g = z_factor[0, 0], fock[0, 0], cotangent[0, 0]
    lists = (tasks_zg, tasks_fock, tasks_fz, tasks_zgt, tasks_trans)
    tzg, tfock, tfz, tzgt, ttrans = (t.reshape(t.shape[2], 1, t.shape[3]) for t in lists)
    a_list = jax.ShapeDtypeStruct(tzg.shape, I32)
    lead = per_cell // 3
    rooms = rooms_of(per_cell, lead)
    g_rooms = sorted({room[0] for room in rooms})
    packs = 2 * len(g_rooms)
    met = pl.pallas_call(
        functools.partial(meet_kernel, rooms=rooms, g_rooms=g_rooms, lead=lead, cuts=lead // 4),
        name="meet_kernel",
        out_shape=[tiles(lead)] * 2 + [a_list] * 8 + [tiles(room) for room in g_rooms for _ in range(2)] + [jax.ShapeDtypeStruct((1, 1), I32)],
        in_specs=[VMEM] * 5 + [ANY],
        out_specs=[ANY] * 2 + [VMEM] * 8 + [ANY] * packs + [SMEM],
        scratch_shapes=[
            pltpu.VMEM((2,) + tzg.shape, I32),
            pltpu.VMEM((2,) + tzg.shape, I32),
            pltpu.VMEM((1, TILE), I32),
            pltpu.VMEM((ny, TILE), I32),
            pltpu.VMEM((nx, ny, TILE), I32),
            pltpu.VMEM((8, TILE), I32),
            pltpu.SMEM((8, TILE), I32),
            pltpu.VMEM((per_cell - lead, TILE, TILE), F32),
            pltpu.VMEM((2, per_cell - lead, TILE, TILE), F32),
            DMA((4,)),
            DMA((4,)),
            DMA((12,)),
            DMA((12,)),
            DMA((ny,)),
            DMA((ny,)),
            DMA((nx,)),
            DMA((nx,)),
            DMA((4,)),
            DMA((packs,)),
        ],
        compiler_params=pltpu.CompilerParams(collective_id=0, has_side_effects=True),
    )(tzg, tfock, tfz, tzgt, ttrans, g)
    ga, tn, fn, zl, gp, level = met[:2], met[2:6], met[6:8], met[8:10], met[10 : 10 + packs], met[-1]

    def branch(g_room, z_room, x_room, y_room):
        at = 2 * g_rooms.index(g_room)
        return lambda gp, *rest: finish(z_room, x_room, y_room, gp[at], gp[at + 1], *rest)

    operands = (gp, z, f, g, tzg, tfock, tfz, tzgt, ttrans, tn, fn, zl, ga)
    fock_grad, factor_grad = lax.switch(level[0, 0], [branch(*room) for room in rooms], *operands)
    return fock_grad[None, None], factor_grad[None, None]


def solution(mesh):
    cells = P("gx", "gy", None, None, None)
    lists = P("gx", "gy", None, None)
    return jax.shard_map(
        body,
        mesh=mesh,
        in_specs=(cells,) * 3 + (lists,) * 5,
        out_specs=(cells, cells),
        check_vma=False,
    )
```

```python
import functools

import jax
import jax.numpy as jnp
from jax import lax
from jax.experimental import pallas as pl
from jax.experimental.pallas import tpu as pltpu
from jax.sharding import PartitionSpec as P


TILE = 128
UNROLL = 8
F32 = jnp.float32
I32 = jnp.int32
MESH = pl.DeviceIdType.MESH
STEPS = (("gx", -1), ("gx", 1), ("gy", -1), ("gy", 1))


def split(tile):
    high = tile.astype(jnp.bfloat16)
    low = (tile - high.astype(F32)).astype(jnp.bfloat16)
    return jnp.concatenate([high, low], axis=1)


def product(left, right, turned):
    if turned:
        high, low = right[:, :TILE], right[:, TILE:]
        rows = jnp.concatenate([high, low], axis=0)
        operand = jnp.concatenate([rows, rows], axis=1)
        both = lax.dot_general(left, operand, (((1,), (1,)), ((), ())), preferred_element_type=F32)
    else:
        operand = jnp.concatenate([right, right], axis=0)
        both = lax.dot_general(left, operand, (((1,), (0,)), ((), ())), preferred_element_type=F32)
    return both[:, :TILE] + both[:, TILE:]


def run_list(count, entry, left_of, right_of, turned, total, unroll=UNROLL):
    def step(turn, _):
        entries = [entry(turn * unroll + i) for i in range(unroll)]
        values = [product(left_of(a), right_of(b), turned) for _, a, b in entries]
        for (t, _, _), value in zip(entries, values):
            total[t] += value
        return 0

    lax.fori_loop(0, (count + unroll - 1) // unroll, step, 0)


def live_count(tasks, per_cell):
    length = tasks.shape[2]
    return lax.while_loop(
        lambda n: jnp.logical_and(n < length, tasks[0, 0, jnp.minimum(n, length - 1)] < per_cell),
        lambda n: n + 1,
        jnp.int32(0),
    )


def split_all(source, target, per_cell):
    def step(i, _):
        target[i] = split(source[i])
        return 0

    lax.fori_loop(0, per_cell, step, 0)


def each(count, do):
    def step(i, _):
        do(i)
        return 0

    lax.fori_loop(0, count, step, 0)


def clear(total, first, count):
    def do(i):
        total[first + i] = jnp.zeros(total.shape[1:], total.dtype)

    each(count, do)


def moved_entry(tasks, plan, at):
    return lambda e: (tasks[0, 0, e], tasks[1, 0, e], plan[at, e])


def fetch(sources, grown, sems):
    copies = [
        pltpu.make_async_copy(src, grown.at[pl.ds(at, src.shape[0])], sems.at[i]) for i, (src, at) in enumerate(sources)
    ]
    for c in copies:
        c.start()
    return copies


FOCK_ROW, FZ_ROW, MAP_ROW, ZG_ROW, ZGT_ROW, LIST_ROW, PLAN_ROWS = 0, 1, 2, 6, 7, 8, 32


class Tables:
    def __init__(self, per_cell, length):
        self.per_cell, self.length = per_cell, length
        self.row = lax.broadcasted_iota(I32, (per_cell, length), 0)
        self.lane = lax.broadcasted_iota(I32, (1, TILE), 1)
        self.number = lax.broadcasted_iota(I32, (per_cell, TILE), 0)

    def hits(self, key):
        return jnp.broadcast_to(key, self.row.shape) == self.row

    def named(self, keys, first=0):
        found = sum(self.hits(key).astype(I32) for key in keys)
        found = jnp.where(self.row >= first, found, 0)
        return jnp.minimum(jnp.max(found, axis=1, keepdims=True), 1)

    def of_cell(self, lists, k, first=0):
        return self.named([tasks[2] - k * self.per_cell for tasks in lists], first)

    def inside(self, tasks, k):
        a = tasks[1]
        here = jnp.logical_and(a >= k * self.per_cell, a < (k + 1) * self.per_cell)
        return jnp.logical_and(here, tasks[0] < self.per_cell)

    def outs(self, tasks, k):
        return jnp.where(self.inside(tasks, k), tasks[0], self.per_cell)

    def ranked(self, found):
        square = (self.per_cell, self.per_cell)
        below = (lax.broadcasted_iota(I32, square, 1) < lax.broadcasted_iota(I32, square, 0)).astype(F32)
        return jnp.dot(below, jnp.broadcast_to(found, self.number.shape).astype(F32), preferred_element_type=F32)

    def packed_rows(self, found, first=0):
        spread = jnp.broadcast_to(self.lane - first, self.number.shape).astype(F32)
        here = jnp.logical_and(self.ranked(found) == spread, jnp.broadcast_to(found, self.number.shape) == 1)
        order = jnp.sum(jnp.where(here, self.number, 0), axis=0, keepdims=True)
        return jnp.where(self.lane == TILE - 1, jnp.sum(found), order)

    def rank_of(self, key, found):
        rank = self.ranked(found)[:, : self.length].astype(I32)
        return jnp.sum(jnp.where(self.hits(key), rank, 0), axis=0, keepdims=True)

    def places(self, tasks, lists, first, starts):
        place = tasks[2]
        for k in (3, 4):
            key = tasks[2] - k * self.per_cell
            here = jnp.logical_and(key >= first, key < self.per_cell)
            rank = self.rank_of(key, self.of_cell(lists, k, first))
            place = jnp.where(here, starts[k] + rank, place)
        return place


def by_quarter(lane, values):
    result = values[3]
    for i in (2, 1, 0):
        result = jnp.where(lane < (i + 1) * (TILE // 4), values[i], result)
    return result


def meet_kernel(tzg, tfock, tfz, tzgt, ttrans, g, z, *refs, rooms, lead, cuts):
    ga, tn, gp = refs[:2], refs[2:6], refs[6:8]
    (level, pick, gl, gt, fl, zl, msg, line, lines, picked, source, packed, bulk_s, bulk_r, list_s, list_r) = refs[8:24]
    line_s, line_r, lines_s, lines_r, own, put = refs[24:]
    ny, nx = line.shape[0], lines.shape[0]
    per_cell = g.shape[0]
    ix, iy = lax.axis_index("gx"), lax.axis_index("gy")
    barrier = pltpu.get_barrier_semaphore()
    for j in range(1, nx):
        pl.semaphore_signal(barrier, inc=1, device_id=(lax.rem(ix + j, nx), iy), device_id_type=MESH)
    for j in range(1, ny):
        pl.semaphore_signal(barrier, inc=1, device_id=(ix, lax.rem(iy + j, ny)), device_id_type=MESH)
    rest_g = per_cell - lead
    loads = [
        pltpu.make_async_copy(g.at[pl.ds(lead, rest_g)], source.at[pl.ds(0, rest_g)], own.at[3]),
        pltpu.make_async_copy(z, source.at[pl.ds(rest_g, per_cell)], own.at[4]),
    ]
    for c in loads:
        c.start()
    others = []
    for axis, by in STEPS:
        others.append((lax.rem(ix + by + nx, nx), iy) if axis == "gx" else (ix, lax.rem(iy + by + ny, ny)))
    pl.semaphore_wait(barrier, nx + ny - 2)

    def bulk(i, k, start, size):
        part = pl.ds(start, size)
        return pltpu.make_async_remote_copy(
            g.at[part], ga[(k ^ 1) - 2].at[part], bulk_s.at[i], bulk_r.at[i], device_id=others[k], device_id_type=MESH
        )

    large = [bulk(0, 2, 0, cuts), bulk(1, 3, 0, cuts)]
    for c in large:
        c.start()

    lists = []
    for i in range(2):
        lists += [(tzg, gl.at[i], others[2 + i]), (tzgt, gt.at[i], others[2 + i])]
        lists += [(tfock, fl.at[i], others[2 + i]), (tfz, zl.at[i], others[2 + i])]
    lists += [(ttrans, tn[k], others[k]) for k in range(4)]
    small = []
    for i, (src, dst, to) in enumerate(lists):
        small.append(pltpu.make_async_remote_copy(src, dst, list_s.at[i], list_r.at[i], device_id=to, device_id_type=MESH))
        small[-1].start()

    tables = Tables(per_cell, tfock.shape[2])

    def most(found):
        return functools.reduce(jnp.maximum, [jnp.sum(v) for v in found])

    needs = (
        most([tables.of_cell((tzg, tzgt), k, lead) + tables.of_cell((tfock, tfz), k) for k in (3, 4)]),
        most([tables.named((tables.outs(ttrans, k),)) for k in (1, 2)]),
        most([tables.named((tables.outs(ttrans, k),)) for k in (3, 4)]),
        0,
    )
    msg[...] = by_quarter(tables.lane, needs)
    keep = pltpu.make_async_copy(msg, line.at[pl.ds(0, 1)], own.at[0])
    keep.start()
    keep.wait()
    first = []
    for j in range(1, ny):
        to = (ix, lax.rem(iy + j, ny))
        row = line.at[pl.ds(0, 1)]
        first.append(pltpu.make_async_remote_copy(row, line.at[pl.ds(j, 1)], line_s.at[j], line_r.at[j], device_id=to, device_id_type=MESH))
        first[-1].start()
    rest = [bulk(2, 2, cuts, lead - cuts), bulk(3, 3, cuts, lead - cuts)]
    for c in rest:
        c.start()
    for c in first:
        c.wait()
    keep = pltpu.make_async_copy(line, lines.at[0], own.at[1])
    keep.start()
    second = []
    for j in range(1, nx):
        to = (lax.rem(ix + j, nx), iy)
        second.append(pltpu.make_async_remote_copy(line, lines.at[j], lines_s.at[j], lines_r.at[j], device_id=to, device_id_type=MESH))
        second[-1].start()
    for c in small:
        c.wait()

    pick[...] = jnp.zeros_like(pick)
    for side in range(2):
        g_named = tables.of_cell((gl.at[side], gt.at[side]), 3 + side, lead)
        z_named = tables.of_cell((fl.at[side], zl.at[side]), 3 + side)
        count = jnp.sum(g_named)
        order = jnp.where(tables.lane < count, tables.packed_rows(g_named) - lead, tables.packed_rows(z_named, count) + rest_g)
        pick[side : side + 1, :] = jnp.clip(order, 0, rest_g + per_cell - 1)
    copy = pltpu.make_async_copy(pick, picked, own.at[2])
    copy.start()
    copy.wait()
    for c in loads:
        c.wait()
    puts = []
    for side in range(2):

        def take(s, _, side=side):
            packed[side, s] = source[picked[side, s]]
            return 0

        lax.fori_loop(0, rest_g, take, 0)
        puts.append(pltpu.make_async_copy(packed.at[side], gp[side], put.at[side]))
        puts[-1].start()
    keep.wait()
    for c in second:
        c.wait()
    found = jnp.max(lines[...], axis=0)
    lane = lax.broadcasted_iota(I32, found.shape, 1)
    needs = [jnp.max(jnp.where(by_quarter(lane, [int(i == j) for j in range(4)]) == 1, found, 0)) for i in range(4)]
    first_fit, unfit = 0, jnp.int32(1)
    for level_rooms in rooms[:-1]:
        over = [need > room for need, room in zip(needs, level_rooms)]
        unfit = unfit * functools.reduce(jnp.logical_or, over).astype(I32)
        first_fit = first_fit + unfit
    level[0, 0] = first_fit
    for c in large + rest + puts:
        c.wait()


def pack_kernel(pick, z, out3, out4, packed, put, *, first):
    per_cell, room = z.shape[0], out3.shape[0]
    puts = []
    for side, out in enumerate((out3, out4)):

        def take(s, _, side=side):
            packed[side, s] = z[jnp.clip(pick[side, first + s] - first, 0, per_cell - 1)]
            return 0

        lax.fori_loop(0, room, take, 0)
        puts.append(pltpu.make_async_copy(packed.at[side], out, put.at[side]))
        puts[-1].start()
    for c in puts:
        c.wait()


def run_start(per_cell, lead, k):
    return 3 * per_cell + (k - 3) * (2 * per_cell - lead)


def plan_kernel(tzg, tfock, tfz, tzgt, t0, t1, t2, t3, t4, f, z, plan, fs, ft, zs, table, cut, put, *, lead):
    per_cell, length = f.shape[0], tfock.shape[2]

    def cut_all(i, _):
        tile = f[i]
        cut[0, i] = split(tile)
        cut[1, i] = split(tile.T)
        cut[2, i] = split(z[i])
        return 0

    lax.fori_loop(0, per_cell, cut_all, 0)
    puts = [pltpu.make_async_copy(cut.at[i], out, put.at[i]) for i, out in enumerate((fs, ft, zs))]
    for c in puts:
        c.start()
    tables = Tables(per_cell, length)
    lane = tables.lane
    plan[...] = jnp.zeros_like(plan)
    g_starts = {k: k * per_cell + lead for k in (3, 4)}
    z_starts = {k: run_start(per_cell, lead, k) + jnp.sum(tables.of_cell((tzg, tzgt), k, lead)) for k in (3, 4)}
    for at, tasks, lists, first, starts in (
        (FOCK_ROW, tfock, (tfock, tfz), 0, z_starts),
        (FZ_ROW, tfz, (tfock, tfz), 0, z_starts),
        (ZG_ROW, tzg, (tzg, tzgt), lead, g_starts),
        (ZGT_ROW, tzgt, (tzg, tzgt), lead, g_starts),
    ):
        plan[at : at + 1, pl.ds(0, length)] = tables.places(tasks, lists, first, starts)
    for k in range(1, 5):
        plan[MAP_ROW + k - 1 : MAP_ROW + k, :] = tables.packed_rows(tables.named((tables.outs(t0, k),)))
    square = (length, length)
    before = (lax.broadcasted_iota(I32, square, 0) < lax.broadcasted_iota(I32, square, 1)).astype(F32)
    same = (lax.broadcasted_iota(I32, square, 0) == lax.broadcasted_iota(I32, square, 1)).astype(F32)
    slots = lax.broadcasted_iota(I32, (length, TILE), 1).astype(F32)
    table[...] = jnp.zeros_like(table)
    for k, tasks in enumerate((t0, t1, t2, t3, t4)):
        here, out = tables.inside(tasks, k), tables.outs(tasks, k)
        slot = out if k == 0 else tables.rank_of(out, tables.named((out,)))
        for i, value in enumerate((slot, tasks[1] - k * per_cell, tasks[2] - k * per_cell, here)):
            table[i : i + 1, :] = value.astype(F32)
        earlier = jnp.dot(table[...], before, preferred_element_type=F32)
        table[4:5, :] = earlier[3:4, :]
        turned = lax.dot_general(same, table[...], (((1,), (1,)), ((), ())), preferred_element_type=F32)
        to_slot = jnp.logical_and(jnp.broadcast_to(turned[:, 4:5], slots.shape) == slots, jnp.broadcast_to(turned[:, 3:4], slots.shape) > 0.5)
        moved = jnp.dot(table[...], to_slot.astype(F32), preferred_element_type=F32).astype(I32)
        count = jnp.sum(here.astype(I32))
        at = LIST_ROW + 4 * k
        for i in range(3):
            plan[at + i : at + i + 1, :] = moved[i : i + 1, :]
        plan[at : at + 1, :] = jnp.where(lane < count, moved[0:1, :], TILE - 1)
        plan[at + 3 : at + 4, :] = jnp.where(lane == TILE - 1, count, 0)
    for c in puts:
        c.wait()


def w_kernel(tasks, plan, zs, g0, g1, g2, a3, g3, a4, g4, ws, grown, cut, total, sems, osem):
    per_cell, lead = zs.shape[0], a3.shape[0]
    copies = fetch(g_places(per_cell, lead, g0, g1, g2, a3, g3, a4, g4), grown, sems)
    clear(total, 0, per_cell)
    live = live_count(tasks, per_cell)
    for c in copies:
        c.wait()
    entry = moved_entry(tasks, plan, ZG_ROW)
    run_list(live, entry, lambda a: zs[a], lambda b: split(grown[b]), False, total, 4)
    split_all(total, cut, per_cell)
    out = pltpu.make_async_copy(cut, ws, osem)
    out.start()
    out.wait()


def g_places(per_cell, lead, g0, g1, g2, a3, g3, a4, g4):
    places = [(src, k * per_cell) for k, src in enumerate((g0, g1, g2, a3, a4))]
    return places + [(g3, 3 * per_cell + lead), (g4, 4 * per_cell + lead)]


def p_kernel(plan, ft, ws, p0, p1, p2, p3, p4, total, osem):
    outs = (p0, p1, p2, p3, p4)
    starts = [sum(p.shape[0] for p in outs[:k]) for k in range(6)]
    last = starts[5]

    clear(total, 0, last)

    def one(k, _):
        at = LIST_ROW + 4 * k
        first = sum(jnp.where(k == i, start, 0) for i, start in enumerate(starts[:5]))

        def entry(e):
            return jnp.minimum(first + plan[at, e], last), plan[at + 1, e], plan[at + 2, e]

        run_list(plan[at + 3, TILE - 1], entry, lambda a: ft[a], lambda b: ws[b], False, total, 4)
        return 0

    lax.fori_loop(0, 5, one, 0)
    copies = [pltpu.make_async_copy(total.at[pl.ds(starts[k], p.shape[0])], p, osem.at[k]) for k, p in enumerate(outs)]
    for c in copies:
        c.start()
    for c in copies:
        c.wait()


def add_packed(plan, side, packed, total):
    at = MAP_ROW + side

    def add(s, _):
        total[plan[at, s]] += packed[s]
        return 0

    lax.fori_loop(0, jnp.minimum(plan[at, TILE - 1], packed.shape[0]), add, 0)


def rest_kernel(tfock, tfz, tzgt, plan, fs, ws, p0, p1, p2, z0, z1, z2, z3, z4, g0, g1, g2, a3, g3, a4, g4, fock, factor, zgrown, ggrown, us, total, zsem, gsem, osem):
    per_cell, lead = p0.shape[0], a3.shape[0]
    places = [(src, k * per_cell) for k, src in enumerate((z0, z1, z2))]
    for k, first, then in ((3, g3, z3), (4, g4, z4)):
        start = run_start(per_cell, lead, k)
        places += [(first, start), (then, start + first.shape[0])]
    zcopies = fetch(places, zgrown, zsem)
    gcopies = fetch(g_places(per_cell, lead, g0, g1, g2, a3, g3, a4, g4), ggrown, gsem)
    clear(total.at[0], 0, per_cell)
    clear(total.at[1], 0, per_cell)

    def begin(i):
        total[2, i] = p0[i]

    each(per_cell, begin)
    add_packed(plan, 0, p1, total.at[2])
    add_packed(plan, 1, p2, total.at[2])
    fz_live, fock_live, zgt_live = (live_count(tasks, per_cell) for tasks in (tfz, tfock, tzgt))
    for c in zcopies:
        c.wait()
    run_list(fz_live, moved_entry(tfz, plan, FZ_ROW), lambda a: fs[a], lambda b: split(zgrown[b]), False, total.at[0])
    split_all(total.at[0], us, per_cell)
    run_list(fock_live, moved_entry(tfock, plan, FOCK_ROW), lambda a: ws[a], lambda b: split(zgrown[b]), True, total.at[1])
    out1 = pltpu.make_async_copy(total.at[1, pl.ds(0, per_cell)], fock, osem.at[0])
    out1.start()
    for c in gcopies:
        c.wait()
    run_list(zgt_live, moved_entry(tzgt, plan, ZGT_ROW), lambda a: us[a], lambda b: split(ggrown[b]), True, total.at[2])
    out2 = pltpu.make_async_copy(total.at[2, pl.ds(0, per_cell)], factor, osem.at[1])
    out2.start()
    out1.wait()
    out2.wait()


def join_kernel(plan, part, pa, pb, factor, total, puts, *, sides, pieces):
    per_cell = part.shape[0]
    size = per_cell // pieces
    lists = tuple(zip(sides, (pa, pb)))
    counts = [jnp.minimum(plan[MAP_ROW + side, TILE - 1], p.shape[0]) for side, p in lists]
    at = [jnp.int32(0), jnp.int32(0)]
    stored = []
    for i in range(pieces):
        piece = pl.ds(i * size, size)

        def begin(t, i=i):
            total[i * size + t] = part[i * size + t]

        each(size, begin)
        for j, (side, p) in enumerate(lists):

            def more(s, j=j, side=side, i=i):
                return jnp.logical_and(s < counts[j], plan[MAP_ROW + side, s] < (i + 1) * size)

            def add(s, side=side, p=p):
                total[plan[MAP_ROW + side, s]] += p[s]
                return s + 1

            at[j] = lax.while_loop(more, add, at[j])
        stored.append(pltpu.make_async_copy(total.at[piece], factor.at[piece], puts.at[i]))
        stored[-1].start()
    for c in stored:
        c.wait()


SMEM = pl.BlockSpec(memory_space=pltpu.SMEM)
VMEM = pl.BlockSpec(memory_space=pltpu.VMEM)
ANY = pl.BlockSpec(memory_space=pl.ANY)
HBM = pl.BlockSpec(memory_space=pltpu.HBM)
DMA = pltpu.SemaphoreType.DMA


def cost(tasks, tiles):
    return pl.CostEstimate(flops=tasks * 2 * TILE**3 * 8, bytes_accessed=tiles * TILE * TILE * 4, transcendentals=0)


def shifted(array, axis, by):
    n = lax.axis_size(axis)
    return lax.ppermute(array, axis, [(i, (i + by) % n) for i in range(n)])


def tiles(n):
    return jax.ShapeDtypeStruct((n, TILE, TILE), F32)


def cut_tiles(n):
    return jax.ShapeDtypeStruct((n, TILE, 2 * TILE), jnp.bfloat16)


def join(plan, part, pa, pb, sides):
    per_cell = part.shape[0]
    pieces = 4 if per_cell % 4 == 0 else 1
    return pl.pallas_call(
        functools.partial(join_kernel, sides=sides, pieces=pieces),
        name="join_kernel",
        out_shape=pltpu.HBM((per_cell, TILE, TILE), F32),
        in_specs=[SMEM, VMEM, VMEM, VMEM],
        out_specs=HBM,
        scratch_shapes=[pltpu.VMEM((per_cell, TILE, TILE), F32), DMA((pieces,))],
        compiler_params=pltpu.CompilerParams(vmem_limit_bytes=16 * 2**20),
        cost_estimate=cost(0, 4 * per_cell),
    )(plan, part, pa, pb)


def finish(run_room, x_room, y_room, gp, z, f, g, tzg, tfock, tfz, tzgt, ttrans, tn, pick, ga):
    per_cell = z.shape[0]
    cap = tzg.shape[2]
    grown = pltpu.VMEM((5 * per_cell, TILE, TILE), F32)
    cut = pltpu.VMEM((per_cell, TILE, 2 * TILE), jnp.bfloat16)
    params = pltpu.CompilerParams(vmem_limit_bytes=40 * 2**20)
    gy = (shifted(gp[0], "gy", 1), shifted(gp[1], "gy", -1))
    first = gp[0].shape[0]
    z_room = run_room - first
    pack = pl.pallas_call(
        functools.partial(pack_kernel, first=first),
        name="pack_kernel",
        out_shape=[tiles(z_room)] * 2,
        in_specs=[SMEM, VMEM],
        out_specs=[ANY] * 2,
        scratch_shapes=[pltpu.VMEM((2, z_room, TILE, TILE), F32), DMA((2,))],
        compiler_params=pltpu.CompilerParams(vmem_limit_bytes=16 * 2**20),
        cost_estimate=cost(0, 4 * per_cell),
    )
    z3, z4 = pack(pick, z)
    g_late, z_late, z3, z4 = lax.optimization_barrier((g, z, z3, z4))
    gn = (shifted(g_late, "gx", 1), shifted(g_late, "gx", -1), ga[0], gy[0], ga[1], gy[1])
    zn = (shifted(z_late, "gx", 1), shifted(z_late, "gx", -1), shifted(z3, "gy", 1), shifted(z4, "gy", -1))
    plan, fs, ft, zs = pl.pallas_call(
        functools.partial(plan_kernel, lead=ga[0].shape[0]),
        name="plan_kernel",
        out_shape=[jax.ShapeDtypeStruct((PLAN_ROWS, TILE), I32)] + [cut_tiles(per_cell)] * 3,
        in_specs=[VMEM] * 11,
        out_specs=[VMEM] + [ANY] * 3,
        scratch_shapes=[pltpu.VMEM((8, cap), F32), pltpu.VMEM((3, per_cell, TILE, 2 * TILE), jnp.bfloat16), DMA((3,))],
        compiler_params=pltpu.CompilerParams(vmem_limit_bytes=24 * 2**20),
        cost_estimate=cost(cap, 8 * per_cell),
    )(tzg, tfock, tfz, tzgt, ttrans, *tn, f, z)
    ws = pl.pallas_call(
        w_kernel,
        name="w_kernel",
        out_shape=cut_tiles(per_cell),
        in_specs=[SMEM, SMEM, VMEM] + [ANY] * 7,
        out_specs=ANY,
        scratch_shapes=[grown, cut, pltpu.VMEM((per_cell + 1, TILE, TILE), F32), DMA((7,)), DMA],
        compiler_params=params,
        cost_estimate=cost(cap, 7 * per_cell),
    )(tzg, plan, zs, g, *gn)
    p = pl.pallas_call(
        p_kernel,
        name="p_kernel",
        out_shape=[tiles(n) for n in (per_cell, x_room, x_room, y_room, y_room)],
        in_specs=[SMEM] + [VMEM] * 2,
        out_specs=[ANY] * 5,
        scratch_shapes=[pltpu.VMEM((per_cell + 2 * x_room + 2 * y_room + 1, TILE, TILE), F32), DMA((5,))],
        compiler_params=params,
        cost_estimate=cost(2 * cap, 7 * per_cell),
    )(plan, ft, ws)
    pn = [shifted(p[k + 1], axis, -by) for k, (axis, by) in enumerate(STEPS)]
    fock_grad, part = pl.pallas_call(
        rest_kernel,
        name="rest_kernel",
        out_shape=[pltpu.HBM((per_cell, TILE, TILE), F32), tiles(per_cell)],
        in_specs=[SMEM] * 4 + [VMEM] * 5 + [ANY] * 12,
        out_specs=[HBM, ANY],
        scratch_shapes=[
            pltpu.VMEM((run_start(per_cell, ga[0].shape[0], 5), TILE, TILE), F32),
            grown,
            cut,
            pltpu.VMEM((3, per_cell + 1, TILE, TILE), F32),
            DMA((7,)),
            DMA((7,)),
            DMA((2,)),
        ],
        compiler_params=params,
        cost_estimate=cost(3 * cap, 14 * per_cell),
    )(tfock, tfz, tzgt, plan, fs, ws, p[0], pn[0], pn[1], z, *zn, g, *gn)
    return fock_grad, join(plan, part, pn[2], pn[3], (2, 3))


def rooms_of(per_cell, lead):
    levels = ((29, 18, 12), (29, 18, 14), (30, 18, 13), (31, 18, 15), (34, 18, 17))
    scaled = [tuple(per_cell * room // 24 for room in level) for level in levels]
    return scaled + [(2 * per_cell - lead, per_cell, per_cell)]


def body(z_factor, fock, cotangent, tasks_zg, tasks_fock, tasks_fz, tasks_zgt, tasks_trans):
    per_cell = z_factor.shape[2]
    nx, ny = lax.axis_size("gx"), lax.axis_size("gy")
    z, f, g = z_factor[0, 0], fock[0, 0], cotangent[0, 0]
    lists = (tasks_zg, tasks_fock, tasks_fz, tasks_zgt, tasks_trans)
    tzg, tfock, tfz, tzgt, ttrans = (t.reshape(t.shape[2], 1, t.shape[3]) for t in lists)
    a_list = jax.ShapeDtypeStruct(tzg.shape, I32)
    lead = per_cell // 3
    rooms = rooms_of(per_cell, lead)
    met = pl.pallas_call(
        functools.partial(meet_kernel, rooms=rooms, lead=lead, cuts=lead // 4),
        name="meet_kernel",
        out_shape=[tiles(lead)] * 2
        + [a_list] * 4
        + [tiles(per_cell - lead)] * 2
        + [jax.ShapeDtypeStruct((1, 1), I32), jax.ShapeDtypeStruct((8, TILE), I32)],
        in_specs=[VMEM] * 5 + [ANY] * 2,
        out_specs=[ANY] * 2 + [VMEM] * 4 + [ANY] * 2 + [SMEM, VMEM],
        scratch_shapes=[pltpu.VMEM((2,) + tzg.shape, I32)] * 4
        + [
            pltpu.VMEM((1, TILE), I32),
            pltpu.VMEM((ny, TILE), I32),
            pltpu.VMEM((nx, ny, TILE), I32),
            pltpu.SMEM((8, TILE), I32),
            pltpu.VMEM((2 * per_cell - lead, TILE, TILE), F32),
            pltpu.VMEM((2, per_cell - lead, TILE, TILE), F32),
            DMA((4,)),
            DMA((4,)),
            DMA((12,)),
            DMA((12,)),
            DMA((ny,)),
            DMA((ny,)),
            DMA((nx,)),
            DMA((nx,)),
            DMA((5,)),
            DMA((2,)),
        ],
        compiler_params=pltpu.CompilerParams(collective_id=0, has_side_effects=True),
    )(tzg, tfock, tfz, tzgt, ttrans, g, z)
    ga, tn, gp, level, pick = met[:2], met[2:6], met[6:8], met[8], met[9]
    operands = (gp, z, f, g, tzg, tfock, tfz, tzgt, ttrans, tn, pick, ga)
    fock_grad, factor_grad = lax.switch(level[0, 0], [functools.partial(finish, *room) for room in rooms], *operands)
    return fock_grad[None, None], factor_grad[None, None]


def solution(mesh):
    cells = P("gx", "gy", None, None, None)
    lists = P("gx", "gy", None, None)
    return jax.shard_map(
        body,
        mesh=mesh,
        in_specs=(cells,) * 3 + (lists,) * 5,
        out_specs=(cells, cells),
        check_vma=False,
    )
```

```python
import functools

import jax
import jax.numpy as jnp
from jax import lax
from jax.experimental import pallas as pl
from jax.experimental.pallas import tpu as pltpu
from jax.sharding import PartitionSpec as P


TILE = 128
UNROLL = 8
F32 = jnp.float32
I32 = jnp.int32
MESH = pl.DeviceIdType.MESH
STEPS = (("gx", -1), ("gx", 1), ("gy", -1), ("gy", 1))


def split(tile):
    high = tile.astype(jnp.bfloat16)
    low = (tile - high.astype(F32)).astype(jnp.bfloat16)
    return jnp.concatenate([high, low], axis=1)


def product(left, right, turned):
    if turned:
        high, low = right[:, :TILE], right[:, TILE:]
        rows = jnp.concatenate([high, low], axis=0)
        operand = jnp.concatenate([rows, rows], axis=1)
        both = lax.dot_general(left, operand, (((1,), (1,)), ((), ())), preferred_element_type=F32)
    else:
        operand = jnp.concatenate([right, right], axis=0)
        both = lax.dot_general(left, operand, (((1,), (0,)), ((), ())), preferred_element_type=F32)
    return both[:, :TILE] + both[:, TILE:]


def run_list(count, entry, left_of, right_of, turned, total, unroll=UNROLL):
    def step(turn, _):
        entries = [entry(turn * unroll + i) for i in range(unroll)]
        values = [product(left_of(a), right_of(b), turned) for _, a, b in entries]
        for (t, _, _), value in zip(entries, values):
            total[t] += value
        return 0

    lax.fori_loop(0, (count + unroll - 1) // unroll, step, 0)


def live_count(tasks, per_cell):
    length = tasks.shape[2]
    return lax.while_loop(
        lambda n: jnp.logical_and(n < length, tasks[0, 0, jnp.minimum(n, length - 1)] < per_cell),
        lambda n: n + 1,
        jnp.int32(0),
    )


def split_all(source, target, per_cell):
    def step(i, _):
        target[i] = split(source[i])
        return 0

    lax.fori_loop(0, per_cell, step, 0)


def each(count, do):
    def step(i, _):
        do(i)
        return 0

    lax.fori_loop(0, count, step, 0)


def clear(total, first, count):
    def do(i):
        total[first + i] = jnp.zeros(total.shape[1:], total.dtype)

    each(count, do)


def moved_entry(tasks, plan, at):
    return lambda e: (tasks[0, 0, e], tasks[1, 0, e], plan[at, e])


def fetch(sources, grown, sems):
    copies = [
        pltpu.make_async_copy(src, grown.at[pl.ds(at, src.shape[0])], sems.at[i]) for i, (src, at) in enumerate(sources)
    ]
    for c in copies:
        c.start()
    return copies


FOCK_ROW, FZ_ROW, MAP_ROW, ZG_ROW, ZGT_ROW, LIST_ROW, PLAN_ROWS = 0, 1, 2, 6, 7, 8, 32


class Tables:
    def __init__(self, per_cell, length):
        self.per_cell, self.length = per_cell, length
        self.row = lax.broadcasted_iota(I32, (per_cell, length), 0)
        self.lane = lax.broadcasted_iota(I32, (1, TILE), 1)
        self.number = lax.broadcasted_iota(I32, (per_cell, TILE), 0)

    def hits(self, key):
        return jnp.broadcast_to(key, self.row.shape) == self.row

    def named(self, keys, first=0):
        found = sum(self.hits(key).astype(I32) for key in keys)
        found = jnp.where(self.row >= first, found, 0)
        return jnp.minimum(jnp.max(found, axis=1, keepdims=True), 1)

    def of_cell(self, lists, k, first=0):
        return self.named([tasks[2] - k * self.per_cell for tasks in lists], first)

    def inside(self, tasks, k):
        a = tasks[1]
        here = jnp.logical_and(a >= k * self.per_cell, a < (k + 1) * self.per_cell)
        return jnp.logical_and(here, tasks[0] < self.per_cell)

    def outs(self, tasks, k):
        return jnp.where(self.inside(tasks, k), tasks[0], self.per_cell)

    def ranked(self, found):
        square = (self.per_cell, self.per_cell)
        below = (lax.broadcasted_iota(I32, square, 1) < lax.broadcasted_iota(I32, square, 0)).astype(F32)
        return jnp.dot(below, jnp.broadcast_to(found, self.number.shape).astype(F32), preferred_element_type=F32)

    def packed_rows(self, found, first=0):
        spread = jnp.broadcast_to(self.lane - first, self.number.shape).astype(F32)
        here = jnp.logical_and(self.ranked(found) == spread, jnp.broadcast_to(found, self.number.shape) == 1)
        order = jnp.sum(jnp.where(here, self.number, 0), axis=0, keepdims=True)
        return jnp.where(self.lane == TILE - 1, jnp.sum(found), order)

    def rank_of(self, key, found):
        rank = self.ranked(found)[:, : self.length].astype(I32)
        return jnp.sum(jnp.where(self.hits(key), rank, 0), axis=0, keepdims=True)

    def places(self, tasks, lists, first, starts):
        place = tasks[2]
        for k in (3, 4):
            key = tasks[2] - k * self.per_cell
            here = jnp.logical_and(key >= first, key < self.per_cell)
            rank = self.rank_of(key, self.of_cell(lists, k, first))
            place = jnp.where(here, starts[k] + rank, place)
        return place


def by_quarter(lane, values):
    result = values[3]
    for i in (2, 1, 0):
        result = jnp.where(lane < (i + 1) * (TILE // 4), values[i], result)
    return result


def meet_kernel(tzg, tfock, tfz, tzgt, ttrans, g, z, *refs, rooms, lead, cuts):
    ga, tn, gp = refs[:2], refs[2:6], refs[6:8]
    (level, pick, gl, gt, fl, zl, msg, line, lines, picked, source, packed, bulk_s, bulk_r, list_s, list_r) = refs[8:24]
    line_s, line_r, lines_s, lines_r, own, put = refs[24:]
    ny, nx = line.shape[0], lines.shape[0]
    per_cell = g.shape[0]
    ix, iy = lax.axis_index("gx"), lax.axis_index("gy")
    barrier = pltpu.get_barrier_semaphore()
    for j in range(1, nx):
        pl.semaphore_signal(barrier, inc=1, device_id=(lax.rem(ix + j, nx), iy), device_id_type=MESH)
    for j in range(1, ny):
        pl.semaphore_signal(barrier, inc=1, device_id=(ix, lax.rem(iy + j, ny)), device_id_type=MESH)
    rest_g = per_cell - lead
    loads = [
        pltpu.make_async_copy(g.at[pl.ds(lead, rest_g)], source.at[pl.ds(0, rest_g)], own.at[3]),
        pltpu.make_async_copy(z, source.at[pl.ds(rest_g, per_cell)], own.at[4]),
    ]
    for c in loads:
        c.start()
    others = []
    for axis, by in STEPS:
        others.append((lax.rem(ix + by + nx, nx), iy) if axis == "gx" else (ix, lax.rem(iy + by + ny, ny)))
    pl.semaphore_wait(barrier, nx + ny - 2)

    def bulk(i, k, start, size):
        part = pl.ds(start, size)
        return pltpu.make_async_remote_copy(
            g.at[part], ga[(k ^ 1) - 2].at[part], bulk_s.at[i], bulk_r.at[i], device_id=others[k], device_id_type=MESH
        )

    large = [bulk(0, 2, 0, cuts), bulk(1, 3, 0, cuts)]
    for c in large:
        c.start()

    lists = []
    for i in range(2):
        lists += [(tzg, gl.at[i], others[2 + i]), (tzgt, gt.at[i], others[2 + i])]
        lists += [(tfock, fl.at[i], others[2 + i]), (tfz, zl.at[i], others[2 + i])]
    lists += [(ttrans, tn[k], others[k]) for k in range(4)]
    small = []
    for i, (src, dst, to) in enumerate(lists):
        small.append(pltpu.make_async_remote_copy(src, dst, list_s.at[i], list_r.at[i], device_id=to, device_id_type=MESH))
        small[-1].start()

    tables = Tables(per_cell, tfock.shape[2])

    def most(found):
        return functools.reduce(jnp.maximum, [jnp.sum(v) for v in found])

    needs = (
        most([tables.of_cell((tzg, tzgt), k, lead) + tables.of_cell((tfock, tfz), k) for k in (3, 4)]),
        most([tables.named((tables.outs(ttrans, k),)) for k in (1, 2)]),
        most([tables.named((tables.outs(ttrans, k),)) for k in (3, 4)]),
        0,
    )
    msg[...] = by_quarter(tables.lane, needs)
    keep = pltpu.make_async_copy(msg, line.at[pl.ds(0, 1)], own.at[0])
    keep.start()
    keep.wait()
    first = []
    for j in range(1, ny):
        to = (ix, lax.rem(iy + j, ny))
        row = line.at[pl.ds(0, 1)]
        first.append(pltpu.make_async_remote_copy(row, line.at[pl.ds(j, 1)], line_s.at[j], line_r.at[j], device_id=to, device_id_type=MESH))
        first[-1].start()
    rest = [bulk(2, 2, cuts, lead - cuts), bulk(3, 3, cuts, lead - cuts)]
    for c in rest:
        c.start()
    for c in first:
        c.wait()
    keep = pltpu.make_async_copy(line, lines.at[0], own.at[1])
    keep.start()
    second = []
    for j in range(1, nx):
        to = (lax.rem(ix + j, nx), iy)
        second.append(pltpu.make_async_remote_copy(line, lines.at[j], lines_s.at[j], lines_r.at[j], device_id=to, device_id_type=MESH))
        second[-1].start()
    for c in small:
        c.wait()

    pick[...] = jnp.zeros_like(pick)
    for side in range(2):
        g_named = tables.of_cell((gl.at[side], gt.at[side]), 3 + side, lead)
        z_named = tables.of_cell((fl.at[side], zl.at[side]), 3 + side)
        count = jnp.sum(g_named)
        order = jnp.where(tables.lane < count, tables.packed_rows(g_named) - lead, tables.packed_rows(z_named, count) + rest_g)
        pick[side : side + 1, :] = jnp.clip(order, 0, rest_g + per_cell - 1)
    copy = pltpu.make_async_copy(pick, picked, own.at[2])
    copy.start()
    copy.wait()
    for c in loads:
        c.wait()
    puts = []
    for side in range(2):

        def take(s, _, side=side):
            packed[side, s] = source[picked[side, s]]
            return 0

        lax.fori_loop(0, rest_g, take, 0)
        puts.append(pltpu.make_async_copy(packed.at[side], gp[side], put.at[side]))
        puts[-1].start()
    keep.wait()
    for c in second:
        c.wait()
    found = jnp.max(lines[...], axis=0)
    lane = lax.broadcasted_iota(I32, found.shape, 1)
    needs = [jnp.max(jnp.where(by_quarter(lane, [int(i == j) for j in range(4)]) == 1, found, 0)) for i in range(4)]
    first_fit, unfit = 0, jnp.int32(1)
    for level_rooms in rooms[:-1]:
        over = [need > room for need, room in zip(needs, level_rooms)]
        unfit = unfit * functools.reduce(jnp.logical_or, over).astype(I32)
        first_fit = first_fit + unfit
    level[0, 0] = first_fit
    for c in large + rest + puts:
        c.wait()


def pack_kernel(pick, z, out3, out4, packed, put, *, first):
    per_cell, room = z.shape[0], out3.shape[0]
    puts = []
    for side, out in enumerate((out3, out4)):

        def take(s, _, side=side):
            packed[side, s] = z[jnp.clip(pick[side, first + s] - first, 0, per_cell - 1)]
            return 0

        lax.fori_loop(0, room, take, 0)
        puts.append(pltpu.make_async_copy(packed.at[side], out, put.at[side]))
        puts[-1].start()
    for c in puts:
        c.wait()


def run_start(per_cell, lead, k):
    return 3 * per_cell + (k - 3) * (2 * per_cell - lead)


def plan_kernel(tzg, tfock, tfz, tzgt, t0, t1, t2, t3, t4, f, z, plan, fs, ft, zs, table, cut, put, *, lead):
    per_cell, length = f.shape[0], tfock.shape[2]

    def cut_all(i, _):
        tile = f[i]
        cut[0, i] = split(tile)
        cut[1, i] = split(tile.T)
        cut[2, i] = split(z[i])
        return 0

    lax.fori_loop(0, per_cell, cut_all, 0)
    puts = [pltpu.make_async_copy(cut.at[i], out, put.at[i]) for i, out in enumerate((fs, ft, zs))]
    for c in puts:
        c.start()
    tables = Tables(per_cell, length)
    lane = tables.lane
    plan[...] = jnp.zeros_like(plan)
    g_starts = {k: k * per_cell + lead for k in (3, 4)}
    z_starts = {k: run_start(per_cell, lead, k) + jnp.sum(tables.of_cell((tzg, tzgt), k, lead)) for k in (3, 4)}
    for at, tasks, lists, first, starts in (
        (FOCK_ROW, tfock, (tfock, tfz), 0, z_starts),
        (FZ_ROW, tfz, (tfock, tfz), 0, z_starts),
        (ZG_ROW, tzg, (tzg, tzgt), lead, g_starts),
        (ZGT_ROW, tzgt, (tzg, tzgt), lead, g_starts),
    ):
        plan[at : at + 1, pl.ds(0, length)] = tables.places(tasks, lists, first, starts)
    for k in range(1, 5):
        plan[MAP_ROW + k - 1 : MAP_ROW + k, :] = tables.packed_rows(tables.named((tables.outs(t0, k),)))
    square = (length, length)
    before = (lax.broadcasted_iota(I32, square, 0) < lax.broadcasted_iota(I32, square, 1)).astype(F32)
    same = (lax.broadcasted_iota(I32, square, 0) == lax.broadcasted_iota(I32, square, 1)).astype(F32)
    slots = lax.broadcasted_iota(I32, (length, TILE), 1).astype(F32)
    table[...] = jnp.zeros_like(table)
    for k, tasks in enumerate((t0, t1, t2, t3, t4)):
        here, out = tables.inside(tasks, k), tables.outs(tasks, k)
        slot = out if k == 0 else tables.rank_of(out, tables.named((out,)))
        for i, value in enumerate((slot, tasks[1] - k * per_cell, tasks[2] - k * per_cell, here)):
            table[i : i + 1, :] = value.astype(F32)
        earlier = jnp.dot(table[...], before, preferred_element_type=F32)
        table[4:5, :] = earlier[3:4, :]
        turned = lax.dot_general(same, table[...], (((1,), (1,)), ((), ())), preferred_element_type=F32)
        to_slot = jnp.logical_and(jnp.broadcast_to(turned[:, 4:5], slots.shape) == slots, jnp.broadcast_to(turned[:, 3:4], slots.shape) > 0.5)
        moved = jnp.dot(table[...], to_slot.astype(F32), preferred_element_type=F32).astype(I32)
        count = jnp.sum(here.astype(I32))
        at = LIST_ROW + 4 * k
        for i in range(3):
            plan[at + i : at + i + 1, :] = moved[i : i + 1, :]
        plan[at : at + 1, :] = jnp.where(lane < count, moved[0:1, :], TILE - 1)
        plan[at + 3 : at + 4, :] = jnp.where(lane == TILE - 1, count, 0)
    for c in puts:
        c.wait()


def w_kernel(tasks, plan, zs, g0, g1, g2, a3, g3, a4, g4, ws, grown, cut, total, sems, osem):
    per_cell, lead = zs.shape[0], a3.shape[0]
    copies = fetch(g_places(per_cell, lead, g0, g1, g2, a3, g3, a4, g4), grown, sems)
    clear(total, 0, per_cell)
    live = live_count(tasks, per_cell)
    for c in copies:
        c.wait()
    entry = moved_entry(tasks, plan, ZG_ROW)
    run_list(live, entry, lambda a: zs[a], lambda b: split(grown[b]), False, total, 4)
    split_all(total, cut, per_cell)
    out = pltpu.make_async_copy(cut, ws, osem)
    out.start()
    out.wait()


def g_places(per_cell, lead, g0, g1, g2, a3, g3, a4, g4):
    places = [(src, k * per_cell) for k, src in enumerate((g0, g1, g2, a3, a4))]
    return places + [(g3, 3 * per_cell + lead), (g4, 4 * per_cell + lead)]


def p_kernel(plan, ft, ws, p0, p1, p2, p3, p4, total, osem):
    outs = (p0, p1, p2, p3, p4)
    starts = [sum(p.shape[0] for p in outs[:k]) for k in range(6)]
    last = starts[5]

    clear(total, 0, last)

    def one(k, _):
        at = LIST_ROW + 4 * k
        first = sum(jnp.where(k == i, start, 0) for i, start in enumerate(starts[:5]))

        def entry(e):
            return jnp.minimum(first + plan[at, e], last), plan[at + 1, e], plan[at + 2, e]

        run_list(plan[at + 3, TILE - 1], entry, lambda a: ft[a], lambda b: ws[b], False, total, 4)
        return 0

    lax.fori_loop(0, 5, one, 0)
    copies = [pltpu.make_async_copy(total.at[pl.ds(starts[k], p.shape[0])], p, osem.at[k]) for k, p in enumerate(outs)]
    for c in copies:
        c.start()
    for c in copies:
        c.wait()


def add_packed(plan, side, packed, total):
    at = MAP_ROW + side

    def add(s, _):
        total[plan[at, s]] += packed[s]
        return 0

    lax.fori_loop(0, jnp.minimum(plan[at, TILE - 1], packed.shape[0]), add, 0)


def rest_kernel(tfock, tfz, tzgt, plan, fs, ws, p0, p1, p2, z0, z1, z2, z3, z4, g0, g1, g2, a3, g3, a4, g4, fock, factor, zgrown, ggrown, us, total, zsem, gsem, osem):
    per_cell, lead = p0.shape[0], a3.shape[0]
    places = [(src, k * per_cell) for k, src in enumerate((z0, z1, z2))]
    for k, first, then in ((3, g3, z3), (4, g4, z4)):
        start = run_start(per_cell, lead, k)
        places += [(first, start), (then, start + first.shape[0])]
    zcopies = fetch(places, zgrown, zsem)
    gcopies = fetch(g_places(per_cell, lead, g0, g1, g2, a3, g3, a4, g4), ggrown, gsem)
    clear(total.at[0], 0, per_cell)
    clear(total.at[1], 0, per_cell)

    def begin(i):
        total[2, i] = p0[i]

    each(per_cell, begin)
    add_packed(plan, 0, p1, total.at[2])
    add_packed(plan, 1, p2, total.at[2])
    fz_live, fock_live, zgt_live = (live_count(tasks, per_cell) for tasks in (tfz, tfock, tzgt))
    for c in zcopies:
        c.wait()
    run_list(fz_live, moved_entry(tfz, plan, FZ_ROW), lambda a: fs[a], lambda b: split(zgrown[b]), False, total.at[0])
    split_all(total.at[0], us, per_cell)
    run_list(fock_live, moved_entry(tfock, plan, FOCK_ROW), lambda a: ws[a], lambda b: split(zgrown[b]), True, total.at[1])
    out1 = pltpu.make_async_copy(total.at[1, pl.ds(0, per_cell)], fock, osem.at[0])
    out1.start()
    for c in gcopies:
        c.wait()
    run_list(zgt_live, moved_entry(tzgt, plan, ZGT_ROW), lambda a: us[a], lambda b: split(ggrown[b]), True, total.at[2])
    out2 = pltpu.make_async_copy(total.at[2, pl.ds(0, per_cell)], factor, osem.at[1])
    out2.start()
    out1.wait()
    out2.wait()


def join_kernel(plan, part, pa, pb, factor, total, puts, *, sides, pieces):
    per_cell = part.shape[0]
    size = per_cell // pieces
    lists = tuple(zip(sides, (pa, pb)))
    counts = [jnp.minimum(plan[MAP_ROW + side, TILE - 1], p.shape[0]) for side, p in lists]
    at = [jnp.int32(0), jnp.int32(0)]
    stored = []
    for i in range(pieces):
        piece = pl.ds(i * size, size)

        def begin(t, i=i):
            total[i * size + t] = part[i * size + t]

        each(size, begin)
        for j, (side, p) in enumerate(lists):

            def more(s, j=j, side=side, i=i):
                return jnp.logical_and(s < counts[j], plan[MAP_ROW + side, s] < (i + 1) * size)

            def add(s, side=side, p=p):
                total[plan[MAP_ROW + side, s]] += p[s]
                return s + 1

            at[j] = lax.while_loop(more, add, at[j])
        stored.append(pltpu.make_async_copy(total.at[piece], factor.at[piece], puts.at[i]))
        stored[-1].start()
    for c in stored:
        c.wait()


SMEM = pl.BlockSpec(memory_space=pltpu.SMEM)
VMEM = pl.BlockSpec(memory_space=pltpu.VMEM)
ANY = pl.BlockSpec(memory_space=pl.ANY)
HBM = pl.BlockSpec(memory_space=pltpu.HBM)
DMA = pltpu.SemaphoreType.DMA


def cost(tasks, tiles):
    return pl.CostEstimate(flops=tasks * 2 * TILE**3 * 8, bytes_accessed=tiles * TILE * TILE * 4, transcendentals=0)


def shifted(array, axis, by):
    n = lax.axis_size(axis)
    return lax.ppermute(array, axis, [(i, (i + by) % n) for i in range(n)])


def tiles(n):
    return jax.ShapeDtypeStruct((n, TILE, TILE), F32)


def cut_tiles(n):
    return jax.ShapeDtypeStruct((n, TILE, 2 * TILE), jnp.bfloat16)


def join(plan, part, pa, pb, sides):
    per_cell = part.shape[0]
    pieces = 4 if per_cell % 4 == 0 else 1
    return pl.pallas_call(
        functools.partial(join_kernel, sides=sides, pieces=pieces),
        name="join_kernel",
        out_shape=pltpu.HBM((per_cell, TILE, TILE), F32),
        in_specs=[SMEM, VMEM, VMEM, VMEM],
        out_specs=HBM,
        scratch_shapes=[pltpu.VMEM((per_cell, TILE, TILE), F32), DMA((pieces,))],
        compiler_params=pltpu.CompilerParams(vmem_limit_bytes=16 * 2**20),
        cost_estimate=cost(0, 4 * per_cell),
    )(plan, part, pa, pb)


def finish(run_room, x_room, y_room, gp, z, f, g, tzg, tfock, tfz, tzgt, ttrans, tn, pick, ga):
    per_cell = z.shape[0]
    cap = tzg.shape[2]
    grown = pltpu.VMEM((5 * per_cell, TILE, TILE), F32)
    cut = pltpu.VMEM((per_cell, TILE, 2 * TILE), jnp.bfloat16)
    params = pltpu.CompilerParams(vmem_limit_bytes=40 * 2**20)
    gy = (shifted(gp[0], "gy", 1), shifted(gp[1], "gy", -1))
    first = gp[0].shape[0]
    z_room = run_room - first
    pack = pl.pallas_call(
        functools.partial(pack_kernel, first=first),
        name="pack_kernel",
        out_shape=[tiles(z_room)] * 2,
        in_specs=[SMEM, VMEM],
        out_specs=[ANY] * 2,
        scratch_shapes=[pltpu.VMEM((2, z_room, TILE, TILE), F32), DMA((2,))],
        compiler_params=pltpu.CompilerParams(vmem_limit_bytes=16 * 2**20),
        cost_estimate=cost(0, 4 * per_cell),
    )
    z3, z4 = pack(pick, z)
    g_late, z_late, z3, z4 = lax.optimization_barrier((g, z, z3, z4))
    gn = (shifted(g_late, "gx", 1), shifted(g_late, "gx", -1), ga[0], gy[0], ga[1], gy[1])
    zy = (shifted(z3, "gy", 1), shifted(z4, "gy", -1))
    zn = (shifted(z_late, "gx", 1), shifted(z_late, "gx", -1)) + zy
    make_plan = pl.pallas_call(
        functools.partial(plan_kernel, lead=ga[0].shape[0]),
        name="plan_kernel",
        out_shape=[jax.ShapeDtypeStruct((PLAN_ROWS, TILE), I32)] + [cut_tiles(per_cell)] * 3,
        in_specs=[VMEM] * 11,
        out_specs=[VMEM] + [ANY] * 3,
        scratch_shapes=[pltpu.VMEM((8, cap), F32), pltpu.VMEM((3, per_cell, TILE, 2 * TILE), jnp.bfloat16), DMA((3,))],
        compiler_params=pltpu.CompilerParams(vmem_limit_bytes=24 * 2**20),
        cost_estimate=cost(cap, 8 * per_cell),
    )
    plan, fs, ft, zs = make_plan(tzg, tfock, tfz, tzgt, ttrans, *tn, f, z)
    ws = pl.pallas_call(
        w_kernel,
        name="w_kernel",
        out_shape=cut_tiles(per_cell),
        in_specs=[SMEM, SMEM, VMEM] + [ANY] * 7,
        out_specs=ANY,
        scratch_shapes=[grown, cut, pltpu.VMEM((per_cell + 1, TILE, TILE), F32), DMA((7,)), DMA],
        compiler_params=params,
        cost_estimate=cost(cap, 7 * per_cell),
    )(tzg, plan, zs, g, *gn)
    p = pl.pallas_call(
        p_kernel,
        name="p_kernel",
        out_shape=[tiles(n) for n in (per_cell, x_room, x_room, y_room, y_room)],
        in_specs=[SMEM] + [VMEM] * 2,
        out_specs=[ANY] * 5,
        scratch_shapes=[pltpu.VMEM((per_cell + 2 * x_room + 2 * y_room + 1, TILE, TILE), F32), DMA((5,))],
        compiler_params=params,
        cost_estimate=cost(2 * cap, 7 * per_cell),
    )(plan, ft, ws)
    pn = [shifted(p[k + 1], axis, -by) for k, (axis, by) in enumerate(STEPS)]
    fock_grad, part = pl.pallas_call(
        rest_kernel,
        name="rest_kernel",
        out_shape=[pltpu.HBM((per_cell, TILE, TILE), F32), tiles(per_cell)],
        in_specs=[SMEM] * 4 + [VMEM] * 5 + [ANY] * 12,
        out_specs=[HBM, ANY],
        scratch_shapes=[
            pltpu.VMEM((run_start(per_cell, ga[0].shape[0], 5), TILE, TILE), F32),
            grown,
            cut,
            pltpu.VMEM((3, per_cell + 1, TILE, TILE), F32),
            DMA((7,)),
            DMA((7,)),
            DMA((2,)),
        ],
        compiler_params=params,
        cost_estimate=cost(3 * cap, 14 * per_cell),
    )(tfock, tfz, tzgt, plan, fs, ws, p[0], pn[0], pn[1], z, *zn, g, *gn)
    return fock_grad, join(plan, part, pn[2], pn[3], (2, 3))


def rooms_of(per_cell, lead):
    levels = ((29, 18, 12), (29, 18, 14), (30, 18, 13), (31, 18, 15), (34, 18, 17))
    scaled = [tuple(per_cell * room // 24 for room in level) for level in levels]
    return scaled + [(2 * per_cell - lead, per_cell, per_cell)]


def body(z_factor, fock, cotangent, tasks_zg, tasks_fock, tasks_fz, tasks_zgt, tasks_trans):
    per_cell = z_factor.shape[2]
    nx, ny = lax.axis_size("gx"), lax.axis_size("gy")
    z, f, g = z_factor[0, 0], fock[0, 0], cotangent[0, 0]
    lists = (tasks_zg, tasks_fock, tasks_fz, tasks_zgt, tasks_trans)
    tzg, tfock, tfz, tzgt, ttrans = (t.reshape(t.shape[2], 1, t.shape[3]) for t in lists)
    a_list = jax.ShapeDtypeStruct(tzg.shape, I32)
    lead = per_cell // 3
    rooms = rooms_of(per_cell, lead)
    met = pl.pallas_call(
        functools.partial(meet_kernel, rooms=rooms, lead=lead, cuts=lead // 4),
        name="meet_kernel",
        out_shape=[tiles(lead)] * 2
        + [a_list] * 4
        + [tiles(per_cell - lead)] * 2
        + [jax.ShapeDtypeStruct((1, 1), I32), jax.ShapeDtypeStruct((8, TILE), I32)],
        in_specs=[VMEM] * 5 + [ANY] * 2,
        out_specs=[ANY] * 2 + [VMEM] * 4 + [ANY] * 2 + [SMEM, VMEM],
        scratch_shapes=[pltpu.VMEM((2,) + tzg.shape, I32)] * 4
        + [
            pltpu.VMEM((1, TILE), I32),
            pltpu.VMEM((ny, TILE), I32),
            pltpu.VMEM((nx, ny, TILE), I32),
            pltpu.SMEM((8, TILE), I32),
            pltpu.VMEM((2 * per_cell - lead, TILE, TILE), F32),
            pltpu.VMEM((2, per_cell - lead, TILE, TILE), F32),
            DMA((4,)),
            DMA((4,)),
            DMA((12,)),
            DMA((12,)),
            DMA((ny,)),
            DMA((ny,)),
            DMA((nx,)),
            DMA((nx,)),
            DMA((5,)),
            DMA((2,)),
        ],
        compiler_params=pltpu.CompilerParams(collective_id=0, has_side_effects=True),
    )(tzg, tfock, tfz, tzgt, ttrans, g, z)
    ga, tn, gp, level, pick = met[:2], met[2:6], met[6:8], met[8], met[9]
    operands = (gp, z, f, g, tzg, tfock, tfz, tzgt, ttrans, tn, pick, ga)
    fock_grad, factor_grad = lax.switch(level[0, 0], [functools.partial(finish, *room) for room in rooms], *operands)
    return fock_grad[None, None], factor_grad[None, None]


def solution(mesh):
    cells = P("gx", "gy", None, None, None)
    lists = P("gx", "gy", None, None)
    return jax.shard_map(
        body,
        mesh=mesh,
        in_specs=(cells,) * 3 + (lists,) * 5,
        out_specs=(cells, cells),
        check_vma=False,
    )
```

```python
import functools

import jax
import jax.numpy as jnp
from jax import lax
from jax.experimental import pallas as pl
from jax.experimental.pallas import tpu as pltpu
from jax.sharding import PartitionSpec as P


TILE = 128
UNROLL = 8
F32 = jnp.float32
I32 = jnp.int32
MESH = pl.DeviceIdType.MESH
STEPS = (("gx", -1), ("gx", 1), ("gy", -1), ("gy", 1))


def split(tile):
    high = tile.astype(jnp.bfloat16)
    low = (tile - high.astype(F32)).astype(jnp.bfloat16)
    return jnp.concatenate([high, low], axis=1)


def product(left, right, turned):
    if turned:
        high, low = right[:, :TILE], right[:, TILE:]
        rows = jnp.concatenate([high, low], axis=0)
        operand = jnp.concatenate([rows, rows], axis=1)
        both = lax.dot_general(left, operand, (((1,), (1,)), ((), ())), preferred_element_type=F32)
    else:
        operand = jnp.concatenate([right, right], axis=0)
        both = lax.dot_general(left, operand, (((1,), (0,)), ((), ())), preferred_element_type=F32)
    return both[:, :TILE] + both[:, TILE:]


def run_list(count, entry, left_of, right_of, turned, total, unroll=UNROLL):
    def step(turn, _):
        entries = [entry(turn * unroll + i) for i in range(unroll)]
        values = [product(left_of(a), right_of(b), turned) for _, a, b in entries]
        for (t, _, _), value in zip(entries, values):
            total[t] += value
        return 0

    lax.fori_loop(0, (count + unroll - 1) // unroll, step, 0)


def live_count(tasks, per_cell):
    length = tasks.shape[2]
    return lax.while_loop(
        lambda n: jnp.logical_and(n < length, tasks[0, 0, jnp.minimum(n, length - 1)] < per_cell),
        lambda n: n + 1,
        jnp.int32(0),
    )


def split_all(source, target, per_cell):
    def step(i, _):
        target[i] = split(source[i])
        return 0

    lax.fori_loop(0, per_cell, step, 0)


def each(count, do):
    def step(i, _):
        do(i)
        return 0

    lax.fori_loop(0, count, step, 0)


def clear(total, first, count):
    def do(i):
        total[first + i] = jnp.zeros(total.shape[1:], total.dtype)

    each(count, do)


def moved_entry(tasks, plan, at):
    return lambda e: (tasks[0, 0, e], tasks[1, 0, e], plan[at, e])


def fetch(sources, grown, sems):
    copies = [
        pltpu.make_async_copy(src, grown.at[pl.ds(at, src.shape[0])], sems.at[i]) for i, (src, at) in enumerate(sources)
    ]
    for c in copies:
        c.start()
    return copies


FOCK_ROW, FZ_ROW, MAP_ROW, ZG_ROW, ZGT_ROW, LIST_ROW, PLAN_ROWS = 0, 1, 2, 6, 7, 8, 32


class Tables:
    def __init__(self, per_cell, length):
        self.per_cell, self.length = per_cell, length
        self.row = lax.broadcasted_iota(I32, (per_cell, length), 0)
        self.lane = lax.broadcasted_iota(I32, (1, TILE), 1)
        self.number = lax.broadcasted_iota(I32, (per_cell, TILE), 0)

    def hits(self, key):
        return jnp.broadcast_to(key, self.row.shape) == self.row

    def named(self, keys, first=0):
        found = sum(self.hits(key).astype(I32) for key in keys)
        found = jnp.where(self.row >= first, found, 0)
        return jnp.minimum(jnp.max(found, axis=1, keepdims=True), 1)

    def of_cell(self, lists, k, first=0):
        return self.named([tasks[2] - k * self.per_cell for tasks in lists], first)

    def inside(self, tasks, k):
        a = tasks[1]
        here = jnp.logical_and(a >= k * self.per_cell, a < (k + 1) * self.per_cell)
        return jnp.logical_and(here, tasks[0] < self.per_cell)

    def outs(self, tasks, k):
        return jnp.where(self.inside(tasks, k), tasks[0], self.per_cell)

    def ranked(self, found):
        square = (self.per_cell, self.per_cell)
        below = (lax.broadcasted_iota(I32, square, 1) < lax.broadcasted_iota(I32, square, 0)).astype(F32)
        return jnp.dot(below, jnp.broadcast_to(found, self.number.shape).astype(F32), preferred_element_type=F32)

    def packed_rows(self, found, first=0):
        spread = jnp.broadcast_to(self.lane - first, self.number.shape).astype(F32)
        here = jnp.logical_and(self.ranked(found) == spread, jnp.broadcast_to(found, self.number.shape) == 1)
        order = jnp.sum(jnp.where(here, self.number, 0), axis=0, keepdims=True)
        return jnp.where(self.lane == TILE - 1, jnp.sum(found), order)

    def rank_of(self, key, found):
        rank = self.ranked(found)[:, : self.length].astype(I32)
        return jnp.sum(jnp.where(self.hits(key), rank, 0), axis=0, keepdims=True)

    def places(self, tasks, lists, first, starts):
        place = tasks[2]
        for k in (3, 4):
            key = tasks[2] - k * self.per_cell
            here = jnp.logical_and(key >= first, key < self.per_cell)
            rank = self.rank_of(key, self.of_cell(lists, k, first))
            place = jnp.where(here, starts[k] + rank, place)
        return place


def by_quarter(lane, values):
    result = values[3]
    for i in (2, 1, 0):
        result = jnp.where(lane < (i + 1) * (TILE // 4), values[i], result)
    return result


def meet_kernel(tzg, tfock, tfz, tzgt, ttrans, g, z, *refs, rooms, lead, cuts):
    ga, tn, gp = refs[:2], refs[2:6], refs[6:8]
    (level, pick, gl, gt, fl, zl, msg, line, lines, picked, source, packed, bulk_s, bulk_r, list_s, list_r) = refs[8:24]
    line_s, line_r, lines_s, lines_r, own, put = refs[24:]
    ny, nx = line.shape[0], lines.shape[0]
    per_cell = g.shape[0]
    ix, iy = lax.axis_index("gx"), lax.axis_index("gy")
    barrier = pltpu.get_barrier_semaphore()
    for j in range(1, nx):
        pl.semaphore_signal(barrier, inc=1, device_id=(lax.rem(ix + j, nx), iy), device_id_type=MESH)
    for j in range(1, ny):
        pl.semaphore_signal(barrier, inc=1, device_id=(ix, lax.rem(iy + j, ny)), device_id_type=MESH)
    rest_g = per_cell - lead
    loads = [
        pltpu.make_async_copy(g.at[pl.ds(lead, rest_g)], source.at[pl.ds(0, rest_g)], own.at[3]),
        pltpu.make_async_copy(z, source.at[pl.ds(rest_g, per_cell)], own.at[4]),
    ]
    for c in loads:
        c.start()
    others = []
    for axis, by in STEPS:
        others.append((lax.rem(ix + by + nx, nx), iy) if axis == "gx" else (ix, lax.rem(iy + by + ny, ny)))
    pl.semaphore_wait(barrier, nx + ny - 2)

    def bulk(i, k, start, size):
        part = pl.ds(start, size)
        return pltpu.make_async_remote_copy(
            g.at[part], ga[(k ^ 1) - 2].at[part], bulk_s.at[i], bulk_r.at[i], device_id=others[k], device_id_type=MESH
        )

    large = [bulk(0, 2, 0, cuts), bulk(1, 3, 0, cuts)]
    for c in large:
        c.start()

    lists = []
    for i in range(2):
        lists += [(tzg, gl.at[i], others[2 + i]), (tzgt, gt.at[i], others[2 + i])]
        lists += [(tfock, fl.at[i], others[2 + i]), (tfz, zl.at[i], others[2 + i])]
    lists += [(ttrans, tn[k], others[k]) for k in range(4)]
    small = []
    for i, (src, dst, to) in enumerate(lists):
        small.append(pltpu.make_async_remote_copy(src, dst, list_s.at[i], list_r.at[i], device_id=to, device_id_type=MESH))
        small[-1].start()

    tables = Tables(per_cell, tfock.shape[2])

    def most(found):
        return functools.reduce(jnp.maximum, [jnp.sum(v) for v in found])

    needs = (
        most([tables.of_cell((tzg, tzgt), k, lead) + tables.of_cell((tfock, tfz), k) for k in (3, 4)]),
        most([tables.named((tables.outs(ttrans, k),)) for k in (1, 2)]),
        most([tables.named((tables.outs(ttrans, k),)) for k in (3, 4)]),
        0,
    )
    msg[...] = by_quarter(tables.lane, needs)
    keep = pltpu.make_async_copy(msg, line.at[pl.ds(0, 1)], own.at[0])
    keep.start()
    keep.wait()
    first = []
    for j in range(1, ny):
        to = (ix, lax.rem(iy + j, ny))
        row = line.at[pl.ds(0, 1)]
        first.append(pltpu.make_async_remote_copy(row, line.at[pl.ds(j, 1)], line_s.at[j], line_r.at[j], device_id=to, device_id_type=MESH))
        first[-1].start()
    rest = [bulk(2, 2, cuts, lead - cuts), bulk(3, 3, cuts, lead - cuts)]
    for c in rest:
        c.start()
    for c in first:
        c.wait()
    keep = pltpu.make_async_copy(line, lines.at[0], own.at[1])
    keep.start()
    second = []
    for j in range(1, nx):
        to = (lax.rem(ix + j, nx), iy)
        second.append(pltpu.make_async_remote_copy(line, lines.at[j], lines_s.at[j], lines_r.at[j], device_id=to, device_id_type=MESH))
        second[-1].start()
    for c in small:
        c.wait()

    pick[...] = jnp.zeros_like(pick)
    for side in range(2):
        g_named = tables.of_cell((gl.at[side], gt.at[side]), 3 + side, lead)
        z_named = tables.of_cell((fl.at[side], zl.at[side]), 3 + side)
        count = jnp.sum(g_named)
        order = jnp.where(tables.lane < count, tables.packed_rows(g_named) - lead, tables.packed_rows(z_named, count) + rest_g)
        pick[side : side + 1, :] = jnp.clip(order, 0, rest_g + per_cell - 1)
    copy = pltpu.make_async_copy(pick, picked, own.at[2])
    copy.start()
    copy.wait()
    for c in loads:
        c.wait()
    puts = []
    for side in range(2):

        def take(s, _, side=side):
            packed[side, s] = source[picked[side, s]]
            return 0

        lax.fori_loop(0, rest_g, take, 0)
        puts.append(pltpu.make_async_copy(packed.at[side], gp[side], put.at[side]))
        puts[-1].start()
    keep.wait()
    for c in second:
        c.wait()
    found = jnp.max(lines[...], axis=0)
    lane = lax.broadcasted_iota(I32, found.shape, 1)
    needs = [jnp.max(jnp.where(by_quarter(lane, [int(i == j) for j in range(4)]) == 1, found, 0)) for i in range(4)]
    first_fit, unfit = 0, jnp.int32(1)
    for level_rooms in rooms[:-1]:
        over = [need > room for need, room in zip(needs, level_rooms)]
        unfit = unfit * functools.reduce(jnp.logical_or, over).astype(I32)
        first_fit = first_fit + unfit
    level[0, 0] = first_fit
    for c in large + rest + puts:
        c.wait()


def pack_kernel(pick, z, out3, out4, packed, put, *, first):
    per_cell, room = z.shape[0], out3.shape[0]
    puts = []
    for side, out in enumerate((out3, out4)):

        def take(s, _, side=side):
            packed[side, s] = z[jnp.clip(pick[side, first + s] - first, 0, per_cell - 1)]
            return 0

        lax.fori_loop(0, room, take, 0)
        puts.append(pltpu.make_async_copy(packed.at[side], out, put.at[side]))
        puts[-1].start()
    for c in puts:
        c.wait()


def run_start(per_cell, lead, k):
    return 3 * per_cell + (k - 3) * (2 * per_cell - lead)


def plan_kernel(tzg, tfock, tfz, tzgt, t0, t1, t2, t3, t4, f, z, plan, fs, ft, zs, table, cut, put, *, lead):
    per_cell, length = f.shape[0], tfock.shape[2]

    def cut_all(i, _):
        tile = f[i]
        cut[0, i] = split(tile)
        cut[1, i] = split(tile.T)
        cut[2, i] = split(z[i])
        return 0

    lax.fori_loop(0, per_cell, cut_all, 0)
    puts = [pltpu.make_async_copy(cut.at[i], out, put.at[i]) for i, out in enumerate((fs, ft, zs))]
    for c in puts:
        c.start()
    tables = Tables(per_cell, length)
    lane = tables.lane
    plan[...] = jnp.zeros_like(plan)
    g_starts = {k: k * per_cell + lead for k in (3, 4)}
    z_starts = {k: run_start(per_cell, lead, k) + jnp.sum(tables.of_cell((tzg, tzgt), k, lead)) for k in (3, 4)}
    for at, tasks, lists, first, starts in (
        (FOCK_ROW, tfock, (tfock, tfz), 0, z_starts),
        (FZ_ROW, tfz, (tfock, tfz), 0, z_starts),
        (ZG_ROW, tzg, (tzg, tzgt), lead, g_starts),
        (ZGT_ROW, tzgt, (tzg, tzgt), lead, g_starts),
    ):
        plan[at : at + 1, pl.ds(0, length)] = tables.places(tasks, lists, first, starts)
    for k in range(1, 5):
        plan[MAP_ROW + k - 1 : MAP_ROW + k, :] = tables.packed_rows(tables.named((tables.outs(t0, k),)))
    square = (length, length)
    before = (lax.broadcasted_iota(I32, square, 0) < lax.broadcasted_iota(I32, square, 1)).astype(F32)
    same = (lax.broadcasted_iota(I32, square, 0) == lax.broadcasted_iota(I32, square, 1)).astype(F32)
    slots = lax.broadcasted_iota(I32, (length, TILE), 1).astype(F32)
    table[...] = jnp.zeros_like(table)
    for k, tasks in enumerate((t0, t1, t2, t3, t4)):
        here, out = tables.inside(tasks, k), tables.outs(tasks, k)
        slot = out if k == 0 else tables.rank_of(out, tables.named((out,)))
        for i, value in enumerate((slot, tasks[1] - k * per_cell, tasks[2] - k * per_cell, here)):
            table[i : i + 1, :] = value.astype(F32)
        earlier = jnp.dot(table[...], before, preferred_element_type=F32)
        table[4:5, :] = earlier[3:4, :]
        turned = lax.dot_general(same, table[...], (((1,), (1,)), ((), ())), preferred_element_type=F32)
        to_slot = jnp.logical_and(jnp.broadcast_to(turned[:, 4:5], slots.shape) == slots, jnp.broadcast_to(turned[:, 3:4], slots.shape) > 0.5)
        moved = jnp.dot(table[...], to_slot.astype(F32), preferred_element_type=F32).astype(I32)
        count = jnp.sum(here.astype(I32))
        at = LIST_ROW + 4 * k
        for i in range(3):
            plan[at + i : at + i + 1, :] = moved[i : i + 1, :]
        plan[at : at + 1, :] = jnp.where(lane < count, moved[0:1, :], TILE - 1)
        plan[at + 3 : at + 4, :] = jnp.where(lane == TILE - 1, count, 0)
    for c in puts:
        c.wait()


def w_kernel(tasks, plan, zs, g0, g1, g2, a3, g3, a4, g4, ws, grown, cut, total, sems, osem):
    per_cell, lead = zs.shape[0], a3.shape[0]
    copies = fetch(g_places(per_cell, lead, g0, g1, g2, a3, g3, a4, g4), grown, sems)
    clear(total, 0, per_cell)
    live = live_count(tasks, per_cell)
    for c in copies:
        c.wait()
    entry = moved_entry(tasks, plan, ZG_ROW)
    run_list(live, entry, lambda a: zs[a], lambda b: split(grown[b]), False, total, 4)
    split_all(total, cut, per_cell)
    out = pltpu.make_async_copy(cut, ws, osem)
    out.start()
    out.wait()


def g_places(per_cell, lead, g0, g1, g2, a3, g3, a4, g4):
    places = [(src, k * per_cell) for k, src in enumerate((g0, g1, g2, a3, a4))]
    return places + [(g3, 3 * per_cell + lead), (g4, 4 * per_cell + lead)]


def p_kernel(plan, ft, ws, p0, p1, p2, p3, p4, total, osem):
    outs = (p0, p1, p2, p3, p4)
    starts = [sum(p.shape[0] for p in outs[:k]) for k in range(6)]
    last = starts[5]

    clear(total, 0, last)

    def one(k, _):
        at = LIST_ROW + 4 * k
        first = sum(jnp.where(k == i, start, 0) for i, start in enumerate(starts[:5]))

        def entry(e):
            return jnp.minimum(first + plan[at, e], last), plan[at + 1, e], plan[at + 2, e]

        run_list(plan[at + 3, TILE - 1], entry, lambda a: ft[a], lambda b: ws[b], False, total, 4)
        return 0

    lax.fori_loop(0, 5, one, 0)
    copies = [pltpu.make_async_copy(total.at[pl.ds(starts[k], p.shape[0])], p, osem.at[k]) for k, p in enumerate(outs)]
    for c in copies:
        c.start()
    for c in copies:
        c.wait()


def rest_kernel(tfock, tfz, tzgt, plan, fs, ws, p0, z0, z1, z2, z3, z4, g0, g1, g2, a3, g3, a4, g4, fock, factor, zgrown, ggrown, us, total, zsem, gsem, osem):
    per_cell, lead = p0.shape[0], a3.shape[0]
    places = [(src, k * per_cell) for k, src in enumerate((z0, z1, z2))]
    for k, first, then in ((3, g3, z3), (4, g4, z4)):
        start = run_start(per_cell, lead, k)
        places += [(first, start), (then, start + first.shape[0])]
    zcopies = fetch(places, zgrown, zsem)
    gcopies = fetch(g_places(per_cell, lead, g0, g1, g2, a3, g3, a4, g4), ggrown, gsem)
    clear(total.at[0], 0, per_cell)
    clear(total.at[1], 0, per_cell)

    def begin(i):
        total[2, i] = p0[i]

    each(per_cell, begin)
    fz_live, fock_live, zgt_live = (live_count(tasks, per_cell) for tasks in (tfz, tfock, tzgt))
    for c in zcopies:
        c.wait()
    run_list(fz_live, moved_entry(tfz, plan, FZ_ROW), lambda a: fs[a], lambda b: split(zgrown[b]), False, total.at[0])
    split_all(total.at[0], us, per_cell)
    run_list(fock_live, moved_entry(tfock, plan, FOCK_ROW), lambda a: ws[a], lambda b: split(zgrown[b]), True, total.at[1])
    out1 = pltpu.make_async_copy(total.at[1, pl.ds(0, per_cell)], fock, osem.at[0])
    out1.start()
    for c in gcopies:
        c.wait()
    run_list(zgt_live, moved_entry(tzgt, plan, ZGT_ROW), lambda a: us[a], lambda b: split(ggrown[b]), True, total.at[2])
    out2 = pltpu.make_async_copy(total.at[2, pl.ds(0, per_cell)], factor, osem.at[1])
    out2.start()
    out1.wait()
    out2.wait()


def join_kernel(plan, part, p1, p2, p3, p4, factor, total, puts, *, pieces):
    per_cell = part.shape[0]
    size = per_cell // pieces
    lists = tuple(enumerate((p1, p2, p3, p4)))
    counts = [jnp.minimum(plan[MAP_ROW + side, TILE - 1], p.shape[0]) for side, p in lists]
    at = [jnp.int32(0)] * len(lists)
    stored = []
    for i in range(pieces):
        piece = pl.ds(i * size, size)

        def begin(t, i=i):
            total[i * size + t] = part[i * size + t]

        each(size, begin)
        for j, (side, p) in enumerate(lists):

            def more(s, j=j, side=side, i=i):
                return jnp.logical_and(s < counts[j], plan[MAP_ROW + side, s] < (i + 1) * size)

            def add(s, side=side, p=p):
                total[plan[MAP_ROW + side, s]] += p[s]
                return s + 1

            at[j] = lax.while_loop(more, add, at[j])
        stored.append(pltpu.make_async_copy(total.at[piece], factor.at[piece], puts.at[i]))
        stored[-1].start()
    for c in stored:
        c.wait()


SMEM = pl.BlockSpec(memory_space=pltpu.SMEM)
VMEM = pl.BlockSpec(memory_space=pltpu.VMEM)
ANY = pl.BlockSpec(memory_space=pl.ANY)
HBM = pl.BlockSpec(memory_space=pltpu.HBM)
DMA = pltpu.SemaphoreType.DMA


def cost(tasks, tiles):
    return pl.CostEstimate(flops=tasks * 2 * TILE**3 * 8, bytes_accessed=tiles * TILE * TILE * 4, transcendentals=0)


def shifted(array, axis, by):
    n = lax.axis_size(axis)
    return lax.ppermute(array, axis, [(i, (i + by) % n) for i in range(n)])


def tiles(n):
    return jax.ShapeDtypeStruct((n, TILE, TILE), F32)


def cut_tiles(n):
    return jax.ShapeDtypeStruct((n, TILE, 2 * TILE), jnp.bfloat16)


def join(plan, part, sums):
    per_cell = part.shape[0]
    pieces = 2 if per_cell % 2 == 0 else 1
    return pl.pallas_call(
        functools.partial(join_kernel, pieces=pieces),
        name="join_kernel",
        out_shape=pltpu.HBM((per_cell, TILE, TILE), F32),
        in_specs=[SMEM] + [VMEM] * 5,
        out_specs=HBM,
        scratch_shapes=[pltpu.VMEM((per_cell, TILE, TILE), F32), DMA((pieces,))],
        compiler_params=pltpu.CompilerParams(vmem_limit_bytes=16 * 2**20),
        cost_estimate=cost(0, 4 * per_cell),
    )(plan, part, *sums)


def finish(run_room, x_room, y_room, gp, z, f, g, tzg, tfock, tfz, tzgt, ttrans, tn, pick, ga):
    per_cell = z.shape[0]
    cap = tzg.shape[2]
    grown = pltpu.VMEM((5 * per_cell, TILE, TILE), F32)
    cut = pltpu.VMEM((per_cell, TILE, 2 * TILE), jnp.bfloat16)
    params = pltpu.CompilerParams(vmem_limit_bytes=40 * 2**20)
    gy = (shifted(gp[0], "gy", 1), shifted(gp[1], "gy", -1))
    first = gp[0].shape[0]
    z_room = run_room - first
    pack = pl.pallas_call(
        functools.partial(pack_kernel, first=first),
        name="pack_kernel",
        out_shape=[tiles(z_room)] * 2,
        in_specs=[SMEM, VMEM],
        out_specs=[ANY] * 2,
        scratch_shapes=[pltpu.VMEM((2, z_room, TILE, TILE), F32), DMA((2,))],
        compiler_params=pltpu.CompilerParams(vmem_limit_bytes=16 * 2**20),
        cost_estimate=cost(0, 4 * per_cell),
    )
    z3, z4 = pack(pick, z)
    g_late, z_late, z3, z4 = lax.optimization_barrier((g, z, z3, z4))
    gn = (shifted(g_late, "gx", 1), shifted(g_late, "gx", -1), ga[0], gy[0], ga[1], gy[1])
    zy = (shifted(z3, "gy", 1), shifted(z4, "gy", -1))
    zn = (shifted(z_late, "gx", 1), shifted(z_late, "gx", -1)) + zy
    make_plan = pl.pallas_call(
        functools.partial(plan_kernel, lead=ga[0].shape[0]),
        name="plan_kernel",
        out_shape=[jax.ShapeDtypeStruct((PLAN_ROWS, TILE), I32)] + [cut_tiles(per_cell)] * 3,
        in_specs=[VMEM] * 11,
        out_specs=[VMEM] + [ANY] * 3,
        scratch_shapes=[pltpu.VMEM((8, cap), F32), pltpu.VMEM((3, per_cell, TILE, 2 * TILE), jnp.bfloat16), DMA((3,))],
        compiler_params=pltpu.CompilerParams(vmem_limit_bytes=24 * 2**20),
        cost_estimate=cost(cap, 8 * per_cell),
    )
    plan, fs, ft, zs = make_plan(tzg, tfock, tfz, tzgt, ttrans, *tn, f, z)
    ws = pl.pallas_call(
        w_kernel,
        name="w_kernel",
        out_shape=cut_tiles(per_cell),
        in_specs=[SMEM, SMEM, VMEM] + [ANY] * 7,
        out_specs=ANY,
        scratch_shapes=[grown, cut, pltpu.VMEM((per_cell + 1, TILE, TILE), F32), DMA((7,)), DMA],
        compiler_params=params,
        cost_estimate=cost(cap, 7 * per_cell),
    )(tzg, plan, zs, g, *gn)
    p = pl.pallas_call(
        p_kernel,
        name="p_kernel",
        out_shape=[tiles(n) for n in (per_cell, x_room, x_room, y_room, y_room)],
        in_specs=[SMEM] + [VMEM] * 2,
        out_specs=[ANY] * 5,
        scratch_shapes=[pltpu.VMEM((per_cell + 2 * x_room + 2 * y_room + 1, TILE, TILE), F32), DMA((5,))],
        compiler_params=params,
        cost_estimate=cost(2 * cap, 7 * per_cell),
    )(plan, ft, ws)
    pn = []
    for k, (axis, by) in enumerate(STEPS):
        pn.append(shifted(p[k + 1], axis, -by))
    fock_grad, part = pl.pallas_call(
        rest_kernel,
        name="rest_kernel",
        out_shape=[pltpu.HBM((per_cell, TILE, TILE), F32), tiles(per_cell)],
        in_specs=[SMEM] * 4 + [VMEM] * 3 + [ANY] * 12,
        out_specs=[HBM, ANY],
        scratch_shapes=[
            pltpu.VMEM((run_start(per_cell, ga[0].shape[0], 5), TILE, TILE), F32),
            grown,
            cut,
            pltpu.VMEM((3, per_cell + 1, TILE, TILE), F32),
            DMA((7,)),
            DMA((7,)),
            DMA((2,)),
        ],
        compiler_params=params,
        cost_estimate=cost(3 * cap, 14 * per_cell),
    )(tfock, tfz, tzgt, plan, fs, ws, p[0], z, *zn, g, *gn)
    return fock_grad, join(plan, part, pn)


def rooms_of(per_cell, lead):
    levels = ((29, 18, 12), (29, 18, 14), (30, 18, 13), (31, 18, 15), (34, 18, 17))
    scaled = [tuple(per_cell * room // 24 for room in level) for level in levels]
    return scaled + [(2 * per_cell - lead, per_cell, per_cell)]


def body(z_factor, fock, cotangent, tasks_zg, tasks_fock, tasks_fz, tasks_zgt, tasks_trans):
    per_cell = z_factor.shape[2]
    nx, ny = lax.axis_size("gx"), lax.axis_size("gy")
    z, f, g = z_factor[0, 0], fock[0, 0], cotangent[0, 0]
    lists = (tasks_zg, tasks_fock, tasks_fz, tasks_zgt, tasks_trans)
    tzg, tfock, tfz, tzgt, ttrans = (t.reshape(t.shape[2], 1, t.shape[3]) for t in lists)
    a_list = jax.ShapeDtypeStruct(tzg.shape, I32)
    lead = per_cell // 3
    rooms = rooms_of(per_cell, lead)
    met = pl.pallas_call(
        functools.partial(meet_kernel, rooms=rooms, lead=lead, cuts=lead // 4),
        name="meet_kernel",
        out_shape=[tiles(lead)] * 2
        + [a_list] * 4
        + [tiles(per_cell - lead)] * 2
        + [jax.ShapeDtypeStruct((1, 1), I32), jax.ShapeDtypeStruct((8, TILE), I32)],
        in_specs=[VMEM] * 5 + [ANY] * 2,
        out_specs=[ANY] * 2 + [VMEM] * 4 + [ANY] * 2 + [SMEM, VMEM],
        scratch_shapes=[pltpu.VMEM((2,) + tzg.shape, I32)] * 4
        + [
            pltpu.VMEM((1, TILE), I32),
            pltpu.VMEM((ny, TILE), I32),
            pltpu.VMEM((nx, ny, TILE), I32),
            pltpu.SMEM((8, TILE), I32),
            pltpu.VMEM((2 * per_cell - lead, TILE, TILE), F32),
            pltpu.VMEM((2, per_cell - lead, TILE, TILE), F32),
            DMA((4,)),
            DMA((4,)),
            DMA((12,)),
            DMA((12,)),
            DMA((ny,)),
            DMA((ny,)),
            DMA((nx,)),
            DMA((nx,)),
            DMA((5,)),
            DMA((2,)),
        ],
        compiler_params=pltpu.CompilerParams(collective_id=0, has_side_effects=True),
    )(tzg, tfock, tfz, tzgt, ttrans, g, z)
    ga, tn, gp, level, pick = met[:2], met[2:6], met[6:8], met[8], met[9]
    operands = (gp, z, f, g, tzg, tfock, tfz, tzgt, ttrans, tn, pick, ga)
    fock_grad, factor_grad = lax.switch(level[0, 0], [functools.partial(finish, *room) for room in rooms], *operands)
    return fock_grad[None, None], factor_grad[None, None]


def solution(mesh):
    cells = P("gx", "gy", None, None, None)
    lists = P("gx", "gy", None, None)
    return jax.shard_map(
        body,
        mesh=mesh,
        in_specs=(cells,) * 3 + (lists,) * 5,
        out_specs=(cells, cells),
        check_vma=False,
    )
```

```python
import functools

import jax
import jax.numpy as jnp
from jax import lax
from jax.experimental import pallas as pl
from jax.experimental.pallas import tpu as pltpu
from jax.sharding import PartitionSpec as P


TILE = 128
UNROLL = 8
F32 = jnp.float32
I32 = jnp.int32
MESH = pl.DeviceIdType.MESH
STEPS = (("gx", -1), ("gx", 1), ("gy", -1), ("gy", 1))


def split(tile):
    high = tile.astype(jnp.bfloat16)
    low = (tile - high.astype(F32)).astype(jnp.bfloat16)
    return jnp.concatenate([high, low], axis=1)


def product(left, right, turned):
    if turned:
        high, low = right[:, :TILE], right[:, TILE:]
        rows = jnp.concatenate([high, low], axis=0)
        operand = jnp.concatenate([rows, rows], axis=1)
        both = lax.dot_general(left, operand, (((1,), (1,)), ((), ())), preferred_element_type=F32)
    else:
        operand = jnp.concatenate([right, right], axis=0)
        both = lax.dot_general(left, operand, (((1,), (0,)), ((), ())), preferred_element_type=F32)
    return both[:, :TILE] + both[:, TILE:]


def run_list(count, entry, left_of, right_of, turned, total, unroll=UNROLL):
    def step(turn, _):
        entries = [entry(turn * unroll + i) for i in range(unroll)]
        values = [product(left_of(a), right_of(b), turned) for _, a, b in entries]
        for (t, _, _), value in zip(entries, values):
            total[t] += value
        return 0

    lax.fori_loop(0, (count + unroll - 1) // unroll, step, 0)


def live_count(tasks, per_cell):
    length = tasks.shape[2]
    return lax.while_loop(
        lambda n: jnp.logical_and(n < length, tasks[0, 0, jnp.minimum(n, length - 1)] < per_cell),
        lambda n: n + 1,
        jnp.int32(0),
    )


def split_all(source, target, per_cell):
    def step(i, _):
        target[i] = split(source[i])
        return 0

    lax.fori_loop(0, per_cell, step, 0)


def each(count, do):
    def step(i, _):
        do(i)
        return 0

    lax.fori_loop(0, count, step, 0)


def clear(total, first, count):
    def do(i):
        total[first + i] = jnp.zeros(total.shape[1:], total.dtype)

    each(count, do)


def moved_entry(tasks, plan, at):
    return lambda e: (tasks[0, 0, e], tasks[1, 0, e], plan[at, e])


def fetch(sources, grown, sems):
    copies = [
        pltpu.make_async_copy(src, grown.at[pl.ds(at, src.shape[0])], sems.at[i]) for i, (src, at) in enumerate(sources)
    ]
    for c in copies:
        c.start()
    return copies


FOCK_ROW, FZ_ROW, MAP_ROW, ZG_ROW, ZGT_ROW, LIST_ROW, PLAN_ROWS = 0, 1, 2, 6, 7, 8, 32


class Tables:
    def __init__(self, per_cell, length):
        self.per_cell, self.length = per_cell, length
        self.row = lax.broadcasted_iota(I32, (per_cell, length), 0)
        self.lane = lax.broadcasted_iota(I32, (1, TILE), 1)
        self.number = lax.broadcasted_iota(I32, (per_cell, TILE), 0)

    def hits(self, key):
        return jnp.broadcast_to(key, self.row.shape) == self.row

    def named(self, keys, first=0):
        found = sum(self.hits(key).astype(I32) for key in keys)
        found = jnp.where(self.row >= first, found, 0)
        return jnp.minimum(jnp.max(found, axis=1, keepdims=True), 1)

    def of_cell(self, lists, k, first=0):
        return self.named([tasks[2] - k * self.per_cell for tasks in lists], first)

    def inside(self, tasks, k):
        a = tasks[1]
        here = jnp.logical_and(a >= k * self.per_cell, a < (k + 1) * self.per_cell)
        return jnp.logical_and(here, tasks[0] < self.per_cell)

    def outs(self, tasks, k):
        return jnp.where(self.inside(tasks, k), tasks[0], self.per_cell)

    def ranked(self, found):
        square = (self.per_cell, self.per_cell)
        below = (lax.broadcasted_iota(I32, square, 1) < lax.broadcasted_iota(I32, square, 0)).astype(F32)
        return jnp.dot(below, jnp.broadcast_to(found, self.number.shape).astype(F32), preferred_element_type=F32)

    def packed_rows(self, found, first=0):
        spread = jnp.broadcast_to(self.lane - first, self.number.shape).astype(F32)
        here = jnp.logical_and(self.ranked(found) == spread, jnp.broadcast_to(found, self.number.shape) == 1)
        order = jnp.sum(jnp.where(here, self.number, 0), axis=0, keepdims=True)
        return jnp.where(self.lane == TILE - 1, jnp.sum(found), order)

    def rank_of(self, key, found):
        rank = self.ranked(found)[:, : self.length].astype(I32)
        return jnp.sum(jnp.where(self.hits(key), rank, 0), axis=0, keepdims=True)

    def places(self, tasks, lists, first, starts):
        place = tasks[2]
        for k in (3, 4):
            key = tasks[2] - k * self.per_cell
            here = jnp.logical_and(key >= first, key < self.per_cell)
            rank = self.rank_of(key, self.of_cell(lists, k, first))
            place = jnp.where(here, starts[k] + rank, place)
        return place


def by_quarter(lane, values):
    result = values[3]
    for i in (2, 1, 0):
        result = jnp.where(lane < (i + 1) * (TILE // 4), values[i], result)
    return result


def meet_kernel(tzg, tfock, tfz, tzgt, ttrans, g, z, *refs, rooms, lead, cuts):
    ga, tn, gp = refs[:2], refs[2:6], refs[6:8]
    (level, pick, gl, gt, fl, zl, msg, line, lines, picked, source, packed, bulk_s, bulk_r, list_s, list_r) = refs[8:24]
    line_s, line_r, lines_s, lines_r, own, put = refs[24:]
    ny, nx = line.shape[0], lines.shape[0]
    per_cell = g.shape[0]
    ix, iy = lax.axis_index("gx"), lax.axis_index("gy")
    barrier = pltpu.get_barrier_semaphore()
    for j in range(1, nx):
        pl.semaphore_signal(barrier, inc=1, device_id=(lax.rem(ix + j, nx), iy), device_id_type=MESH)
    for j in range(1, ny):
        pl.semaphore_signal(barrier, inc=1, device_id=(ix, lax.rem(iy + j, ny)), device_id_type=MESH)
    rest_g = per_cell - lead
    loads = [
        pltpu.make_async_copy(g.at[pl.ds(lead, rest_g)], source.at[pl.ds(0, rest_g)], own.at[3]),
        pltpu.make_async_copy(z, source.at[pl.ds(rest_g, per_cell)], own.at[4]),
    ]
    for c in loads:
        c.start()
    others = []
    for axis, by in STEPS:
        others.append((lax.rem(ix + by + nx, nx), iy) if axis == "gx" else (ix, lax.rem(iy + by + ny, ny)))
    pl.semaphore_wait(barrier, nx + ny - 2)

    def bulk(i, k, start, size):
        part = pl.ds(start, size)
        return pltpu.make_async_remote_copy(
            g.at[part], ga[(k ^ 1) - 2].at[part], bulk_s.at[i], bulk_r.at[i], device_id=others[k], device_id_type=MESH
        )

    large = [bulk(0, 2, 0, cuts), bulk(1, 3, 0, cuts)]
    for c in large:
        c.start()

    lists = []
    for i in range(2):
        lists += [(tzg, gl.at[i], others[2 + i]), (tzgt, gt.at[i], others[2 + i])]
        lists += [(tfock, fl.at[i], others[2 + i]), (tfz, zl.at[i], others[2 + i])]
    lists += [(ttrans, tn[k], others[k]) for k in range(4)]
    small = []
    for i, (src, dst, to) in enumerate(lists):
        small.append(pltpu.make_async_remote_copy(src, dst, list_s.at[i], list_r.at[i], device_id=to, device_id_type=MESH))
        small[-1].start()

    tables = Tables(per_cell, tfock.shape[2])

    def most(found):
        return functools.reduce(jnp.maximum, [jnp.sum(v) for v in found])

    needs = (
        most([tables.of_cell((tzg, tzgt), k, lead) + tables.of_cell((tfock, tfz), k) for k in (3, 4)]),
        most([tables.named((tables.outs(ttrans, k),)) for k in (1, 2)]),
        most([tables.named((tables.outs(ttrans, k),)) for k in (3, 4)]),
        0,
    )
    msg[...] = by_quarter(tables.lane, needs)
    keep = pltpu.make_async_copy(msg, line.at[pl.ds(0, 1)], own.at[0])
    keep.start()
    keep.wait()
    first = []
    for j in range(1, ny):
        to = (ix, lax.rem(iy + j, ny))
        row = line.at[pl.ds(0, 1)]
        first.append(pltpu.make_async_remote_copy(row, line.at[pl.ds(j, 1)], line_s.at[j], line_r.at[j], device_id=to, device_id_type=MESH))
        first[-1].start()
    rest = [bulk(2, 2, cuts, lead - cuts), bulk(3, 3, cuts, lead - cuts)]
    for c in rest:
        c.start()
    for c in first:
        c.wait()
    keep = pltpu.make_async_copy(line, lines.at[0], own.at[1])
    keep.start()
    second = []
    for j in range(1, nx):
        to = (lax.rem(ix + j, nx), iy)
        second.append(pltpu.make_async_remote_copy(line, lines.at[j], lines_s.at[j], lines_r.at[j], device_id=to, device_id_type=MESH))
        second[-1].start()
    for c in small:
        c.wait()

    pick[...] = jnp.zeros_like(pick)
    for side in range(2):
        g_named = tables.of_cell((gl.at[side], gt.at[side]), 3 + side, lead)
        z_named = tables.of_cell((fl.at[side], zl.at[side]), 3 + side)
        count = jnp.sum(g_named)
        order = jnp.where(tables.lane < count, tables.packed_rows(g_named) - lead, tables.packed_rows(z_named, count) + rest_g)
        pick[side : side + 1, :] = jnp.clip(order, 0, rest_g + per_cell - 1)
    copy = pltpu.make_async_copy(pick, picked, own.at[2])
    copy.start()
    copy.wait()
    for c in loads:
        c.wait()
    puts = []
    for side in range(2):

        def take(s, _, side=side):
            packed[side, s] = source[picked[side, s]]
            return 0

        lax.fori_loop(0, rest_g, take, 0)
        puts.append(pltpu.make_async_copy(packed.at[side], gp[side], put.at[side]))
        puts[-1].start()
    keep.wait()
    for c in second:
        c.wait()
    found = jnp.max(lines[...], axis=0)
    lane = lax.broadcasted_iota(I32, found.shape, 1)
    needs = [jnp.max(jnp.where(by_quarter(lane, [int(i == j) for j in range(4)]) == 1, found, 0)) for i in range(4)]
    first_fit, unfit = 0, jnp.int32(1)
    for level_rooms in rooms[:-1]:
        over = [need > room for need, room in zip(needs, level_rooms)]
        unfit = unfit * functools.reduce(jnp.logical_or, over).astype(I32)
        first_fit = first_fit + unfit
    level[0, 0] = first_fit
    for c in large + rest + puts:
        c.wait()


def pack_kernel(pick, z, out3, out4, packed, put, *, first):
    per_cell, room = z.shape[0], out3.shape[0]
    puts = []
    for side, out in enumerate((out3, out4)):

        def take(s, _, side=side):
            packed[side, s] = z[jnp.clip(pick[side, first + s] - first, 0, per_cell - 1)]
            return 0

        lax.fori_loop(0, room, take, 0)
        puts.append(pltpu.make_async_copy(packed.at[side], out, put.at[side]))
        puts[-1].start()
    for c in puts:
        c.wait()


def run_start(per_cell, lead, k):
    return 3 * per_cell + (k - 3) * (2 * per_cell - lead)


def plan_kernel(tzg, tfock, tfz, tzgt, t0, t1, t2, t3, t4, f, z, plan, fs, ft, zs, table, cut, put, *, lead):
    per_cell, length = f.shape[0], tfock.shape[2]

    def cut_all(i, _):
        tile = f[i]
        cut[0, i] = split(tile)
        cut[1, i] = split(tile.T)
        cut[2, i] = split(z[i])
        return 0

    lax.fori_loop(0, per_cell, cut_all, 0)
    puts = [pltpu.make_async_copy(cut.at[i], out, put.at[i]) for i, out in enumerate((fs, ft, zs))]
    for c in puts:
        c.start()
    tables = Tables(per_cell, length)
    lane = tables.lane
    plan[...] = jnp.zeros_like(plan)
    g_starts = {k: k * per_cell + lead for k in (3, 4)}
    z_starts = {k: run_start(per_cell, lead, k) + jnp.sum(tables.of_cell((tzg, tzgt), k, lead)) for k in (3, 4)}
    for at, tasks, lists, first, starts in (
        (FOCK_ROW, tfock, (tfock, tfz), 0, z_starts),
        (FZ_ROW, tfz, (tfock, tfz), 0, z_starts),
        (ZG_ROW, tzg, (tzg, tzgt), lead, g_starts),
        (ZGT_ROW, tzgt, (tzg, tzgt), lead, g_starts),
    ):
        plan[at : at + 1, pl.ds(0, length)] = tables.places(tasks, lists, first, starts)
    for k in range(1, 5):
        plan[MAP_ROW + k - 1 : MAP_ROW + k, :] = tables.packed_rows(tables.named((tables.outs(t0, k),)))
    square = (length, length)
    before = (lax.broadcasted_iota(I32, square, 0) < lax.broadcasted_iota(I32, square, 1)).astype(F32)
    same = (lax.broadcasted_iota(I32, square, 0) == lax.broadcasted_iota(I32, square, 1)).astype(F32)
    slots = lax.broadcasted_iota(I32, (length, TILE), 1).astype(F32)
    table[...] = jnp.zeros_like(table)
    for k, tasks in enumerate((t0, t1, t2, t3, t4)):
        here, out = tables.inside(tasks, k), tables.outs(tasks, k)
        slot = out if k == 0 else tables.rank_of(out, tables.named((out,)))
        for i, value in enumerate((slot, tasks[1] - k * per_cell, tasks[2] - k * per_cell, here)):
            table[i : i + 1, :] = value.astype(F32)
        earlier = jnp.dot(table[...], before, preferred_element_type=F32)
        table[4:5, :] = earlier[3:4, :]
        turned = lax.dot_general(same, table[...], (((1,), (1,)), ((), ())), preferred_element_type=F32)
        to_slot = jnp.logical_and(jnp.broadcast_to(turned[:, 4:5], slots.shape) == slots, jnp.broadcast_to(turned[:, 3:4], slots.shape) > 0.5)
        moved = jnp.dot(table[...], to_slot.astype(F32), preferred_element_type=F32).astype(I32)
        count = jnp.sum(here.astype(I32))
        at = LIST_ROW + 4 * k
        for i in range(3):
            plan[at + i : at + i + 1, :] = moved[i : i + 1, :]
        plan[at : at + 1, :] = jnp.where(lane < count, moved[0:1, :], TILE - 1)
        plan[at + 3 : at + 4, :] = jnp.where(lane == TILE - 1, count, 0)
    for c in puts:
        c.wait()


def w_kernel(tasks, plan, zs, g0, g1, g2, a3, g3, a4, g4, ws, grown, cut, total, sems, osem):
    per_cell, lead = zs.shape[0], a3.shape[0]
    copies = fetch(g_places(per_cell, lead, g0, g1, g2, a3, g3, a4, g4), grown, sems)
    clear(total, 0, per_cell)
    live = live_count(tasks, per_cell)
    for c in copies:
        c.wait()
    entry = moved_entry(tasks, plan, ZG_ROW)
    run_list(live, entry, lambda a: zs[a], lambda b: split(grown[b]), False, total, 4)
    split_all(total, cut, per_cell)
    out = pltpu.make_async_copy(cut, ws, osem)
    out.start()
    out.wait()


def g_places(per_cell, lead, g0, g1, g2, a3, g3, a4, g4):
    places = [(src, k * per_cell) for k, src in enumerate((g0, g1, g2, a3, a4))]
    return places + [(g3, 3 * per_cell + lead), (g4, 4 * per_cell + lead)]


def p_kernel(plan, ft, ws, p0, p1, p2, p3, p4, total, osem):
    outs = (p0, p1, p2, p3, p4)
    starts = [sum(p.shape[0] for p in outs[:k]) for k in range(6)]
    last = starts[5]

    clear(total, 0, last)

    def one(k, _):
        at = LIST_ROW + 4 * k
        first = sum(jnp.where(k == i, start, 0) for i, start in enumerate(starts[:5]))

        def entry(e):
            return jnp.minimum(first + plan[at, e], last), plan[at + 1, e], plan[at + 2, e]

        run_list(plan[at + 3, TILE - 1], entry, lambda a: ft[a], lambda b: ws[b], False, total, 4)
        return 0

    lax.fori_loop(0, 5, one, 0)
    copies = [pltpu.make_async_copy(total.at[pl.ds(starts[k], p.shape[0])], p, osem.at[k]) for k, p in enumerate(outs)]
    for c in copies:
        c.start()
    for c in copies:
        c.wait()


def rest_kernel(tfock, tfz, tzgt, plan, fs, ws, p0, z0, z1, z2, z3, z4, g0, g1, g2, a3, g3, a4, g4, fock, factor, zgrown, ggrown, us, total, zsem, gsem, osem):
    per_cell, lead = p0.shape[0], a3.shape[0]
    places = [(src, k * per_cell) for k, src in enumerate((z0, z1, z2))]
    for k, first, then in ((3, g3, z3), (4, g4, z4)):
        start = run_start(per_cell, lead, k)
        places += [(first, start), (then, start + first.shape[0])]
    zcopies = fetch(places, zgrown, zsem)
    gcopies = fetch(g_places(per_cell, lead, g0, g1, g2, a3, g3, a4, g4), ggrown, gsem)
    clear(total.at[0], 0, per_cell)
    clear(total.at[1], 0, per_cell)

    def begin(i):
        total[2, i] = p0[i]

    each(per_cell, begin)
    fz_live, fock_live, zgt_live = (live_count(tasks, per_cell) for tasks in (tfz, tfock, tzgt))
    for c in zcopies:
        c.wait()
    run_list(fz_live, moved_entry(tfz, plan, FZ_ROW), lambda a: fs[a], lambda b: split(zgrown[b]), False, total.at[0])
    split_all(total.at[0], us, per_cell)
    run_list(fock_live, moved_entry(tfock, plan, FOCK_ROW), lambda a: ws[a], lambda b: split(zgrown[b]), True, total.at[1])
    out1 = pltpu.make_async_copy(total.at[1, pl.ds(0, per_cell)], fock, osem.at[0])
    out1.start()
    for c in gcopies:
        c.wait()
    run_list(zgt_live, moved_entry(tzgt, plan, ZGT_ROW), lambda a: us[a], lambda b: split(ggrown[b]), True, total.at[2])
    out2 = pltpu.make_async_copy(total.at[2, pl.ds(0, per_cell)], factor, osem.at[1])
    out2.start()
    out1.wait()
    out2.wait()


def join_kernel(plan, part, p1, p2, p3, p4, factor, total, puts, *, pieces):
    per_cell = part.shape[0]
    size = per_cell // pieces
    lists = tuple(enumerate((p1, p2, p3, p4)))
    counts = [jnp.minimum(plan[MAP_ROW + side, TILE - 1], p.shape[0]) for side, p in lists]
    at = [jnp.int32(0)] * len(lists)
    stored = []
    for i in range(pieces):
        piece = pl.ds(i * size, size)

        def begin(t, i=i):
            total[i * size + t] = part[i * size + t]

        each(size, begin)
        for j, (side, p) in enumerate(lists):

            def more(s, j=j, side=side, i=i):
                return jnp.logical_and(s < counts[j], plan[MAP_ROW + side, s] < (i + 1) * size)

            def add(s, side=side, p=p):
                total[plan[MAP_ROW + side, s]] += p[s]
                return s + 1

            at[j] = lax.while_loop(more, add, at[j])
        stored.append(pltpu.make_async_copy(total.at[piece], factor.at[piece], puts.at[i]))
        stored[-1].start()
    for c in stored:
        c.wait()


SMEM = pl.BlockSpec(memory_space=pltpu.SMEM)
VMEM = pl.BlockSpec(memory_space=pltpu.VMEM)
ANY = pl.BlockSpec(memory_space=pl.ANY)
HBM = pl.BlockSpec(memory_space=pltpu.HBM)
DMA = pltpu.SemaphoreType.DMA


def cost(tasks, tiles):
    return pl.CostEstimate(flops=tasks * 2 * TILE**3 * 8, bytes_accessed=tiles * TILE * TILE * 4, transcendentals=0)


def shifted(array, axis, by):
    n = lax.axis_size(axis)
    return lax.ppermute(array, axis, [(i, (i + by) % n) for i in range(n)])


def tiles(n):
    return jax.ShapeDtypeStruct((n, TILE, TILE), F32)


def cut_tiles(n):
    return jax.ShapeDtypeStruct((n, TILE, 2 * TILE), jnp.bfloat16)


def join(plan, part, sums):
    per_cell = part.shape[0]
    pieces = 2 if per_cell % 2 == 0 else 1
    return pl.pallas_call(
        functools.partial(join_kernel, pieces=pieces),
        name="join_kernel",
        out_shape=pltpu.HBM((per_cell, TILE, TILE), F32),
        in_specs=[SMEM] + [VMEM] * 5,
        out_specs=HBM,
        scratch_shapes=[pltpu.VMEM((per_cell, TILE, TILE), F32), DMA((pieces,))],
        compiler_params=pltpu.CompilerParams(vmem_limit_bytes=16 * 2**20),
        cost_estimate=cost(0, 4 * per_cell),
    )(plan, part, *sums)


def finish(run_room, x_room, y_room, gp, z, f, g, tzg, tfock, tfz, tzgt, ttrans, tn, pick, ga):
    per_cell = z.shape[0]
    cap = tzg.shape[2]
    grown = pltpu.VMEM((5 * per_cell, TILE, TILE), F32)
    cut = pltpu.VMEM((per_cell, TILE, 2 * TILE), jnp.bfloat16)
    params = pltpu.CompilerParams(vmem_limit_bytes=40 * 2**20)
    gy = (shifted(gp[0], "gy", 1), shifted(gp[1], "gy", -1))
    first = gp[0].shape[0]
    z_room = run_room - first
    pack = pl.pallas_call(
        functools.partial(pack_kernel, first=first),
        name="pack_kernel",
        out_shape=[tiles(z_room)] * 2,
        in_specs=[SMEM, VMEM],
        out_specs=[ANY] * 2,
        scratch_shapes=[pltpu.VMEM((2, z_room, TILE, TILE), F32), DMA((2,))],
        compiler_params=pltpu.CompilerParams(vmem_limit_bytes=16 * 2**20),
        cost_estimate=cost(0, 4 * per_cell),
    )
    z3, z4 = pack(pick, z)
    g_late, z_late, z3, z4 = lax.optimization_barrier((g, z, z3, z4))
    gn = (shifted(g_late, "gx", 1), shifted(g_late, "gx", -1), ga[0], gy[0], ga[1], gy[1])
    zy = (shifted(z3, "gy", 1), shifted(z4, "gy", -1))
    zn = (shifted(z_late, "gx", 1), shifted(z_late, "gx", -1)) + zy
    make_plan = pl.pallas_call(
        functools.partial(plan_kernel, lead=ga[0].shape[0]),
        name="plan_kernel",
        out_shape=[jax.ShapeDtypeStruct((PLAN_ROWS, TILE), I32)] + [cut_tiles(per_cell)] * 3,
        in_specs=[VMEM] * 11,
        out_specs=[VMEM] + [ANY] * 3,
        scratch_shapes=[pltpu.VMEM((8, cap), F32), pltpu.VMEM((3, per_cell, TILE, 2 * TILE), jnp.bfloat16), DMA((3,))],
        compiler_params=pltpu.CompilerParams(vmem_limit_bytes=24 * 2**20),
        cost_estimate=cost(cap, 8 * per_cell),
    )
    plan, fs, ft, zs = make_plan(tzg, tfock, tfz, tzgt, ttrans, *tn, f, z)
    ws = pl.pallas_call(
        w_kernel,
        name="w_kernel",
        out_shape=cut_tiles(per_cell),
        in_specs=[SMEM, SMEM, VMEM] + [ANY] * 7,
        out_specs=ANY,
        scratch_shapes=[grown, cut, pltpu.VMEM((per_cell + 1, TILE, TILE), F32), DMA((7,)), DMA],
        compiler_params=params,
        cost_estimate=cost(cap, 7 * per_cell),
    )(tzg, plan, zs, g, *gn)
    p = pl.pallas_call(
        p_kernel,
        name="p_kernel",
        out_shape=[tiles(n) for n in (per_cell, x_room, x_room, y_room, y_room)],
        in_specs=[SMEM] + [VMEM] * 2,
        out_specs=[ANY] * 5,
        scratch_shapes=[pltpu.VMEM((per_cell + 2 * x_room + 2 * y_room + 1, TILE, TILE), F32), DMA((5,))],
        compiler_params=params,
        cost_estimate=cost(2 * cap, 7 * per_cell),
    )(plan, ft, ws)
    pn = [shifted(p[k + 1], axis, -by) for k, (axis, by) in enumerate(STEPS)]
    fock_grad, part = pl.pallas_call(
        rest_kernel,
        name="rest_kernel",
        out_shape=[pltpu.HBM((per_cell, TILE, TILE), F32), tiles(per_cell)],
        in_specs=[SMEM] * 4 + [VMEM] * 3 + [ANY] * 12,
        out_specs=[HBM, ANY],
        scratch_shapes=[
            pltpu.VMEM((run_start(per_cell, ga[0].shape[0], 5), TILE, TILE), F32),
            grown,
            cut,
            pltpu.VMEM((3, per_cell + 1, TILE, TILE), F32),
            DMA((7,)),
            DMA((7,)),
            DMA((2,)),
        ],
        compiler_params=params,
        cost_estimate=cost(3 * cap, 14 * per_cell),
    )(tfock, tfz, tzgt, plan, fs, ws, p[0], z, *zn, g, *gn)
    return fock_grad, join(plan, part, pn)


def rooms_of(per_cell, lead):
    levels = ((30, 18, 12), (31, 18, 13), (31, 18, 14), (33, 18, 15), (36, 18, 17))
    scaled = [tuple(per_cell * room // 24 for room in level) for level in levels]
    return scaled + [(2 * per_cell - lead, per_cell, per_cell)]


def body(z_factor, fock, cotangent, tasks_zg, tasks_fock, tasks_fz, tasks_zgt, tasks_trans):
    per_cell = z_factor.shape[2]
    nx, ny = lax.axis_size("gx"), lax.axis_size("gy")
    z, f, g = z_factor[0, 0], fock[0, 0], cotangent[0, 0]
    lists = (tasks_zg, tasks_fock, tasks_fz, tasks_zgt, tasks_trans)
    tzg, tfock, tfz, tzgt, ttrans = (t.reshape(t.shape[2], 1, t.shape[3]) for t in lists)
    a_list = jax.ShapeDtypeStruct(tzg.shape, I32)
    lead = per_cell // 4
    rooms = rooms_of(per_cell, lead)
    met = pl.pallas_call(
        functools.partial(meet_kernel, rooms=rooms, lead=lead, cuts=lead // 3),
        name="meet_kernel",
        out_shape=[tiles(lead)] * 2
        + [a_list] * 4
        + [tiles(per_cell - lead)] * 2
        + [jax.ShapeDtypeStruct((1, 1), I32), jax.ShapeDtypeStruct((8, TILE), I32)],
        in_specs=[VMEM] * 5 + [ANY] * 2,
        out_specs=[ANY] * 2 + [VMEM] * 4 + [ANY] * 2 + [SMEM, VMEM],
        scratch_shapes=[pltpu.VMEM((2,) + tzg.shape, I32)] * 4
        + [
            pltpu.VMEM((1, TILE), I32),
            pltpu.VMEM((ny, TILE), I32),
            pltpu.VMEM((nx, ny, TILE), I32),
            pltpu.SMEM((8, TILE), I32),
            pltpu.VMEM((2 * per_cell - lead, TILE, TILE), F32),
            pltpu.VMEM((2, per_cell - lead, TILE, TILE), F32),
            DMA((4,)),
            DMA((4,)),
            DMA((12,)),
            DMA((12,)),
            DMA((ny,)),
            DMA((ny,)),
            DMA((nx,)),
            DMA((nx,)),
            DMA((5,)),
            DMA((2,)),
        ],
        compiler_params=pltpu.CompilerParams(collective_id=0, has_side_effects=True),
    )(tzg, tfock, tfz, tzgt, ttrans, g, z)
    ga, tn, gp, level, pick = met[:2], met[2:6], met[6:8], met[8], met[9]
    operands = (gp, z, f, g, tzg, tfock, tfz, tzgt, ttrans, tn, pick, ga)
    fock_grad, factor_grad = lax.switch(level[0, 0], [functools.partial(finish, *room) for room in rooms], *operands)
    return fock_grad[None, None], factor_grad[None, None]


def solution(mesh):
    cells = P("gx", "gy", None, None, None)
    lists = P("gx", "gy", None, None)
    return jax.shard_map(
        body,
        mesh=mesh,
        in_specs=(cells,) * 3 + (lists,) * 5,
        out_specs=(cells, cells),
        check_vma=False,
    )
```
